512 devices in a mesh: seq: 32 (over z, x), tensor: 16 (over y, core).
Axes of the slice: x: 4, y: 8, z: 8, core: 2. Of those that a mesh axis runs over, the one named last changes fastest.
Arguments:
- queries: bfloat16 [4096, 32, 128], P('seq', 'tensor'), may hold values from -6 to 6
- keys: bfloat16 [2, 4096, 32, 128], P(None, 'seq', 'tensor'), may hold values from -6 to 6
- values: bfloat16 [2, 4096, 32, 128], P(None, 'seq', 'tensor'), may hold values from -24 to 24
- beta: float32 [2, 32, 4096], P(None, 'tensor', 'seq'), may hold values from 0.25 to 2
- decay: float32 [32, 4096], P('tensor', 'seq'), may hold values from -0.75 to 0
- out_gain: float32 [128], replicated, may hold values from 0.1 to 1.9
- residual: bfloat16 [4096, 4096], P('seq', 'tensor'), may hold values from -40 to 40
- ffn_gain: float32 [4096], replicated, may hold values from 0.1 to 1.9
- up_blocks: bfloat16 [64, 16, 128, 128], P('tensor'), may hold values from -0.125 to 0.125
- up_index: int32 [64, 16], P('tensor'), may hold values from 0 to 31, as said below
- down_kept_tiles: bfloat16 [64, 16, 128, 128], P('tensor'), may hold values from -0.09375 to 0.09375
- down_index: int32 [64, 16], P('tensor'), may hold values from 0 to 31, as said below
Outputs:
- layer_out: bfloat16 [4096, 4096], P('seq', 'tensor')
The draws below stay inside these ranges and needn't reach their ends.
Inputs may be any that keep to these rules, and one draw needn't show every extreme that they name: `up_index`: each row names 16 different tiles. `down_index`: each row names 16 different tiles.
All inputs are finite; a program needn't handle non-finite values.
Results may differ from the reference program's by a relative error of at most 0.014.
Values may be sent and summed in bfloat16 or wider, within the bound.
A program may use at most 64 MiB of HBM per device.

```python
import math
import jax
import jax.numpy as jnp
from jax import lax

HEADS = 32
DK = 128
D = 4096
FF = 8192
TILE = 128
BLOCK_TOK = 64
TOK_DEV = 128
TOKENS = 4096
NTILE = 32
HTILE = 64
KEEP = 16
N_TENSOR = 16


def head_class(key):
    ranking = jax.random.permutation(jax.random.fold_in(key, 11), HEADS)
    first_cut = HEADS // 2
    second_cut = HEADS // 2 + HEADS // 8
    third_cut = HEADS // 2 + HEADS // 4
    kind = (ranking >= first_cut).astype(jnp.int32) + (ranking >= second_cut).astype(jnp.int32) + (ranking >= third_cut).astype(jnp.int32)
    return kind


def draw_decay(key, part):
    kind = head_class(key)
    streams = jax.random.split(jax.random.fold_in(key, 23), 5)
    device_rate = jnp.exp(jax.random.uniform(streams[0], (HEADS, TOKENS // TOK_DEV), minval=math.log(0.5), maxval=math.log(2.0)))
    device_rate = jnp.repeat(device_rate, TOK_DEV, axis=1)
    rough = jnp.exp(jax.random.uniform(streams[1], (HEADS, TOKENS), minval=math.log(0.7), maxval=math.log(1.4)))
    fast_rate = jnp.exp(jax.random.uniform(streams[2], (HEADS, 1), minval=math.log(1.0 / 50.0), maxval=math.log(1.0 / 30.0)))
    slow_rate = 0.5 / TOKENS
    middle_rate = 0.4 / TOK_DEV
    base_rate = jnp.where(kind[:, None] <= 1, slow_rate, jnp.where(kind[:, None] == 2, middle_rate, fast_rate))
    speed_ratio = base_rate * device_rate * rough
    slot_positions = jax.random.randint(streams[3], (HEADS, 2), 0, TOKENS)
    tile_locations = jnp.arange(TOKENS, dtype=jnp.int32)
    sudden_count = (tile_locations[None, :] == slot_positions[:, 0:1]) | (tile_locations[None, :] == slot_positions[:, 1:2])
    discard_fraction = jnp.log(jax.random.uniform(streams[4], (HEADS, TOKENS), minval=0.5, maxval=0.8))
    return jnp.where(sudden_count, discard_fraction, -speed_ratio).astype(jnp.float32)


def draw_beta(key, part):
    kind = head_class(key)
    streams = jax.random.split(jax.random.fold_in(key, 37), 3)
    margin = 32.0 / TOKENS * jnp.exp(jax.random.uniform(streams[0], (2, HEADS, TOKENS), minval=math.log(0.5), maxval=math.log(2.0)))
    quick = jax.random.uniform(streams[1], (2, HEADS, TOKENS), minval=0.3, maxval=1.7)
    gentle = jax.random.uniform(streams[2], (2, HEADS, TOKENS), minval=0.25, maxval=0.45)
    kind_all = kind[None, :, None]
    chosen = jnp.where((kind_all == 0) | (kind_all == 2), 2.0 - margin, jnp.where(kind_all == 1, gentle, quick))
    return chosen.astype(jnp.float32)


def draw_values(key, part):
    streams = jax.random.split(jax.random.fold_in(key, 61), 2)
    base = jax.random.truncated_normal(streams[0], -4.0, 4.0, (2, TOKENS, HEADS, DK))
    block_scale = jnp.exp(jax.random.uniform(streams[1], (TOKENS // BLOCK_TOK, HEADS), minval=math.log(0.15), maxval=math.log(6.0)))
    block_scale = jnp.repeat(block_scale, BLOCK_TOK, axis=0)
    return (base * block_scale[None, :, :, None]).astype(jnp.bfloat16)


def draw_residual(key, part):
    streams = jax.random.split(jax.random.fold_in(key, 53), 3)
    base = jax.random.truncated_normal(streams[0], -4.0, 4.0, (TOKENS, D))
    row_scale = jnp.exp(jax.random.uniform(streams[1], (TOKENS, 1), minval=math.log(0.3), maxval=math.log(3.0)))
    columns = jnp.arange(D, dtype=jnp.float32) / (D - 1)
    col_scale = jnp.exp(math.log(3.0) * columns)[None, :] / math.sqrt(3.0)
    col_scale = col_scale * jnp.exp(jax.random.uniform(streams[2], (1, D), minval=-0.35, maxval=0.35))
    return (base * row_scale * col_scale).astype(jnp.bfloat16)


def pick_tiles(key):
    scores = jax.random.randint(key, (HTILE, NTILE), 0, 1 << 20) * NTILE + jnp.arange(NTILE, dtype=jnp.int32)[None, :]
    _, chosen = lax.top_k(scores, KEEP)
    return chosen.astype(jnp.int32)


def draw_up_index(key, part):
    return pick_tiles(jax.random.fold_in(key, 41))


def draw_down_index(key, part):
    return pick_tiles(jax.random.fold_in(key, 43))


def level_of(key, extent, cuts, low, high):
    gain = 1.0
    for axis_at, parts in cuts:
        steps = jax.random.uniform(jax.random.fold_in(jax.random.fold_in(key, 6), axis_at), (parts,), jnp.float32, low / len(cuts), high / len(cuts))
        gain = gain * jnp.repeat(jnp.exp(steps), extent[axis_at] // parts).reshape((-1,) + (1,) * (len(extent) - 1 - axis_at))
    return gain


def bell_draw(rng, extent, spread, most, cuts=(), held_as=jnp.bfloat16):
    values = spread * jax.random.normal(rng, extent, jnp.float32)
    if cuts:
        values = values * level_of(rng, extent, cuts, -0.22, 0.18)
    return jnp.clip(values, -most, most).astype(held_as)


def setup_inputs(seed: int = 0) -> dict:
    key_of = jax.random.split(jax.random.key(seed), 13)
    queries = bell_draw(key_of[0], (TOKENS, HEADS, DK), 1.0, 6.0, ((0, 32), (1, 16)))
    keys = bell_draw(key_of[1], (2, TOKENS, HEADS, DK), 1.0, 6.0, ((1, 32), (2, 16)))
    values = draw_values(jax.random.fold_in(key_of[12], 71), 0)
    beta = draw_beta(jax.random.fold_in(key_of[12], 71), 0)
    decay = draw_decay(jax.random.fold_in(key_of[12], 71), 0)
    out_gain = jnp.clip(1.0 + 0.18 * jax.random.normal(key_of[5], (DK,), jnp.float32), 0.1, 1.9)
    residual = draw_residual(jax.random.fold_in(key_of[12], 71), 0)
    ffn_gain = jnp.clip(1.0 + 0.18 * jax.random.normal(key_of[7], (D,), jnp.float32), 0.1, 1.9)
    up_blocks = bell_draw(key_of[8], (HTILE, KEEP, TILE, TILE), (KEEP * TILE) ** -0.5, 0.125, ((0, 16),))
    up_index = draw_up_index(jax.random.fold_in(key_of[12], 71), 0)
    down_kept_tiles = bell_draw(key_of[10], (HTILE, KEEP, TILE, TILE), (FF // 2) ** -0.5, 0.09375, ((0, 16),))
    down_index = draw_down_index(jax.random.fold_in(key_of[12], 71), 0)
    return {"queries": queries, "keys": keys, "values": values, "beta": beta, "decay": decay, "out_gain": out_gain, "residual": residual, "ffn_gain": ffn_gain, "up_blocks": up_blocks, "up_index": up_index, "down_kept_tiles": down_kept_tiles, "down_index": down_index}


def normed(given):
    wide = given.astype(jnp.float32)
    return wide * lax.rsqrt(lax.optimization_barrier(jnp.sum(wide * wide, -1, keepdims=True)) + 1e-06)

def reference(queries, keys, values, beta, decay, out_gain, residual, ffn_gain, up_blocks, up_index, down_kept_tiles, down_index):
    highest = lax.Precision.HIGHEST
    query_unit = normed(queries)
    key_unit = normed(keys).transpose(1, 0, 2, 3)
    value_all = values.astype(jnp.float32).transpose(1, 0, 2, 3)
    beta_all = beta.transpose(2, 0, 1)
    gate_all = jnp.exp(decay).T

    def advance(state, inputs):
        query_now, key_now, value_now, beta_now, gate_now = inputs
        state = gate_now[:, None, None] * state
        for factor in range(2):
            key_one = key_now[factor]
            read_out = jnp.einsum('hd,hde->he', key_one, state, precision=highest)
            update = value_now[factor] - read_out
            state = state + beta_now[factor][:, None, None] * key_one[:, :, None] * update[:, None, :]
        result = jnp.einsum('hd,hde->he', query_now, state, precision=highest)
        return (state, result)
    start = jnp.zeros((HEADS, DK, DK), jnp.float32)
    _, head_out = lax.scan(advance, start, (query_unit, key_unit, value_all, beta_all, gate_all))
    normed_out = head_out * lax.rsqrt(lax.optimization_barrier(jnp.mean(head_out * head_out, -1, keepdims=True)) + 1e-05) * out_gain
    hidden_state = (residual.astype(jnp.float32) + normed_out.reshape(TOKENS, D)).astype(jnp.bfloat16)
    hidden_wide = hidden_state.astype(jnp.float32)
    ffn_in = (hidden_wide * lax.rsqrt(lax.optimization_barrier(jnp.mean(hidden_wide * hidden_wide, -1, keepdims=True)) + 1e-05) * ffn_gain).astype(jnp.bfloat16)
    tiles_in = ffn_in.astype(jnp.float32).reshape(TOKENS, NTILE, TILE)
    group_tiles = HTILE // N_TENSOR
    up_group = up_blocks.reshape(N_TENSOR, group_tiles, KEEP, TILE, TILE)
    up_place = up_index.reshape(N_TENSOR, group_tiles, KEEP)
    down_group = down_kept_tiles.reshape(N_TENSOR, group_tiles, KEEP, TILE, TILE)
    down_place = down_index.reshape(N_TENSOR, group_tiles, KEEP)
    tile_ids = jnp.arange(NTILE, dtype=jnp.int32)

    def one_group(total, inputs):
        up_part, up_ids, down_part, down_ids = inputs
        picked = jnp.take(tiles_in, up_ids, axis=1)
        pre_act = jnp.einsum('tcjd,cjdh->tch', picked, up_part.astype(jnp.float32), precision=highest)
        activation = lax.optimization_barrier(jax.nn.gelu(pre_act).astype(jnp.bfloat16)).astype(jnp.float32)
        contrib = jnp.einsum('tch,cjho->tcjo', activation, down_part.astype(jnp.float32), precision=highest)
        one_hot = (down_ids[:, :, None] == tile_ids[None, None, :]).astype(jnp.float32)
        group_sum = jnp.einsum('tcjo,cjb->tbo', contrib, one_hot, precision=highest)
        group_sum = lax.optimization_barrier(group_sum.astype(jnp.bfloat16)).astype(jnp.float32)
        return (total + group_sum, None)
    ffn_out, _ = lax.scan(one_group, jnp.zeros((TOKENS, NTILE, TILE), jnp.float32), (up_group, up_place, down_group, down_place))
    return (hidden_wide + ffn_out.reshape(TOKENS, D)).astype(jnp.bfloat16)
```

```python
import functools

import jax
import jax.numpy as jnp
from jax import lax
from jax.experimental import pallas as pl
from jax.experimental.pallas import tpu as pltpu
from jax.sharding import PartitionSpec as P

F32 = jnp.float32
BF16 = jnp.bfloat16
HIGHEST = lax.Precision.HIGHEST
LANES_X = 4
MESH = pl.DeviceIdType.MESH


def dot(a, b, contract=(1, 0), precision=None):
    return lax.dot_general(
        a,
        b,
        (((contract[0],), (contract[1],)), ((), ())),
        precision=precision,
        preferred_element_type=F32,
    )


def split(a):
    high = a.astype(BF16)
    return high, (a - high.astype(F32)).astype(BF16)


def mm3(a, b):
    ah, al = split(a)
    bh, bl = split(b)
    left = jnp.concatenate([ah, al], 1)
    right = jnp.concatenate(
        [jnp.concatenate([bh, bl], 1), jnp.concatenate([bh, jnp.zeros_like(bl)], 1)], 0
    )
    both = dot(left, right)
    n = b.shape[1]
    return both[:, :n] + both[:, n:]


def iota(shape, axis):
    return lax.broadcasted_iota(jnp.int32, shape, axis)


def unit_lower_inverse(lowers):
    n = lowers[0].shape[0]
    rows, cols = iota((n, n), 0), iota((n, n), 1)
    eye = (rows == cols).astype(F32)
    base = (rows >> 3) == (cols >> 3)
    n1 = [jnp.where(base, -low, 0.0) for low in lowers]
    n2 = [mm3(a, a) for a in n1]
    n3 = [mm3(a, b) for a, b in zip(n1, n2)]
    n4 = [mm3(a, a) for a in n2]
    y = [eye + a + b + c for a, b, c in zip(n1, n2, n3)]
    x = [a + mm3(a, b) for a, b in zip(y, n4)]
    shift = 3
    while (1 << shift) < n:
        pick = ((rows >> (shift + 1)) == (cols >> (shift + 1))) & ((rows >> shift) != (cols >> shift))
        links = [jnp.where(pick, low, 0.0) for low in lowers]
        right = [mm3(c, a) for c, a in zip(links, x)]
        x = [a - mm3(a, b) for a, b in zip(x, right)]
        shift += 1
    return x


def local_kernel(
    q_ref, k_ref, v_ref, beta_ref, decay_ref, up_ref, down_ref, tw_ref, qt_ref, lo_ref, inv_ref
):
    tok = q_ref.shape[0] // 2
    span = 2 * tok
    heads = 2
    half = span // 2

    for which, table in enumerate((up_ref, down_ref)):
        for c in range(table.shape[0]):
            for b in range(inv_ref.shape[2]):
                inv_ref[which, c, b] = table.shape[1]
            for j in range(table.shape[1]):
                inv_ref[which, c, table[c, j]] = j

    kv = jnp.concatenate([k_ref[...], v_ref[...]], 1)
    q_all = q_ref[...]
    small = jnp.concatenate(
        [decay_ref[...], beta_ref[0], beta_ref[1], jnp.zeros((2, tok), F32)], 0
    )
    m_at, t_at = iota((span, tok), 0), iota((span, tok), 1)
    upto = (t_at <= (m_at >> 1)).astype(F32)
    first = ((t_at == (m_at >> 1)) & ((m_at & 1) == 0)).astype(F32)
    second = ((t_at == (m_at >> 1)) & ((m_at & 1) == 1)).astype(F32)
    upto_tok = (iota((tok, tok), 1) <= iota((tok, tok), 0)).astype(F32)
    run_col = dot(upto, small, (1, 1), HIGHEST)
    run_row = dot(small, upto, (1, 1), HIGHEST)
    tok_col = dot(upto_tok, small, (1, 1), HIGHEST)
    one_col, two_col = dot(first, small, (1, 1), HIGHEST), dot(second, small, (1, 1), HIGHEST)
    one_row, two_row = dot(small, first, (1, 1), HIGHEST), dot(small, second, (1, 1), HIGHEST)

    rows, cols = iota((span, span), 0), iota((span, span), 1)
    below = cols < rows
    same = rows == cols
    reach = iota((tok, span), 1) <= 2 * iota((tok, span), 0) + 1
    eye = (iota((tok, tok), 0) == iota((tok, tok), 1)).astype(F32)
    row_of = iota((span, 4 * tok), 0)
    place = (row_of & 1) * span + (row_of >> 1) * 2
    column = iota((span, 4 * tok), 1)
    q_place = iota((tok, span), 0) * 2
    q_column = iota((tok, span), 1)

    ks, vs, qs, gammas, lowers, keep = [], [], [], [], [], []
    for h in range(heads):
        pick = (column == place + h).astype(BF16)
        both = dot(pick, kv).astype(BF16)
        k, v = both[:, :128], both[:, 128:]
        q = dot((q_column == q_place + h).astype(BF16), q_all)
        gram = dot(k, k, (1, 1))
        diag = jnp.where(same, gram, 0.0)
        rk_col = lax.rsqrt(jnp.sum(diag, 1, keepdims=True) + 1e-06)
        rk_row = lax.rsqrt(jnp.sum(diag, 0, keepdims=True) + 1e-06)
        run_c, run_r = run_col[:, h : h + 1], run_row[h : h + 1, :]
        beta_c = one_col[:, 2 + h : 3 + h] + two_col[:, 4 + h : 5 + h]
        beta_r = one_row[2 + h : 3 + h, :] + two_row[4 + h : 5 + h, :]
        fade = jnp.exp(jnp.where(below, run_c - run_r, 0.0))
        low = jnp.where(below, (beta_c * rk_col) * fade * gram * rk_row, 0.0)
        keep.append((k, v, q, rk_col, rk_row, run_c, run_r, beta_r, low))
        lowers += [low[:half, :half], low[half:, half:]]

    inverses = unit_lower_inverse(lowers)
    mids = [mm3(keep[h][8][half:, :half], inverses[2 * h]) for h in range(heads)]
    crosses = [mm3(inverses[2 * h + 1], mids[h]) for h in range(heads)]
    for h in range(heads):
        k, v, q, rk_col, rk_row, run_c, run_r, beta_r, low = keep[h]
        a = jnp.concatenate(
            [
                jnp.concatenate([inverses[2 * h], jnp.zeros((half, half), F32)], 1),
                jnp.concatenate([-crosses[h], inverses[2 * h + 1]], 1),
            ],
            0,
        )
        a_val = a * beta_r
        a_key = a_val * (jnp.exp(run_r) * rk_row)
        ah, al = split(a_val)
        u = dot(ah, v) + dot(al, v)
        ah, al = split(a_key)
        w = dot(ah, k) + dot(al, k)
        last = run_c[span - 1 : span, :]
        remain = jnp.exp(last - run_c) * rk_col
        uh, ul = split(u * remain)
        write_t = dot(uh, k, (0, 0)) + dot(ul, k, (0, 0))
        wh, wl = split(w * remain)
        trans = jnp.exp(last) * eye - dot(k, wh, (0, 0)) - dot(k, wl, (0, 0))
        tw_ref[h, 0:64, :] = write_t[:64].astype(BF16)
        tw_ref[h, 64:192, :] = trans.astype(BF16)
        tw_ref[h, 192:256, :] = write_t[64:].astype(BF16)
        tok_run = tok_col[:, h : h + 1]
        rq = lax.rsqrt(jnp.sum(q * q, 1, keepdims=True) + 1e-06)
        qk = dot(q.astype(BF16), k, (1, 1))
        mixing = jnp.where(
            reach, jnp.exp(jnp.where(reach, tok_run - run_r, 0.0)) * qk * rq * rk_row, 0.0
        )
        mh, ml = split(mixing)
        bh, bl = split(jnp.concatenate([w, u], 1))
        mixed = dot(mh, bh) + dot(ml, bh) + dot(mh, bl)
        qt_ref[h] = (jnp.exp(tok_run) * rq) * q - mixed[:, :128]
        lo_ref[h] = mixed[:, 128:]


def chain_step(state, trans, write):
    n = state.shape[0]
    high, low = split(state)
    both = dot(jnp.concatenate([high, low], 0), trans, (1, 1))
    return both[:n] + both[n:] + write.astype(F32)


def main_kernel(
    nz,
    ny,
    inv_ref,
    tw_ref,
    qt_ref,
    lo_ref,
    res_ref,
    og_ref,
    fg_ref,
    up_hbm,
    down_hbm,
    out_ref,
    up_v,
    down_v,
    rx,
    zmsg,
    rz,
    chain,
    pmsg,
    rp,
    xg,
    acc,
    act,
    pair_out,
    pair_in,
    psum,
    rs,
    wsem,
    a_send,
    a_recv,
    b_send,
    b_recv,
    c_send,
    c_recv,
    z_send,
    z_recv,
    p_send,
    p_recv,
    g_send,
    g_recv,
    f_send,
    s_send,
    s_recv,
    r_send,
    r_recv,
):
    seq, ten = lax.axis_index("seq"), lax.axis_index("tensor")
    z, x = seq // LANES_X, lax.rem(seq, LANES_X)
    y, core = ten // 2, lax.rem(ten, 2)
    partner = y * 2 + 1 - core
    head, part = x // 2, lax.rem(x, 2)
    groups = up_hbm.shape[0]
    kept = up_hbm.shape[1]

    def at_x(o):
        return lax.rem(x + o, LANES_X)

    def at_y(o):
        return lax.rem(y + o, ny)

    barrier = pltpu.get_barrier_semaphore()
    peers = [(z * LANES_X + at_x(o), ten) for o in range(1, LANES_X)]
    peers += [(lax.rem(z + o, nz) * LANES_X + x, ten) for o in range(1, nz)]
    peers += [(seq, at_y(o) * 2 + core) for o in range(1, ny)]
    peers += [(seq, partner)]
    for peer in peers:
        pl.semaphore_signal(barrier, inc=1, device_id=peer, device_id_type=MESH)

    load_up = pltpu.make_async_copy(up_hbm, up_v.at[:, pl.ds(0, kept)], wsem.at[0])
    load_down = pltpu.make_async_copy(down_hbm, down_v.at[:, pl.ds(0, kept)], wsem.at[1])
    load_up.start()
    load_down.start()
    rx[x] = tw_ref[...]
    for c in range(groups):
        up_v[c, kept] = jnp.zeros(up_v.shape[2:], BF16)
        down_v[c, kept] = jnp.zeros(up_v.shape[2:], BF16)
    chain[...] = jnp.zeros_like(chain)
    pl.semaphore_wait(barrier, len(peers))

    def remote(src, dst, send, recv, peer):
        return pltpu.make_async_remote_copy(
            src_ref=src,
            dst_ref=dst,
            send_sem=send,
            recv_sem=recv,
            device_id=peer,
            device_id_type=MESH,
        )

    def a_copy(o):
        there = at_x(o)
        h2, p2 = there // 2, lax.rem(there, 2)
        rows = pl.ds(pl.multiple_of(p2 * 64, 64), 192)
        return remote(
            tw_ref.at[h2, rows],
            rx.at[x, h2, rows],
            a_send.at[o],
            a_recv.at[x],
            (z * LANES_X + there, ten),
        )

    def b_copies(o):
        there = at_x(o)
        h2, p2 = there // 2, lax.rem(there, 2)
        rows = pl.ds(pl.multiple_of((1 - p2) * 192, 64), 64)
        peer = (z * LANES_X + there, ten)
        return (
            remote(
                tw_ref.at[h2, rows], rx.at[x, h2, rows], b_send.at[o], b_recv.at[x], peer
            ),
            remote(
                tw_ref.at[1 - h2], rx.at[x, 1 - h2], c_send.at[o], c_recv.at[x], peer
            ),
        )

    for o in (2, 1, 3):
        a_copy(o).start()
    for o in range(1, LANES_X):

        @pl.when(x + o < LANES_X)
        def _():
            for one in b_copies(o):
                one.start()

    my_rows = pl.ds(pl.multiple_of(part * 64, 64), 192)
    for o in (1, 3, 2):
        source = at_x(o)
        remote(
            rx.at[source, head, my_rows],
            rx.at[source, head, my_rows],
            a_send.at[o],
            a_recv.at[source],
            (seq, ten),
        ).wait_recv()

    w_rows = pl.ds(pl.multiple_of(part * 192, 64), 64)
    ts = [rx[i, head, pl.ds(64, 128)] for i in range(LANES_X)]
    ws = [rx[i, head, w_rows] for i in range(LANES_X)]
    t10, t32 = dot(ts[1], ts[0]), dot(ts[3], ts[2])
    w10 = dot(ws[0], ts[1], (1, 1)) + ws[1].astype(F32)
    w32 = dot(ws[2], ts[3], (1, 1)) + ws[3].astype(F32)
    zmsg[64:192] = mm3(t32, t10).astype(BF16)
    th, tl = split(t32)
    wh, wl = split(w10)
    mixed = dot(jnp.concatenate([wh, wl], 0), th, (1, 1))
    w_all = mixed[:64] + mixed[64:] + dot(wh, tl, (1, 1)) + w32
    zmsg[0:64] = w_all.astype(BF16)

    def z_copy(o):
        return remote(
            zmsg,
            rz.at[z],
            z_send.at[o],
            z_recv.at[z],
            ((z + o) * LANES_X + x, ten),
        )

    for o in range(1, nz):

        @pl.when(z + o < nz)
        def _():
            z_copy(o).start()

    for i in range(nz - 1):

        @pl.when(i < z)
        def _():
            remote(
                rz.at[i], rz.at[i], z_send.at[0], z_recv.at[i], (seq, ten)
            ).wait_recv()
            if i == 0:
                chain[...] = rz[0, 0:64].astype(F32)
            else:
                chain[...] = chain_step(chain[...], rz[i, 64:192], rz[i, 0:64])

    entering = chain[...].astype(BF16)
    pmsg[...] = entering
    p_rows = pl.ds(pl.multiple_of(part * 64, 64), 64)
    rp[head, p_rows] = entering

    def p_copy(o):
        return remote(
            pmsg,
            rp.at[head, p_rows],
            p_send.at[o],
            p_recv.at[x],
            (z * LANES_X + at_x(o), ten),
        )

    for o in (2, 1, 3):
        p_copy(o).start()
    for i in range(LANES_X - 1):

        @pl.when(i < x)
        def _():
            other = pl.ds(pl.multiple_of((1 - part) * 192, 64), 64)
            remote(
                rx.at[i, head, other],
                rx.at[i, head, other],
                b_send.at[0],
                b_recv.at[i],
                (seq, ten),
            ).wait_recv()
            remote(
                rx.at[i, 1 - head], rx.at[i, 1 - head], c_send.at[0], c_recv.at[i], (seq, ten)
            ).wait_recv()

    for o in (1, 3, 2):
        source = at_x(o)
        rows = pl.ds(pl.multiple_of(lax.rem(source, 2) * 64, 64), 64)
        remote(
            rp.at[source // 2, rows],
            rp.at[source // 2, rows],
            p_send.at[o],
            p_recv.at[source],
            (seq, ten),
        ).wait_recv()

    state = [rp[h].astype(F32) for h in range(2)]
    for i in range(LANES_X - 1):
        for h in range(2):
            write = jnp.concatenate([rx[i, h, 0:64], rx[i, h, 192:256]], 0)
            moved = chain_step(state[h], rx[i, h, 64:192], write)
            state[h] = jnp.where(i < x, moved, state[h])

    gain = og_ref[...]
    pieces = []
    for h in range(2):
        qh, ql = split(qt_ref[h])
        sh, sl = split(state[h])
        head_out = dot(qh, sh, (1, 1)) + dot(ql, sh, (1, 1)) + dot(qh, sl, (1, 1)) + lo_ref[h]
        power = jnp.mean(head_out * head_out, -1, keepdims=True)
        normed = head_out * lax.rsqrt(power + 1e-05) * gain
        pieces.append(res_ref[:, 128 * h : 128 * h + 128].astype(F32) + normed)
    xg[ten] = jnp.concatenate(pieces, 1).astype(BF16)

    def g_copy(o):
        return remote(
            xg.at[ten],
            xg.at[ten],
            g_send.at[o],
            g_recv.at[ten],
            (seq, partner if o == 0 else at_y(o) * 2 + core),
        )

    order = sorted(range(1, ny), key=lambda o: -min(o, ny - o))
    for o in order:
        g_copy(o).start()
    g_copy(0).start()

    def f_copy(o):
        slot = at_y(o) * 2 + core
        return remote(
            xg.at[slot], xg.at[slot], f_send.at[o], g_recv.at[slot], (seq, partner)
        )

    def arrived(slot):
        remote(
            xg.at[slot], xg.at[slot], g_send.at[0], g_recv.at[slot], (seq, ten)
        ).wait_recv()

    load_up.wait()
    load_down.wait()

    def absorb(slot, first, power):
        wide = xg[slot].astype(F32)
        power = power + jnp.sum(wide * wide, -1, keepdims=True)
        scaled = (wide * fg_ref[slot]).astype(BF16)
        weights = jnp.concatenate(
            [
                jnp.concatenate(
                    [up_v[c, inv_ref[0, c, 2 * slot + b]] for c in range(groups)], 1
                )
                for b in range(2)
            ],
            0,
        )
        term = dot(scaled, weights)
        if first:
            acc[...] = term
        else:
            acc[...] += term
        return power

    power = absorb(ten, True, jnp.zeros((xg.shape[1], 1), F32))
    arrived(partner)
    power = absorb(partner, False, power)
    late = None
    for o in sorted(range(1, ny), key=lambda o: (min(o, ny - o), o)):
        slot = at_y(o) * 2 + core
        arrived(slot)
        f_copy(o).start()
        power = absorb(slot, False, power)
        if late is not None:
            arrived(late)
            power = absorb(late, False, power)
        late = at_y(o) * 2 + 1 - core
    if late is not None:
        arrived(late)
        power = absorb(late, False, power)

    width = 256 * xg.shape[0]
    scale = lax.rsqrt(power / width + 1e-05)
    act[...] = jax.nn.gelu(acc[...] * scale).astype(BF16)

    def share(slot):
        weights = jnp.concatenate(
            [
                jnp.concatenate(
                    [down_v[c, inv_ref[1, c, 2 * slot + b]] for b in range(2)], 1
                )
                for c in range(groups)
            ],
            0,
        )
        return dot(act[...], weights).astype(BF16)

    def s_copy(o):
        return remote(
            pair_out.at[o], pair_in.at[o], s_send.at[o], s_recv.at[o], (seq, partner)
        )

    def r_copy(o):
        return remote(
            psum.at[o],
            rs.at[y],
            r_send.at[o],
            r_recv.at[y],
            (seq, at_y(o) * 2 + core),
        )

    for o in order + [0]:
        pair_out[o] = share(at_y(o) * 2 + 1 - core)
        s_copy(o).start()
    total = None
    for o in order + [0]:
        mine = share(at_y(o) * 2 + core).astype(F32)
        s_copy(o).wait_recv()
        summed = mine + pair_in[o].astype(F32)
        if o == 0:
            total = summed
        else:
            psum[o] = summed.astype(BF16)
            r_copy(o).start()
    total = total + xg[ten].astype(F32)
    for o in sorted(range(1, ny), key=lambda o: (min(o, ny - o), o)):
        source = at_y(o)
        remote(
            rs.at[source], rs.at[source], r_send.at[0], r_recv.at[source], (seq, ten)
        ).wait_recv()
        total = total + rs[source].astype(F32)
    out_ref[...] = total.astype(BF16)

    for o in range(1, LANES_X):
        a_copy(o).wait_send()
        p_copy(o).wait_send()

        @pl.when(x + o < LANES_X)
        def _():
            for one in b_copies(o):
                one.wait_send()

    for o in range(1, nz):

        @pl.when(z + o < nz)
        def _():
            z_copy(o).wait_send()

    g_copy(0).wait_send()
    s_copy(0).wait_send()
    for o in range(1, ny):
        g_copy(o).wait_send()
        f_copy(o).wait_send()
        s_copy(o).wait_send()
        r_copy(o).wait_send()


def solution(mesh):
    nseq, nten = mesh.shape["seq"], mesh.shape["tensor"]
    nz, ny = nseq // LANES_X, nten // 2
    vmem = pl.BlockSpec(memory_space=pltpu.VMEM)
    smem = pl.BlockSpec(memory_space=pltpu.SMEM)
    anywhere = pl.BlockSpec(memory_space=pl.ANY)
    dma = pltpu.SemaphoreType.DMA

    def per_device(
        queries,
        keys,
        values,
        beta,
        decay,
        out_gain,
        residual,
        ffn_gain,
        up_blocks,
        up_index,
        down_kept_tiles,
        down_index,
    ):
        tok = queries.shape[0]
        groups, kept = up_index.shape
        tiles = 2 * nten
        tw, qt, lo, inv = pl.pallas_call(
            local_kernel,
            out_shape=(
                jax.ShapeDtypeStruct((2, 256, 128), BF16),
                jax.ShapeDtypeStruct((2, tok, 128), F32),
                jax.ShapeDtypeStruct((2, tok, 128), F32),
                jax.ShapeDtypeStruct((2, groups, tiles), jnp.int32),
            ),
            in_specs=[vmem] * 5 + [smem] * 2,
            out_specs=(vmem, vmem, vmem, smem),
            name="local_terms",
        )(
            queries.reshape(2 * tok, 128),
            keys.reshape(4 * tok, 128),
            values.reshape(4 * tok, 128),
            beta,
            decay,
            up_index,
            down_index,
        )
        return pl.pallas_call(
            functools.partial(main_kernel, nz, ny),
            out_shape=jax.ShapeDtypeStruct((tok, 256), BF16),
            in_specs=[smem] + [vmem] * 6 + [anywhere] * 2,
            out_specs=vmem,
            scratch_shapes=[
                pltpu.VMEM((groups, kept + 1, 128, 128), BF16),
                pltpu.VMEM((groups, kept + 1, 128, 128), BF16),
                pltpu.VMEM((LANES_X, 2, 256, 128), BF16),
                pltpu.VMEM((192, 128), BF16),
                pltpu.VMEM((nz, 192, 128), BF16),
                pltpu.VMEM((64, 128), F32),
                pltpu.VMEM((64, 128), BF16),
                pltpu.VMEM((2, 128, 128), BF16),
                pltpu.VMEM((nten, tok, 256), BF16),
                pltpu.VMEM((tok, groups * 128), F32),
                pltpu.VMEM((tok, groups * 128), BF16),
                pltpu.VMEM((ny, tok, 256), BF16),
                pltpu.VMEM((ny, tok, 256), BF16),
                pltpu.VMEM((ny, tok, 256), BF16),
                pltpu.VMEM((ny, tok, 256), BF16),
                dma((2,)),
                dma((LANES_X,)),
                dma((LANES_X,)),
                dma((LANES_X,)),
                dma((LANES_X,)),
                dma((LANES_X,)),
                dma((LANES_X,)),
                dma((nz,)),
                dma((nz,)),
                dma((LANES_X,)),
                dma((LANES_X,)),
                dma((ny,)),
                dma((nten,)),
                dma((ny,)),
                dma((ny,)),
                dma((ny,)),
                dma((ny,)),
                dma((ny,)),
            ],
            compiler_params=pltpu.CompilerParams(collective_id=0, has_side_effects=True),
            name="scan_and_ffn",
        )(
            inv,
            tw,
            qt,
            lo,
            residual,
            out_gain.reshape(1, 128),
            ffn_gain.reshape(nten, 1, 256),
            up_blocks,
            down_kept_tiles,
        )

    placed = (
        P("seq", "tensor", None),
        P(None, "seq", "tensor", None),
        P(None, "seq", "tensor", None),
        P(None, "tensor", "seq"),
        P("tensor", "seq"),
        P(),
        P("seq", "tensor"),
        P(),
        P("tensor", None, None, None),
        P("tensor", None),
        P("tensor", None, None, None),
        P("tensor", None),
    )
    return jax.shard_map(
        per_device, mesh=mesh, in_specs=placed, out_specs=P("seq", "tensor"), check_vma=False
    )
```

```python
import functools

import jax
import jax.numpy as jnp
from jax import lax
from jax.experimental import pallas as pl
from jax.experimental.pallas import tpu as pltpu
from jax.sharding import PartitionSpec as P

F32 = jnp.float32
BF16 = jnp.bfloat16
HIGHEST = lax.Precision.HIGHEST
LANES_X = 4
MESH = pl.DeviceIdType.MESH


def dot(a, b, contract=(1, 0), precision=None):
    return lax.dot_general(
        a,
        b,
        (((contract[0],), (contract[1],)), ((), ())),
        precision=precision,
        preferred_element_type=F32,
    )


def split(a):
    high = a.astype(BF16)
    return high, (a - high.astype(F32)).astype(BF16)


def mm3(a, b):
    ah, al = split(a)
    bh, bl = split(b)
    left = jnp.concatenate([ah, al], 1)
    right = jnp.concatenate(
        [jnp.concatenate([bh, bl], 1), jnp.concatenate([bh, jnp.zeros_like(bl)], 1)], 0
    )
    both = dot(left, right)
    n = b.shape[1]
    return both[:, :n] + both[:, n:]


def iota(shape, axis):
    return lax.broadcasted_iota(jnp.int32, shape, axis)


def unit_lower_inverse(lowers):
    n = lowers[0].shape[0]
    rows, cols = iota((n, n), 0), iota((n, n), 1)
    eye = (rows == cols).astype(F32)
    base = (rows >> 3) == (cols >> 3)
    n1 = [jnp.where(base, -low, 0.0) for low in lowers]
    n2 = [mm3(a, a) for a in n1]
    n3 = [mm3(a, b) for a, b in zip(n1, n2)]
    n4 = [mm3(a, a) for a in n2]
    y = [eye + a + b + c for a, b, c in zip(n1, n2, n3)]
    x = [a + mm3(a, b) for a, b in zip(y, n4)]
    shift = 3
    while (1 << shift) < n:
        pick = ((rows >> (shift + 1)) == (cols >> (shift + 1))) & ((rows >> shift) != (cols >> shift))
        links = [jnp.where(pick, low, 0.0) for low in lowers]
        right = [mm3(c, a) for c, a in zip(links, x)]
        x = [a - mm3(a, b) for a, b in zip(x, right)]
        shift += 1
    return x


def local_kernel(
    q_ref, k_ref, v_ref, beta_ref, decay_ref, up_ref, down_ref, tw_ref, qt_ref, lo_ref, inv_ref
):
    tok = q_ref.shape[0] // 2
    span = 2 * tok
    heads = 2
    half = span // 2

    for which, table in enumerate((up_ref, down_ref)):
        for c in range(table.shape[0]):
            for b in range(inv_ref.shape[2]):
                inv_ref[which, c, b] = table.shape[1]
            for j in range(table.shape[1]):
                inv_ref[which, c, table[c, j]] = j

    kv = jnp.concatenate([k_ref[...], v_ref[...]], 1)
    q_all = q_ref[...]
    small = jnp.concatenate(
        [decay_ref[...], beta_ref[0], beta_ref[1], jnp.zeros((2, tok), F32)], 0
    )
    m_at, t_at = iota((span, tok), 0), iota((span, tok), 1)
    upto = (t_at <= (m_at >> 1)).astype(F32)
    first = ((t_at == (m_at >> 1)) & ((m_at & 1) == 0)).astype(F32)
    second = ((t_at == (m_at >> 1)) & ((m_at & 1) == 1)).astype(F32)
    upto_tok = (iota((tok, tok), 1) <= iota((tok, tok), 0)).astype(F32)
    run_col = dot(upto, small, (1, 1), HIGHEST)
    run_row = dot(small, upto, (1, 1), HIGHEST)
    tok_col = dot(upto_tok, small, (1, 1), HIGHEST)
    one_col, two_col = dot(first, small, (1, 1), HIGHEST), dot(second, small, (1, 1), HIGHEST)
    one_row, two_row = dot(small, first, (1, 1), HIGHEST), dot(small, second, (1, 1), HIGHEST)

    rows, cols = iota((span, span), 0), iota((span, span), 1)
    below = cols < rows
    same = rows == cols
    reach = iota((tok, span), 1) <= 2 * iota((tok, span), 0) + 1
    eye = (iota((tok, tok), 0) == iota((tok, tok), 1)).astype(F32)
    row_of = iota((span, 4 * tok), 0)
    place = (row_of & 1) * span + (row_of >> 1) * 2
    column = iota((span, 4 * tok), 1)
    q_place = iota((tok, span), 0) * 2
    q_column = iota((tok, span), 1)

    ks, vs, qs, gammas, lowers, keep = [], [], [], [], [], []
    for h in range(heads):
        pick = (column == place + h).astype(BF16)
        both = dot(pick, kv).astype(BF16)
        k, v = both[:, :128], both[:, 128:]
        q = dot((q_column == q_place + h).astype(BF16), q_all)
        gram = dot(k, k, (1, 1))
        diag = jnp.where(same, gram, 0.0)
        rk_col = lax.rsqrt(jnp.sum(diag, 1, keepdims=True) + 1e-06)
        rk_row = lax.rsqrt(jnp.sum(diag, 0, keepdims=True) + 1e-06)
        run_c, run_r = run_col[:, h : h + 1], run_row[h : h + 1, :]
        beta_c = one_col[:, 2 + h : 3 + h] + two_col[:, 4 + h : 5 + h]
        beta_r = one_row[2 + h : 3 + h, :] + two_row[4 + h : 5 + h, :]
        fade = jnp.exp(jnp.where(below, run_c - run_r, 0.0))
        low = jnp.where(below, (beta_c * rk_col) * fade * gram * rk_row, 0.0)
        keep.append((k, v, q, rk_col, rk_row, run_c, run_r, beta_r, low))
        lowers += [low[:half, :half], low[half:, half:]]

    inverses = unit_lower_inverse(lowers)
    mids = [mm3(keep[h][8][half:, :half], inverses[2 * h]) for h in range(heads)]
    crosses = [mm3(inverses[2 * h + 1], mids[h]) for h in range(heads)]
    for h in range(heads):
        k, v, q, rk_col, rk_row, run_c, run_r, beta_r, low = keep[h]
        a = jnp.concatenate(
            [
                jnp.concatenate([inverses[2 * h], jnp.zeros((half, half), F32)], 1),
                jnp.concatenate([-crosses[h], inverses[2 * h + 1]], 1),
            ],
            0,
        )
        a_val = a * beta_r
        a_key = a_val * (jnp.exp(run_r) * rk_row)
        ah, al = split(a_val)
        u = dot(ah, v) + dot(al, v)
        ah, al = split(a_key)
        w = dot(ah, k) + dot(al, k)
        last = run_c[span - 1 : span, :]
        remain = jnp.exp(last - run_c) * rk_col
        uh, ul = split(u * remain)
        write_t = dot(uh, k, (0, 0)) + dot(ul, k, (0, 0))
        wh, wl = split(w * remain)
        trans = jnp.exp(last) * eye - dot(k, wh, (0, 0)) - dot(k, wl, (0, 0))
        tw_ref[h, 0:64, :] = write_t[:64].astype(BF16)
        tw_ref[h, 64:192, :] = trans.astype(BF16)
        tw_ref[h, 192:256, :] = write_t[64:].astype(BF16)
        tok_run = tok_col[:, h : h + 1]
        rq = lax.rsqrt(jnp.sum(q * q, 1, keepdims=True) + 1e-06)
        qk = dot(q.astype(BF16), k, (1, 1))
        mixing = jnp.where(
            reach, jnp.exp(jnp.where(reach, tok_run - run_r, 0.0)) * qk * rq * rk_row, 0.0
        )
        mh, ml = split(mixing)
        bh, bl = split(jnp.concatenate([w, u], 1))
        mixed = dot(mh, bh) + dot(ml, bh) + dot(mh, bl)
        qt_ref[h] = (jnp.exp(tok_run) * rq) * q - mixed[:, :128]
        lo_ref[h] = mixed[:, 128:]


def chain_step(state, trans, write):
    n = state.shape[0]
    high, low = split(state)
    both = dot(jnp.concatenate([high, low], 0), trans, (1, 1))
    return both[:n] + both[n:] + write.astype(F32)


def main_kernel(
    nz,
    ny,
    inv_ref,
    tw_ref,
    qt_ref,
    lo_ref,
    res_ref,
    og_ref,
    fg_ref,
    up_hbm,
    down_hbm,
    out_ref,
    up_v,
    down_v,
    rx,
    zmsg,
    rz,
    chain,
    pmsg,
    rp,
    xg,
    acc,
    act,
    pair_out,
    pair_in,
    psum,
    rs,
    wsem,
    a_send,
    a_recv,
    b_send,
    b_recv,
    c_send,
    c_recv,
    z_send,
    z_recv,
    p_send,
    p_recv,
    g_send,
    g_recv,
    f_send,
    f_recv,
    o_sem,
    s_send,
    s_recv,
    r_send,
    r_recv,
):
    seq, ten = lax.axis_index("seq"), lax.axis_index("tensor")
    z, x = seq // LANES_X, lax.rem(seq, LANES_X)
    y, core = ten // 2, lax.rem(ten, 2)
    partner = y * 2 + 1 - core
    head, part = x // 2, lax.rem(x, 2)
    groups = up_hbm.shape[0]
    kept = up_hbm.shape[1]

    def at_x(o):
        return lax.rem(x + o, LANES_X)

    def at_y(o):
        return lax.rem(y + o, ny)

    barrier = pltpu.get_barrier_semaphore()
    peers = [(z * LANES_X + at_x(o), ten) for o in range(1, LANES_X)]
    peers += [(lax.rem(z + o, nz) * LANES_X + x, ten) for o in range(1, nz)]
    peers += [(seq, at_y(o) * 2 + core) for o in range(1, ny)]
    peers += [(seq, partner)]
    for peer in peers:
        pl.semaphore_signal(barrier, inc=1, device_id=peer, device_id_type=MESH)

    load_up = pltpu.make_async_copy(up_hbm, up_v.at[:, pl.ds(0, kept)], wsem.at[0])
    load_down = pltpu.make_async_copy(down_hbm, down_v.at[:, pl.ds(0, kept)], wsem.at[1])
    load_up.start()
    load_down.start()
    rx[x] = tw_ref[...]
    for c in range(groups):
        up_v[c, kept] = jnp.zeros(up_v.shape[2:], BF16)
        down_v[c, kept] = jnp.zeros(up_v.shape[2:], BF16)
    chain[...] = jnp.zeros_like(chain)
    pl.semaphore_wait(barrier, len(peers))

    def remote(src, dst, send, recv, peer):
        return pltpu.make_async_remote_copy(
            src_ref=src,
            dst_ref=dst,
            send_sem=send,
            recv_sem=recv,
            device_id=peer,
            device_id_type=MESH,
        )

    def a_copy(o):
        there = at_x(o)
        h2, p2 = there // 2, lax.rem(there, 2)
        rows = pl.ds(pl.multiple_of(p2 * 64, 64), 192)
        return remote(
            tw_ref.at[h2, rows],
            rx.at[x, h2, rows],
            a_send.at[o],
            a_recv.at[x],
            (z * LANES_X + there, ten),
        )

    def b_copies(o):
        there = at_x(o)
        h2, p2 = there // 2, lax.rem(there, 2)
        rows = pl.ds(pl.multiple_of((1 - p2) * 192, 64), 64)
        peer = (z * LANES_X + there, ten)
        return (
            remote(
                tw_ref.at[h2, rows], rx.at[x, h2, rows], b_send.at[o], b_recv.at[x], peer
            ),
            remote(
                tw_ref.at[1 - h2], rx.at[x, 1 - h2], c_send.at[o], c_recv.at[x], peer
            ),
        )

    for o in (2, 1, 3):
        a_copy(o).start()
    my_rows = pl.ds(pl.multiple_of(part * 64, 64), 192)
    for o in (1, 3, 2):
        source = at_x(o)
        remote(
            rx.at[source, head, my_rows],
            rx.at[source, head, my_rows],
            a_send.at[o],
            a_recv.at[source],
            (seq, ten),
        ).wait_recv()

    w_rows = pl.ds(pl.multiple_of(part * 192, 64), 64)
    ts = [rx[i, head, pl.ds(64, 128)] for i in range(LANES_X)]
    ws = [rx[i, head, w_rows] for i in range(LANES_X)]
    t10, t32 = dot(ts[1], ts[0]), dot(ts[3], ts[2])
    w10 = dot(ws[0], ts[1], (1, 1)) + ws[1].astype(F32)
    w32 = dot(ws[2], ts[3], (1, 1)) + ws[3].astype(F32)
    zmsg[64:192] = mm3(t32, t10).astype(BF16)
    th, tl = split(t32)
    wh, wl = split(w10)
    mixed = dot(jnp.concatenate([wh, wl], 0), th, (1, 1))
    w_all = mixed[:64] + mixed[64:] + dot(wh, tl, (1, 1)) + w32
    zmsg[0:64] = w_all.astype(BF16)

    def z_copy(o):
        return remote(
            zmsg,
            rz.at[z],
            z_send.at[o],
            z_recv.at[z],
            ((z + o) * LANES_X + x, ten),
        )

    for o in range(1, nz):

        @pl.when(z + o < nz)
        def _():
            z_copy(o).start()

    for o in range(1, LANES_X):

        @pl.when(x + o < LANES_X)
        def _():
            for one in b_copies(o):
                one.start()

    for i in range(nz - 1):

        @pl.when(i < z)
        def _():
            remote(
                rz.at[i], rz.at[i], z_send.at[0], z_recv.at[i], (seq, ten)
            ).wait_recv()
            if i == 0:
                chain[...] = rz[0, 0:64].astype(F32)
            else:
                chain[...] = chain_step(chain[...], rz[i, 64:192], rz[i, 0:64])

    entering = chain[...].astype(BF16)
    pmsg[...] = entering
    p_rows = pl.ds(pl.multiple_of(part * 64, 64), 64)
    rp[head, p_rows] = entering

    def p_copy(o):
        return remote(
            pmsg,
            rp.at[head, p_rows],
            p_send.at[o],
            p_recv.at[x],
            (z * LANES_X + at_x(o), ten),
        )

    for o in (2, 1, 3):
        p_copy(o).start()
    for i in range(LANES_X - 1):

        @pl.when(i < x)
        def _():
            other = pl.ds(pl.multiple_of((1 - part) * 192, 64), 64)
            remote(
                rx.at[i, head, other],
                rx.at[i, head, other],
                b_send.at[0],
                b_recv.at[i],
                (seq, ten),
            ).wait_recv()
            remote(
                rx.at[i, 1 - head], rx.at[i, 1 - head], c_send.at[0], c_recv.at[i], (seq, ten)
            ).wait_recv()

    for o in (1, 3, 2):
        source = at_x(o)
        rows = pl.ds(pl.multiple_of(lax.rem(source, 2) * 64, 64), 64)
        remote(
            rp.at[source // 2, rows],
            rp.at[source // 2, rows],
            p_send.at[o],
            p_recv.at[source],
            (seq, ten),
        ).wait_recv()

    state = [rp[h].astype(F32) for h in range(2)]
    for i in range(LANES_X - 1):
        for h in range(2):
            write = jnp.concatenate([rx[i, h, 0:64], rx[i, h, 192:256]], 0)
            moved = chain_step(state[h], rx[i, h, 64:192], write)
            state[h] = jnp.where(i < x, moved, state[h])

    gain = og_ref[...]
    pieces = []
    for h in range(2):
        qh, ql = split(qt_ref[h])
        sh, sl = split(state[h])
        head_out = dot(qh, sh, (1, 1)) + dot(ql, sh, (1, 1)) + dot(qh, sl, (1, 1)) + lo_ref[h]
        power = jnp.mean(head_out * head_out, -1, keepdims=True)
        normed = head_out * lax.rsqrt(power + 1e-05) * gain
        pieces.append(res_ref[:, 128 * h : 128 * h + 128].astype(F32) + normed)
    xg[ten] = jnp.concatenate(pieces, 1).astype(BF16)

    reach = ny // 2
    ways = (1, -1)
    halves = [pl.ds(0, xg.shape[1] // 2), pl.ds(xg.shape[1] // 2, xg.shape[1] // 2)]

    def sent(i, d, part_at):
        return d < reach or part_at == i

    messages = [
        (i, d, p)
        for d in range(1, reach + 1)
        for p in range(2)
        for i in range(2)
        if sent(i, d, p)
    ]

    def neighbour(i):
        return (seq, at_y(ways[i] + ny) * 2 + core)

    def ring(i, d, p):
        block = xg.at[at_y(ny - ways[i] * (d - 1)) * 2 + core, halves[p]]
        return remote(block, block, g_send.at[i, d, p], g_recv.at[i, d, p], neighbour(i))

    def got(i, d, p):
        block = xg.at[at_y(ny - ways[i] * d) * 2 + core, halves[p]]
        remote(block, block, g_send.at[i, d, p], g_recv.at[i, d, p], (seq, ten)).wait_recv()

    def pass_on(i, d, p):
        block = xg.at[at_y(ny - ways[i] * d) * 2 + core, halves[p]]
        return remote(block, block, f_send.at[i, d, p], f_recv.at[i, d, p], (seq, partner))

    def passed(i, d, p):
        block = xg.at[at_y(ny - ways[i] * d) * 2 + 1 - core, halves[p]]
        remote(block, block, f_send.at[i, d, p], f_recv.at[i, d, p], (seq, ten)).wait_recv()

    def own_copy():
        return remote(xg.at[ten], xg.at[ten], o_sem.at[0], o_sem.at[1], (seq, partner))

    for i, d, p in messages:
        if d == 1:
            ring(i, d, p).start()
    own_copy().start()

    load_up.wait()
    load_down.wait()

    def absorb(slot, first, power):
        wide = xg[slot].astype(F32)
        power = power + jnp.sum(wide * wide, -1, keepdims=True)
        scaled = (wide * fg_ref[slot]).astype(BF16)
        weights = jnp.concatenate(
            [
                jnp.concatenate(
                    [up_v[c, inv_ref[0, c, 2 * slot + b]] for c in range(groups)], 1
                )
                for b in range(2)
            ],
            0,
        )
        term = dot(scaled, weights)
        if first:
            acc[...] = term
        else:
            acc[...] += term
        return power

    def blocks(d):
        return [at_y(d)] if d == reach else [at_y(ny - d), at_y(d)]

    power = absorb(ten, True, jnp.zeros((xg.shape[1], 1), F32))
    remote(xg.at[partner], xg.at[partner], o_sem.at[0], o_sem.at[1], (seq, ten)).wait_recv()
    power = absorb(partner, False, power)
    for d in range(1, reach + 1):
        for i, e, p in messages:
            if e == d:
                got(i, d, p)
                if d < reach and sent(i, d + 1, p):
                    ring(i, d + 1, p).start()
                pass_on(i, d, p).start()
        if d > 1:
            for i, e, p in messages:
                if e == d - 1:
                    passed(i, e, p)
            for where in blocks(d - 1):
                power = absorb(where * 2 + 1 - core, False, power)
        for where in blocks(d):
            power = absorb(where * 2 + core, False, power)
    for i, e, p in messages:
        if e == reach:
            passed(i, e, p)
    for where in blocks(reach):
        power = absorb(where * 2 + 1 - core, False, power)

    width = 256 * xg.shape[0]
    scale = lax.rsqrt(power / width + 1e-05)
    act[...] = jax.nn.gelu(acc[...] * scale).astype(BF16)

    def share(slot):
        weights = jnp.concatenate(
            [
                jnp.concatenate(
                    [down_v[c, inv_ref[1, c, 2 * slot + b]] for b in range(2)], 1
                )
                for c in range(groups)
            ],
            0,
        )
        return dot(act[...], weights).astype(BF16)

    def s_copy(off):
        k = off + reach - 1
        return remote(
            pair_out.at[k], pair_in.at[k], s_send.at[k], s_recv.at[k], (seq, partner)
        )

    def offer(off):
        pair_out[off + reach - 1] = share(at_y(ny + off) * 2 + 1 - core)
        s_copy(off).start()

    def pair_sum(off):
        mine = share(at_y(ny + off) * 2 + core).astype(F32)
        s_copy(off).wait_recv()
        return mine + pair_in[off + reach - 1].astype(F32)

    def m_copy(i, d, p):
        return remote(
            psum.at[i, d, halves[p]],
            rs.at[i, d, halves[p]],
            r_send.at[i, d, p],
            r_recv.at[i, d, p],
            neighbour(i),
        )

    def m_got(i, d, p):
        block = rs.at[i, d, halves[p]]
        remote(block, block, r_send.at[i, d, p], r_recv.at[i, d, p], (seq, ten)).wait_recv()
        return rs[i, d, halves[p]].astype(F32)

    rows_dev = xg.shape[1] // 2

    def rows_of(value, p):
        return value[p * rows_dev : (p + 1) * rows_dev]

    def offer_level(d):
        for off in (d, -d) if d else (0,):
            offer(off)

    offer(reach)
    offer_level(reach - 1)
    far = pair_sum(reach)
    for i in range(2):
        psum[i, reach, halves[i]] = rows_of(far, i).astype(BF16)
        m_copy(i, reach, i).start()
    for d in range(reach - 1, 0, -1):
        offer_level(d - 1)
        sums = [pair_sum(d), pair_sum(-d)]
        for fresh in (True, False):
            for p in range(2):
                for i in range(2):
                    if sent(i, d + 1, p) == fresh:
                        continue
                    value = rows_of(sums[i], p)
                    if not fresh:
                        value = value + m_got(i, d + 1, p)
                    psum[i, d, halves[p]] = value.astype(BF16)
                    m_copy(i, d, p).start()
    total = pair_sum(0) + xg[ten].astype(F32)
    for p in range(2):
        value = rows_of(total, p)
        for i in range(2):
            if sent(i, 1, p):
                value = value + m_got(i, 1, p)
        out_ref[halves[p], :] = value.astype(BF16)

    for o in range(1, LANES_X):
        a_copy(o).wait_send()
        p_copy(o).wait_send()

        @pl.when(x + o < LANES_X)
        def _():
            for one in b_copies(o):
                one.wait_send()

    for o in range(1, nz):

        @pl.when(z + o < nz)
        def _():
            z_copy(o).wait_send()

    own_copy().wait_send()
    for off in range(1 - reach, reach + 1):
        s_copy(off).wait_send()
    for i, d, p in messages:
        ring(i, d, p).wait_send()
        pass_on(i, d, p).wait_send()
        m_copy(i, d, p).wait_send()


def solution(mesh):
    nseq, nten = mesh.shape["seq"], mesh.shape["tensor"]
    nz, ny = nseq // LANES_X, nten // 2
    vmem = pl.BlockSpec(memory_space=pltpu.VMEM)
    smem = pl.BlockSpec(memory_space=pltpu.SMEM)
    anywhere = pl.BlockSpec(memory_space=pl.ANY)
    dma = pltpu.SemaphoreType.DMA

    def per_device(
        queries,
        keys,
        values,
        beta,
        decay,
        out_gain,
        residual,
        ffn_gain,
        up_blocks,
        up_index,
        down_kept_tiles,
        down_index,
    ):
        tok = queries.shape[0]
        groups, kept = up_index.shape
        tiles = 2 * nten
        tw, qt, lo, inv = pl.pallas_call(
            local_kernel,
            out_shape=(
                jax.ShapeDtypeStruct((2, 256, 128), BF16),
                jax.ShapeDtypeStruct((2, tok, 128), F32),
                jax.ShapeDtypeStruct((2, tok, 128), F32),
                jax.ShapeDtypeStruct((2, groups, tiles), jnp.int32),
            ),
            in_specs=[vmem] * 5 + [smem] * 2,
            out_specs=(vmem, vmem, vmem, smem),
            name="local_terms",
        )(
            queries.reshape(2 * tok, 128),
            keys.reshape(4 * tok, 128),
            values.reshape(4 * tok, 128),
            beta,
            decay,
            up_index,
            down_index,
        )
        return pl.pallas_call(
            functools.partial(main_kernel, nz, ny),
            out_shape=jax.ShapeDtypeStruct((tok, 256), BF16),
            in_specs=[smem] + [vmem] * 6 + [anywhere] * 2,
            out_specs=vmem,
            scratch_shapes=[
                pltpu.VMEM((groups, kept + 1, 128, 128), BF16),
                pltpu.VMEM((groups, kept + 1, 128, 128), BF16),
                pltpu.VMEM((LANES_X, 2, 256, 128), BF16),
                pltpu.VMEM((192, 128), BF16),
                pltpu.VMEM((nz, 192, 128), BF16),
                pltpu.VMEM((64, 128), F32),
                pltpu.VMEM((64, 128), BF16),
                pltpu.VMEM((2, 128, 128), BF16),
                pltpu.VMEM((nten, tok, 256), BF16),
                pltpu.VMEM((tok, groups * 128), F32),
                pltpu.VMEM((tok, groups * 128), BF16),
                pltpu.VMEM((ny, tok, 256), BF16),
                pltpu.VMEM((ny, tok, 256), BF16),
                pltpu.VMEM((2, ny // 2 + 1, tok, 256), BF16),
                pltpu.VMEM((2, ny // 2 + 1, tok, 256), BF16),
                dma((2,)),
                dma((LANES_X,)),
                dma((LANES_X,)),
                dma((LANES_X,)),
                dma((LANES_X,)),
                dma((LANES_X,)),
                dma((LANES_X,)),
                dma((nz,)),
                dma((nz,)),
                dma((LANES_X,)),
                dma((LANES_X,)),
                dma((2, ny // 2 + 1, 2)),
                dma((2, ny // 2 + 1, 2)),
                dma((2, ny // 2 + 1, 2)),
                dma((2, ny // 2 + 1, 2)),
                dma((2,)),
                dma((ny,)),
                dma((ny,)),
                dma((2, ny // 2 + 1, 2)),
                dma((2, ny // 2 + 1, 2)),
            ],
            compiler_params=pltpu.CompilerParams(collective_id=0, has_side_effects=True),
            name="scan_and_ffn",
        )(
            inv,
            tw,
            qt,
            lo,
            residual,
            out_gain.reshape(1, 128),
            ffn_gain.reshape(nten, 1, 256),
            up_blocks,
            down_kept_tiles,
        )

    placed = (
        P("seq", "tensor", None),
        P(None, "seq", "tensor", None),
        P(None, "seq", "tensor", None),
        P(None, "tensor", "seq"),
        P("tensor", "seq"),
        P(),
        P("seq", "tensor"),
        P(),
        P("tensor", None, None, None),
        P("tensor", None),
        P("tensor", None, None, None),
        P("tensor", None),
    )
    return jax.shard_map(
        per_device, mesh=mesh, in_specs=placed, out_specs=P("seq", "tensor"), check_vma=False
    )
```

```python
import functools

import jax
import jax.numpy as jnp
from jax import lax
from jax.experimental import pallas as pl
from jax.experimental.pallas import tpu as pltpu
from jax.sharding import PartitionSpec as P

F32 = jnp.float32
BF16 = jnp.bfloat16
HIGHEST = lax.Precision.HIGHEST
LANES_X = 4
VMEM_LIMIT = 24 << 20
MESH = pl.DeviceIdType.MESH


def dot(a, b, contract=(1, 0), precision=None):
    return lax.dot_general(
        a,
        b,
        (((contract[0],), (contract[1],)), ((), ())),
        precision=precision,
        preferred_element_type=F32,
    )


def split(a):
    high = a.astype(BF16)
    return high, (a - high.astype(F32)).astype(BF16)


def mm3(a, b):
    ah, al = split(a)
    bh, bl = split(b)
    left = jnp.concatenate([ah, al], 1)
    right = jnp.concatenate(
        [jnp.concatenate([bh, bl], 1), jnp.concatenate([bh, jnp.zeros_like(bl)], 1)], 0
    )
    both = dot(left, right)
    n = b.shape[1]
    return both[:, :n] + both[:, n:]


def iota(shape, axis):
    return lax.broadcasted_iota(jnp.int32, shape, axis)


def unit_lower_inverse(lowers):
    n = lowers[0].shape[0]
    rows, cols = iota((n, n), 0), iota((n, n), 1)
    eye = (rows == cols).astype(F32)
    base = (rows >> 3) == (cols >> 3)
    n1 = [jnp.where(base, -low, 0.0) for low in lowers]
    n2 = [mm3(a, a) for a in n1]
    n3 = [mm3(a, b) for a, b in zip(n1, n2)]
    n4 = [mm3(a, a) for a in n2]
    y = [eye + a + b + c for a, b, c in zip(n1, n2, n3)]
    x = [a + mm3(a, b) for a, b in zip(y, n4)]
    shift = 3
    while (1 << shift) < n:
        pick = ((rows >> (shift + 1)) == (cols >> (shift + 1))) & ((rows >> shift) != (cols >> shift))
        links = [jnp.where(pick, low, 0.0) for low in lowers]
        right = [mm3(c, a) for c, a in zip(links, x)]
        x = [a - mm3(a, b) for a, b in zip(x, right)]
        shift += 1
    return x


def inverse_table(index, kept):
    lanes = iota((index.shape[0], 128), 1)
    found = jnp.full(lanes.shape, kept, jnp.int32)
    for j in range(kept):
        found = jnp.where(index[:, j : j + 1] == lanes, j, found)
    return found


def local_terms(q_ref, k_ref, v_ref, beta_ref, decay_ref, tw_ref, qt_ref, lo_ref):
    tok = q_ref.shape[0] // 2
    span = 2 * tok
    heads = 2
    half = span // 2

    kv = jnp.concatenate([k_ref[...], v_ref[...]], 1)
    q_all = q_ref[...]
    small = jnp.concatenate(
        [decay_ref[...], beta_ref[0], beta_ref[1], jnp.zeros((2, tok), F32)], 0
    )
    m_at, t_at = iota((span, tok), 0), iota((span, tok), 1)
    upto = (t_at <= (m_at >> 1)).astype(F32)
    first = ((t_at == (m_at >> 1)) & ((m_at & 1) == 0)).astype(F32)
    second = ((t_at == (m_at >> 1)) & ((m_at & 1) == 1)).astype(F32)
    upto_tok = (iota((tok, tok), 1) <= iota((tok, tok), 0)).astype(F32)
    run_col = dot(upto, small, (1, 1), HIGHEST)
    run_row = dot(small, upto, (1, 1), HIGHEST)
    tok_col = dot(upto_tok, small, (1, 1), HIGHEST)
    one_col, two_col = dot(first, small, (1, 1), HIGHEST), dot(second, small, (1, 1), HIGHEST)
    one_row, two_row = dot(small, first, (1, 1), HIGHEST), dot(small, second, (1, 1), HIGHEST)

    rows, cols = iota((span, span), 0), iota((span, span), 1)
    below = cols < rows
    same = rows == cols
    reach = iota((tok, span), 1) <= 2 * iota((tok, span), 0) + 1
    eye = (iota((tok, tok), 0) == iota((tok, tok), 1)).astype(F32)
    row_of = iota((span, 4 * tok), 0)
    place = (row_of & 1) * span + (row_of >> 1) * 2
    column = iota((span, 4 * tok), 1)
    q_place = iota((tok, span), 0) * 2
    q_column = iota((tok, span), 1)

    ks, vs, qs, gammas, lowers, keep = [], [], [], [], [], []
    for h in range(heads):
        pick = (column == place + h).astype(BF16)
        both = dot(pick, kv).astype(BF16)
        k, v = both[:, :128], both[:, 128:]
        q = dot((q_column == q_place + h).astype(BF16), q_all)
        gram = dot(k, k, (1, 1))
        diag = jnp.where(same, gram, 0.0)
        rk_col = lax.rsqrt(jnp.sum(diag, 1, keepdims=True) + 1e-06)
        rk_row = lax.rsqrt(jnp.sum(diag, 0, keepdims=True) + 1e-06)
        run_c, run_r = run_col[:, h : h + 1], run_row[h : h + 1, :]
        beta_c = one_col[:, 2 + h : 3 + h] + two_col[:, 4 + h : 5 + h]
        beta_r = one_row[2 + h : 3 + h, :] + two_row[4 + h : 5 + h, :]
        fade = jnp.exp(jnp.where(below, run_c - run_r, 0.0))
        low = jnp.where(below, (beta_c * rk_col) * fade * gram * rk_row, 0.0)
        keep.append((k, v, q, rk_col, rk_row, run_c, run_r, beta_r, low))
        lowers += [low[:half, :half], low[half:, half:]]

    inverses = unit_lower_inverse(lowers)
    mids = [mm3(keep[h][8][half:, :half], inverses[2 * h]) for h in range(heads)]
    crosses = [mm3(inverses[2 * h + 1], mids[h]) for h in range(heads)]
    for h in range(heads):
        k, v, q, rk_col, rk_row, run_c, run_r, beta_r, low = keep[h]
        a = jnp.concatenate(
            [
                jnp.concatenate([inverses[2 * h], jnp.zeros((half, half), F32)], 1),
                jnp.concatenate([-crosses[h], inverses[2 * h + 1]], 1),
            ],
            0,
        )
        a_val = a * beta_r
        a_key = a_val * (jnp.exp(run_r) * rk_row)
        ah, al = split(a_val)
        u = dot(ah, v) + dot(al, v)
        ah, al = split(a_key)
        w = dot(ah, k) + dot(al, k)
        last = run_c[span - 1 : span, :]
        remain = jnp.exp(last - run_c) * rk_col
        uh, ul = split(u * remain)
        write_t = dot(uh, k, (0, 0)) + dot(ul, k, (0, 0))
        wh, wl = split(w * remain)
        trans = jnp.exp(last) * eye - dot(k, wh, (0, 0)) - dot(k, wl, (0, 0))
        tw_ref[h, 0:64, :] = write_t[:64].astype(BF16)
        tw_ref[h, 64:192, :] = trans.astype(BF16)
        tw_ref[h, 192:256, :] = write_t[64:].astype(BF16)
        tok_run = tok_col[:, h : h + 1]
        rq = lax.rsqrt(jnp.sum(q * q, 1, keepdims=True) + 1e-06)
        qk = dot(q.astype(BF16), k, (1, 1))
        mixing = jnp.where(
            reach, jnp.exp(jnp.where(reach, tok_run - run_r, 0.0)) * qk * rq * rk_row, 0.0
        )
        mh, ml = split(mixing)
        bh, bl = split(jnp.concatenate([w, u], 1))
        mixed = dot(mh, bh) + dot(ml, bh) + dot(mh, bl)
        qt_ref[h] = (jnp.exp(tok_run) * rq) * q - mixed[:, :128]
        lo_ref[h] = mixed[:, 128:]


def chain_step(state, trans, write):
    n = state.shape[0]
    high, low = split(state)
    both = dot(jnp.concatenate([high, low], 0), trans, (1, 1))
    return both[:n] + both[n:] + write.astype(F32)


def main_kernel(
    nz,
    ny,
    q_ref,
    k_ref,
    v_ref,
    beta_ref,
    decay_ref,
    up_ref,
    down_ref,
    res_ref,
    og_ref,
    fg_ref,
    up_hbm,
    down_hbm,
    out_ref,
    qt_ref,
    lo_ref,
    table_v,
    inv_ref,
    up_v,
    down_v,
    rx,
    zmsg,
    rz,
    chain,
    pmsg,
    rp,
    xg,
    acc,
    act,
    pair_out,
    pair_in,
    psum,
    rs,
    wsem,
    a_send,
    a_recv,
    b_send,
    b_recv,
    c_send,
    c_recv,
    z_send,
    z_recv,
    p_send,
    p_recv,
    g_send,
    g_recv,
    f_send,
    f_recv,
    o_sem,
    s_send,
    s_recv,
    r_send,
    r_recv,
):
    seq, ten = lax.axis_index("seq"), lax.axis_index("tensor")
    z, x = seq // LANES_X, lax.rem(seq, LANES_X)
    y, core = ten // 2, lax.rem(ten, 2)
    partner = y * 2 + 1 - core
    head, part = x // 2, lax.rem(x, 2)
    groups = up_hbm.shape[0]
    kept = up_hbm.shape[1]

    def at_x(o):
        return lax.rem(x + o, LANES_X)

    def at_y(o):
        return lax.rem(y + o, ny)

    barrier = pltpu.get_barrier_semaphore()
    peers = [(z * LANES_X + at_x(o), ten) for o in range(1, LANES_X)]
    peers += [(lax.rem(z + o, nz) * LANES_X + x, ten) for o in range(1, nz)]
    peers += [(seq, at_y(o) * 2 + core) for o in (1, 2, ny - 2, ny - 1)]
    peers += [(seq, partner)]
    for peer in peers:
        pl.semaphore_signal(barrier, inc=1, device_id=peer, device_id_type=MESH)

    load_up = pltpu.make_async_copy(up_hbm, up_v.at[:, pl.ds(0, kept)], wsem.at[0])
    load_down = pltpu.make_async_copy(down_hbm, down_v.at[:, pl.ds(0, kept)], wsem.at[1])
    load_up.start()
    load_down.start()
    for c in range(groups):
        up_v[c, kept] = jnp.zeros(up_v.shape[2:], BF16)
        down_v[c, kept] = jnp.zeros(up_v.shape[2:], BF16)
    chain[...] = jnp.zeros_like(chain)
    table_v[0:groups] = inverse_table(up_ref[...], kept)
    table_v[groups : 2 * groups] = inverse_table(down_ref[...], kept)
    load_table = pltpu.make_async_copy(table_v, inv_ref, wsem.at[2])
    load_table.start()
    local_terms(q_ref, k_ref, v_ref, beta_ref, decay_ref, rx.at[x], qt_ref, lo_ref)
    pl.semaphore_wait(barrier, len(peers))

    def remote(src, dst, send, recv, peer):
        return pltpu.make_async_remote_copy(
            src_ref=src,
            dst_ref=dst,
            send_sem=send,
            recv_sem=recv,
            device_id=peer,
            device_id_type=MESH,
        )

    def a_copy(o):
        there = at_x(o)
        h2, p2 = there // 2, lax.rem(there, 2)
        rows = pl.ds(pl.multiple_of(p2 * 64, 64), 192)
        return remote(
            rx.at[x, h2, rows],
            rx.at[x, h2, rows],
            a_send.at[o],
            a_recv.at[x],
            (z * LANES_X + there, ten),
        )

    def b_copies(o):
        there = at_x(o)
        h2, p2 = there // 2, lax.rem(there, 2)
        rows = pl.ds(pl.multiple_of((1 - p2) * 192, 64), 64)
        peer = (z * LANES_X + there, ten)
        return (
            remote(
                rx.at[x, h2, rows], rx.at[x, h2, rows], b_send.at[o], b_recv.at[x], peer
            ),
            remote(
                rx.at[x, 1 - h2], rx.at[x, 1 - h2], c_send.at[o], c_recv.at[x], peer
            ),
        )

    for o in (2, 1, 3):
        a_copy(o).start()
    my_rows = pl.ds(pl.multiple_of(part * 64, 64), 192)
    for o in (1, 3, 2):
        source = at_x(o)
        remote(
            rx.at[source, head, my_rows],
            rx.at[source, head, my_rows],
            a_send.at[o],
            a_recv.at[source],
            (seq, ten),
        ).wait_recv()

    w_rows = pl.ds(pl.multiple_of(part * 192, 64), 64)
    ts = [rx[i, head, pl.ds(64, 128)] for i in range(LANES_X)]
    ws = [rx[i, head, w_rows] for i in range(LANES_X)]
    t10, t32 = dot(ts[1], ts[0]), dot(ts[3], ts[2])
    w10 = dot(ws[0], ts[1], (1, 1)) + ws[1].astype(F32)
    w32 = dot(ws[2], ts[3], (1, 1)) + ws[3].astype(F32)
    zmsg[64:192] = mm3(t32, t10).astype(BF16)
    th, tl = split(t32)
    wh, wl = split(w10)
    mixed = dot(jnp.concatenate([wh, wl], 0), th, (1, 1))
    w_all = mixed[:64] + mixed[64:] + dot(wh, tl, (1, 1)) + w32
    zmsg[0:64] = w_all.astype(BF16)

    def z_copy(o):
        return remote(
            zmsg,
            rz.at[z],
            z_send.at[o],
            z_recv.at[z],
            ((z + o) * LANES_X + x, ten),
        )

    for o in range(1, nz):

        @pl.when(z + o < nz)
        def _():
            z_copy(o).start()

    for o in range(1, LANES_X):

        @pl.when(x + o < LANES_X)
        def _():
            for one in b_copies(o):
                one.start()

    for i in range(nz - 1):

        @pl.when(i < z)
        def _():
            remote(
                rz.at[i], rz.at[i], z_send.at[0], z_recv.at[i], (seq, ten)
            ).wait_recv()
            if i == 0:
                chain[...] = rz[0, 0:64].astype(F32)
            else:
                chain[...] = chain_step(chain[...], rz[i, 64:192], rz[i, 0:64])

    entering = chain[...].astype(BF16)
    pmsg[...] = entering
    p_rows = pl.ds(pl.multiple_of(part * 64, 64), 64)
    rp[head, p_rows] = entering

    def p_copy(o):
        return remote(
            pmsg,
            rp.at[head, p_rows],
            p_send.at[o],
            p_recv.at[x],
            (z * LANES_X + at_x(o), ten),
        )

    for o in (2, 1, 3):
        p_copy(o).start()
    for i in range(LANES_X - 1):

        @pl.when(i < x)
        def _():
            other = pl.ds(pl.multiple_of((1 - part) * 192, 64), 64)
            remote(
                rx.at[i, head, other],
                rx.at[i, head, other],
                b_send.at[0],
                b_recv.at[i],
                (seq, ten),
            ).wait_recv()
            remote(
                rx.at[i, 1 - head], rx.at[i, 1 - head], c_send.at[0], c_recv.at[i], (seq, ten)
            ).wait_recv()

    for o in (1, 3, 2):
        source = at_x(o)
        rows = pl.ds(pl.multiple_of(lax.rem(source, 2) * 64, 64), 64)
        remote(
            rp.at[source // 2, rows],
            rp.at[source // 2, rows],
            p_send.at[o],
            p_recv.at[source],
            (seq, ten),
        ).wait_recv()

    state = [rp[h].astype(F32) for h in range(2)]
    for i in range(LANES_X - 1):
        for h in range(2):
            write = jnp.concatenate([rx[i, h, 0:64], rx[i, h, 192:256]], 0)
            moved = chain_step(state[h], rx[i, h, 64:192], write)
            state[h] = jnp.where(i < x, moved, state[h])

    gain = og_ref[...]
    pieces = []
    for h in range(2):
        qh, ql = split(qt_ref[h])
        sh, sl = split(state[h])
        head_out = dot(qh, sh, (1, 1)) + dot(ql, sh, (1, 1)) + dot(qh, sl, (1, 1)) + lo_ref[h]
        power = jnp.mean(head_out * head_out, -1, keepdims=True)
        normed = head_out * lax.rsqrt(power + 1e-05) * gain
        pieces.append(res_ref[:, 128 * h : 128 * h + 128].astype(F32) + normed)
    xg[ten] = jnp.concatenate(pieces, 1).astype(BF16)

    reach = ny // 2
    ways = (1, -1)
    halves = [pl.ds(0, xg.shape[1] // 2), pl.ds(xg.shape[1] // 2, xg.shape[1] // 2)]

    def sent(i, d, part_at):
        return d < reach or part_at == i

    messages = [
        (i, d, p)
        for d in range(1, reach + 1)
        for p in range(2)
        for i in range(2)
        if sent(i, d, p)
    ]

    hop = (0, 1, 2, 1, 2)

    def across(i, d):
        return (seq, at_y(ny + ways[i] * hop[d]) * 2 + core)

    def ring(i, d, p):
        origin = 0 if d <= 2 else 2
        block = xg.at[at_y(ny - ways[i] * origin) * 2 + core, halves[p]]
        return remote(block, block, g_send.at[i, d, p], g_recv.at[i, d, p], across(i, d))

    def got(i, d, p):
        block = xg.at[at_y(ny - ways[i] * d) * 2 + core, halves[p]]
        remote(block, block, g_send.at[i, d, p], g_recv.at[i, d, p], (seq, ten)).wait_recv()

    def pass_on(i, d, p):
        block = xg.at[at_y(ny - ways[i] * d) * 2 + core, halves[p]]
        return remote(block, block, f_send.at[i, d, p], f_recv.at[i, d, p], (seq, partner))

    def passed(i, d, p):
        block = xg.at[at_y(ny - ways[i] * d) * 2 + 1 - core, halves[p]]
        remote(block, block, f_send.at[i, d, p], f_recv.at[i, d, p], (seq, ten)).wait_recv()

    def own_copy():
        return remote(xg.at[ten], xg.at[ten], o_sem.at[0], o_sem.at[1], (seq, partner))

    for level in (2, 1):
        for i, d, p in messages:
            if d == level:
                ring(i, d, p).start()
    own_copy().start()

    load_up.wait()
    load_down.wait()
    load_table.wait()

    def absorb(slot, first, power):
        wide = xg[slot].astype(F32)
        power = power + jnp.sum(wide * wide, -1, keepdims=True)
        scaled = (wide * fg_ref[slot]).astype(BF16)
        weights = jnp.concatenate(
            [
                jnp.concatenate(
                    [up_v[c, inv_ref[c, 2 * slot + b]] for c in range(groups)], 1
                )
                for b in range(2)
            ],
            0,
        )
        term = dot(scaled, weights)
        if first:
            acc[...] = term
        else:
            acc[...] += term
        return power

    def blocks(d):
        return [at_y(d)] if d == reach else [at_y(ny - d), at_y(d)]

    power = absorb(ten, True, jnp.zeros((xg.shape[1], 1), F32))
    remote(xg.at[partner], xg.at[partner], o_sem.at[0], o_sem.at[1], (seq, ten)).wait_recv()
    power = absorb(partner, False, power)

    def take(d):
        for i, e, p in messages:
            if e == d:
                got(i, d, p)
                if d == 2:
                    for later in (4, 3):
                        if sent(i, later, p):
                            ring(i, later, p).start()
                pass_on(i, d, p).start()

    def near(d, power):
        for where in blocks(d):
            power = absorb(where * 2 + core, False, power)
        return power

    def far_side(d, power):
        for i, e, p in messages:
            if e == d:
                passed(i, e, p)
        for where in blocks(d):
            power = absorb(where * 2 + 1 - core, False, power)
        return power

    take(2)
    power = near(2, power)
    take(1)
    power = near(1, power)
    power = far_side(2, power)
    power = far_side(1, power)
    take(3)
    power = near(3, power)
    take(4)
    power = near(4, power)
    power = far_side(3, power)
    power = far_side(4, power)

    width = 256 * xg.shape[0]
    scale = lax.rsqrt(power / width + 1e-05)
    act[...] = jax.nn.gelu(acc[...] * scale).astype(BF16)

    def share(slot):
        weights = jnp.concatenate(
            [
                jnp.concatenate(
                    [down_v[c, inv_ref[groups + c, 2 * slot + b]] for b in range(2)], 1
                )
                for c in range(groups)
            ],
            0,
        )
        return dot(act[...], weights).astype(BF16)

    def s_copy(off):
        k = off + reach - 1
        return remote(
            pair_out.at[k], pair_in.at[k], s_send.at[k], s_recv.at[k], (seq, partner)
        )

    def offer(off):
        pair_out[off + reach - 1] = share(at_y(ny + off) * 2 + 1 - core)
        s_copy(off).start()

    def pair_sum(off):
        mine = share(at_y(ny + off) * 2 + core).astype(F32)
        s_copy(off).wait_recv()
        return mine + pair_in[off + reach - 1].astype(F32)

    def m_copy(i, d, p):
        return remote(
            psum.at[i, d, halves[p]],
            rs.at[i, d, halves[p]],
            r_send.at[i, d, p],
            r_recv.at[i, d, p],
            across(i, d),
        )

    def m_got(i, d, p):
        block = rs.at[i, d, halves[p]]
        remote(block, block, r_send.at[i, d, p], r_recv.at[i, d, p], (seq, ten)).wait_recv()
        return rs[i, d, halves[p]].astype(F32)

    rows_dev = xg.shape[1] // 2

    def rows_of(value, p):
        return value[p * rows_dev : (p + 1) * rows_dev]

    def ship(i, d, p, value):
        psum[i, d, halves[p]] = value.astype(BF16)
        m_copy(i, d, p).start()

    def ship_both(d):
        for i in range(2):
            value = pair_sum(ways[i] * d)
            for p in range(2):
                ship(i, d, p, rows_of(value, p))

    for off in (4, 3, -3):
        offer(off)
    far = pair_sum(4)
    for i in range(2):
        ship(i, 4, i, rows_of(far, i))
    for off in (2, -2):
        offer(off)
    ship_both(3)
    for off in (1, -1, 0):
        offer(off)
    ship_both(1)
    sums = [pair_sum(2), pair_sum(-2)]
    total = pair_sum(0) + xg[ten].astype(F32)
    for p in range(2):
        for i in range(2):
            value = rows_of(sums[i], p) + m_got(i, 3, p)
            if sent(i, 4, p):
                value = value + m_got(i, 4, p)
            ship(i, 2, p, value)
    for p in range(2):
        value = rows_of(total, p)
        for d in (1, 2):
            for i in range(2):
                value = value + m_got(i, d, p)
        out_ref[halves[p], :] = value.astype(BF16)

    for o in range(1, LANES_X):
        a_copy(o).wait_send()
        p_copy(o).wait_send()

        @pl.when(x + o < LANES_X)
        def _():
            for one in b_copies(o):
                one.wait_send()

    for o in range(1, nz):

        @pl.when(z + o < nz)
        def _():
            z_copy(o).wait_send()

    own_copy().wait_send()
    for off in range(1 - reach, reach + 1):
        s_copy(off).wait_send()
    for i, d, p in messages:
        ring(i, d, p).wait_send()
        pass_on(i, d, p).wait_send()
        m_copy(i, d, p).wait_send()


def solution(mesh):
    nseq, nten = mesh.shape["seq"], mesh.shape["tensor"]
    nz, ny = nseq // LANES_X, nten // 2
    vmem = pl.BlockSpec(memory_space=pltpu.VMEM)
    anywhere = pl.BlockSpec(memory_space=pl.ANY)
    dma = pltpu.SemaphoreType.DMA

    def per_device(
        queries,
        keys,
        values,
        beta,
        decay,
        out_gain,
        residual,
        ffn_gain,
        up_blocks,
        up_index,
        down_kept_tiles,
        down_index,
    ):
        tok = queries.shape[0]
        groups, kept = up_index.shape
        return pl.pallas_call(
            functools.partial(main_kernel, nz, ny),
            out_shape=jax.ShapeDtypeStruct((tok, 256), BF16),
            in_specs=[vmem] * 10 + [anywhere] * 2,
            out_specs=vmem,
            scratch_shapes=[
                pltpu.VMEM((2, tok, 128), F32),
                pltpu.VMEM((2, tok, 128), F32),
                pltpu.VMEM((2 * groups, 128), jnp.int32),
                pltpu.SMEM((2 * groups, 128), jnp.int32),
                pltpu.VMEM((groups, kept + 1, 128, 128), BF16),
                pltpu.VMEM((groups, kept + 1, 128, 128), BF16),
                pltpu.VMEM((LANES_X, 2, 256, 128), BF16),
                pltpu.VMEM((192, 128), BF16),
                pltpu.VMEM((nz, 192, 128), BF16),
                pltpu.VMEM((64, 128), F32),
                pltpu.VMEM((64, 128), BF16),
                pltpu.VMEM((2, 128, 128), BF16),
                pltpu.VMEM((nten, tok, 256), BF16),
                pltpu.VMEM((tok, groups * 128), F32),
                pltpu.VMEM((tok, groups * 128), BF16),
                pltpu.VMEM((ny, tok, 256), BF16),
                pltpu.VMEM((ny, tok, 256), BF16),
                pltpu.VMEM((2, ny // 2 + 1, tok, 256), BF16),
                pltpu.VMEM((2, ny // 2 + 1, tok, 256), BF16),
                dma((3,)),
                dma((LANES_X,)),
                dma((LANES_X,)),
                dma((LANES_X,)),
                dma((LANES_X,)),
                dma((LANES_X,)),
                dma((LANES_X,)),
                dma((nz,)),
                dma((nz,)),
                dma((LANES_X,)),
                dma((LANES_X,)),
                dma((2, ny // 2 + 1, 2)),
                dma((2, ny // 2 + 1, 2)),
                dma((2, ny // 2 + 1, 2)),
                dma((2, ny // 2 + 1, 2)),
                dma((2,)),
                dma((ny,)),
                dma((ny,)),
                dma((2, ny // 2 + 1, 2)),
                dma((2, ny // 2 + 1, 2)),
            ],
            compiler_params=pltpu.CompilerParams(
                collective_id=0, has_side_effects=True, vmem_limit_bytes=VMEM_LIMIT
            ),
            name="layer",
        )(
            queries.reshape(2 * tok, 128),
            keys.reshape(4 * tok, 128),
            values.reshape(4 * tok, 128),
            beta,
            decay,
            up_index,
            down_index,
            residual,
            out_gain.reshape(1, 128),
            ffn_gain.reshape(nten, 1, 256),
            up_blocks,
            down_kept_tiles,
        )

    placed = (
        P("seq", "tensor", None),
        P(None, "seq", "tensor", None),
        P(None, "seq", "tensor", None),
        P(None, "tensor", "seq"),
        P("tensor", "seq"),
        P(),
        P("seq", "tensor"),
        P(),
        P("tensor", None, None, None),
        P("tensor", None),
        P("tensor", None, None, None),
        P("tensor", None),
    )
    return jax.shard_map(
        per_device, mesh=mesh, in_specs=placed, out_specs=P("seq", "tensor"), check_vma=False
    )
```

```python
import functools

import jax
import jax.numpy as jnp
from jax import lax
from jax.experimental import pallas as pl
from jax.experimental.pallas import tpu as pltpu
from jax.sharding import PartitionSpec as P

F32 = jnp.float32
BF16 = jnp.bfloat16
HIGHEST = lax.Precision.HIGHEST
LANES_X = 4
VMEM_LIMIT = 24 << 20
MESH = pl.DeviceIdType.MESH


def dot(a, b, contract=(1, 0), precision=None):
    return lax.dot_general(
        a,
        b,
        (((contract[0],), (contract[1],)), ((), ())),
        precision=precision,
        preferred_element_type=F32,
    )


def split(a):
    high = a.astype(BF16)
    return high, (a - high.astype(F32)).astype(BF16)


def mm3(a, b):
    ah, al = split(a)
    bh, bl = split(b)
    left = jnp.concatenate([ah, al], 1)
    right = jnp.concatenate(
        [jnp.concatenate([bh, bl], 1), jnp.concatenate([bh, jnp.zeros_like(bl)], 1)], 0
    )
    both = dot(left, right)
    n = b.shape[1]
    return both[:, :n] + both[:, n:]


def iota(shape, axis):
    return lax.broadcasted_iota(jnp.int32, shape, axis)


def unit_lower_inverse(lowers):
    n = lowers[0].shape[0]
    rows, cols = iota((n, n), 0), iota((n, n), 1)
    eye = (rows == cols).astype(F32)
    base = (rows >> 3) == (cols >> 3)
    n1 = [jnp.where(base, -low, 0.0) for low in lowers]
    n2 = [mm3(a, a) for a in n1]
    n3 = [mm3(a, b) for a, b in zip(n1, n2)]
    n4 = [mm3(a, a) for a in n2]
    y = [eye + a + b + c for a, b, c in zip(n1, n2, n3)]
    x = [a + mm3(a, b) for a, b in zip(y, n4)]
    shift = 3
    while (1 << shift) < n:
        pick = ((rows >> (shift + 1)) == (cols >> (shift + 1))) & ((rows >> shift) != (cols >> shift))
        links = [jnp.where(pick, low, 0.0) for low in lowers]
        right = [mm3(c, a) for c, a in zip(links, x)]
        x = [a - mm3(a, b) for a, b in zip(x, right)]
        shift += 1
    return x


def inverse_table(index, kept):
    lanes = iota((index.shape[0], 128), 1)
    found = jnp.full(lanes.shape, kept, jnp.int32)
    for j in range(kept):
        found = jnp.where(index[:, j : j + 1] == lanes, j, found)
    return found


def local_terms(q_ref, k_ref, v_ref, beta_ref, decay_ref, tw_ref, qt_ref, lo_ref):
    tok = q_ref.shape[0] // 2
    span = 2 * tok
    heads = 2
    half = span // 2

    kv = jnp.concatenate([k_ref[...], v_ref[...]], 1)
    q_all = q_ref[...]
    small = jnp.concatenate(
        [decay_ref[...], beta_ref[0], beta_ref[1], jnp.zeros((2, tok), F32)], 0
    )
    m_at, t_at = iota((span, tok), 0), iota((span, tok), 1)
    upto = (t_at <= (m_at >> 1)).astype(F32)
    first = ((t_at == (m_at >> 1)) & ((m_at & 1) == 0)).astype(F32)
    second = ((t_at == (m_at >> 1)) & ((m_at & 1) == 1)).astype(F32)
    upto_tok = (iota((tok, tok), 1) <= iota((tok, tok), 0)).astype(F32)
    run_col = dot(upto, small, (1, 1), HIGHEST)
    run_row = dot(small, upto, (1, 1), HIGHEST)
    tok_col = dot(upto_tok, small, (1, 1), HIGHEST)
    one_col, two_col = dot(first, small, (1, 1), HIGHEST), dot(second, small, (1, 1), HIGHEST)
    one_row, two_row = dot(small, first, (1, 1), HIGHEST), dot(small, second, (1, 1), HIGHEST)

    rows, cols = iota((span, span), 0), iota((span, span), 1)
    below = cols < rows
    same = rows == cols
    reach = iota((tok, span), 1) <= 2 * iota((tok, span), 0) + 1
    eye = (iota((tok, tok), 0) == iota((tok, tok), 1)).astype(F32)
    row_of = iota((span, 4 * tok), 0)
    place = (row_of & 1) * span + (row_of >> 1) * 2
    column = iota((span, 4 * tok), 1)
    q_place = iota((tok, span), 0) * 2
    q_column = iota((tok, span), 1)

    ks, vs, qs, gammas, lowers, keep = [], [], [], [], [], []
    for h in range(heads):
        pick = (column == place + h).astype(BF16)
        both = dot(pick, kv).astype(BF16)
        k, v = both[:, :128], both[:, 128:]
        q = dot((q_column == q_place + h).astype(BF16), q_all)
        gram = dot(k, k, (1, 1))
        diag = jnp.where(same, gram, 0.0)
        rk_col = lax.rsqrt(jnp.sum(diag, 1, keepdims=True) + 1e-06)
        rk_row = lax.rsqrt(jnp.sum(diag, 0, keepdims=True) + 1e-06)
        run_c, run_r = run_col[:, h : h + 1], run_row[h : h + 1, :]
        beta_c = one_col[:, 2 + h : 3 + h] + two_col[:, 4 + h : 5 + h]
        beta_r = one_row[2 + h : 3 + h, :] + two_row[4 + h : 5 + h, :]
        fade = jnp.exp(jnp.where(below, run_c - run_r, 0.0))
        low = jnp.where(below, (beta_c * rk_col) * fade * gram * rk_row, 0.0)
        keep.append((k, v, q, rk_col, rk_row, run_c, run_r, beta_r, low))
        lowers += [low[:half, :half], low[half:, half:]]

    inverses = unit_lower_inverse(lowers)
    mids = [mm3(keep[h][8][half:, :half], inverses[2 * h]) for h in range(heads)]
    crosses = [mm3(inverses[2 * h + 1], mids[h]) for h in range(heads)]
    for h in range(heads):
        k, v, q, rk_col, rk_row, run_c, run_r, beta_r, low = keep[h]
        a = jnp.concatenate(
            [
                jnp.concatenate([inverses[2 * h], jnp.zeros((half, half), F32)], 1),
                jnp.concatenate([-crosses[h], inverses[2 * h + 1]], 1),
            ],
            0,
        )
        a_val = a * beta_r
        a_key = a_val * (jnp.exp(run_r) * rk_row)
        ah, al = split(a_val)
        u = dot(ah, v) + dot(al, v)
        ah, al = split(a_key)
        w = dot(ah, k) + dot(al, k)
        last = run_c[span - 1 : span, :]
        remain = jnp.exp(last - run_c) * rk_col
        uh, ul = split(u * remain)
        write_t = dot(uh, k, (0, 0)) + dot(ul, k, (0, 0))
        wh, wl = split(w * remain)
        trans = jnp.exp(last) * eye - dot(k, wh, (0, 0)) - dot(k, wl, (0, 0))
        tw_ref[h, 0:64, :] = write_t[:64].astype(BF16)
        tw_ref[h, 64:192, :] = trans.astype(BF16)
        tw_ref[h, 192:256, :] = write_t[64:].astype(BF16)
        tok_run = tok_col[:, h : h + 1]
        rq = lax.rsqrt(jnp.sum(q * q, 1, keepdims=True) + 1e-06)
        qk = dot(q.astype(BF16), k, (1, 1))
        mixing = jnp.where(
            reach, jnp.exp(jnp.where(reach, tok_run - run_r, 0.0)) * qk * rq * rk_row, 0.0
        )
        mh, ml = split(mixing)
        bh, bl = split(jnp.concatenate([w, u], 1))
        mixed = dot(mh, bh) + dot(ml, bh) + dot(mh, bl)
        qt_ref[h] = (jnp.exp(tok_run) * rq) * q - mixed[:, :128]
        lo_ref[h] = mixed[:, 128:]


def chain_step(state, trans, write):
    n = state.shape[0]
    high, low = split(state)
    both = dot(jnp.concatenate([high, low], 0), trans, (1, 1))
    return both[:n] + both[n:] + write.astype(F32)


def main_kernel(
    nz,
    ny,
    q_in,
    k_in,
    v_in,
    beta_in,
    decay_in,
    up_in,
    down_in,
    res_in,
    og_in,
    fg_in,
    up_hbm,
    down_hbm,
    out_ref,
    q_ref,
    k_ref,
    v_ref,
    beta_ref,
    decay_ref,
    up_ref,
    down_ref,
    res_ref,
    og_ref,
    fg_ref,
    l_sem,
    qt_ref,
    lo_ref,
    table_v,
    inv_ref,
    up_v,
    down_v,
    rx,
    zmsg,
    rz,
    chain,
    pmsg,
    rp,
    xg,
    acc,
    act,
    pair_out,
    pair_in,
    psum,
    rs,
    wsem,
    a_send,
    a_recv,
    b_send,
    b_recv,
    c_send,
    c_recv,
    z_send,
    z_recv,
    p_send,
    p_recv,
    g_send,
    g_recv,
    f_send,
    f_recv,
    o_sem,
    s_send,
    s_recv,
    r_send,
    r_recv,
):
    seq, ten = lax.axis_index("seq"), lax.axis_index("tensor")
    z, x = seq // LANES_X, lax.rem(seq, LANES_X)
    y, core = ten // 2, lax.rem(ten, 2)
    partner = y * 2 + 1 - core
    head, part = x // 2, lax.rem(x, 2)
    groups = up_hbm.shape[0]
    kept = up_hbm.shape[1]

    def at_x(o):
        return lax.rem(x + o, LANES_X)

    def at_y(o):
        return lax.rem(y + o, ny)

    barrier = pltpu.get_barrier_semaphore()
    peers = [(z * LANES_X + at_x(o), ten) for o in range(1, LANES_X)]
    peers += [(lax.rem(z + o, nz) * LANES_X + x, ten) for o in range(1, nz)]
    peers += [(seq, at_y(o) * 2 + core) for o in (1, 2, ny - 2, ny - 1)]
    peers += [(seq, partner)]
    for peer in peers:
        pl.semaphore_signal(barrier, inc=1, device_id=peer, device_id_type=MESH)

    inputs = (
        (k_in, k_ref),
        (v_in, v_ref),
        (q_in, q_ref),
        (beta_in, beta_ref),
        (decay_in, decay_ref),
        (up_in, up_ref),
        (down_in, down_ref),
        (res_in, res_ref),
        (og_in, og_ref),
        (fg_in, fg_ref),
    )
    loads = [
        pltpu.make_async_copy(here, there, l_sem.at[n]) for n, (here, there) in enumerate(inputs)
    ]
    for load in loads:
        load.start()
    load_up = pltpu.make_async_copy(up_hbm, up_v.at[:, pl.ds(0, kept)], wsem.at[0])
    load_down = pltpu.make_async_copy(down_hbm, down_v.at[:, pl.ds(0, kept)], wsem.at[1])
    load_up.start()
    load_down.start()
    for c in range(groups):
        up_v[c, kept] = jnp.zeros(up_v.shape[2:], BF16)
        down_v[c, kept] = jnp.zeros(up_v.shape[2:], BF16)
    chain[...] = jnp.zeros_like(chain)
    for load in loads:
        load.wait()
    table_v[0:groups] = inverse_table(up_ref[...], kept)
    table_v[groups : 2 * groups] = inverse_table(down_ref[...], kept)
    load_table = pltpu.make_async_copy(table_v, inv_ref, wsem.at[2])
    load_table.start()
    local_terms(q_ref, k_ref, v_ref, beta_ref, decay_ref, rx.at[x], qt_ref, lo_ref)
    pl.semaphore_wait(barrier, len(peers))

    def remote(src, dst, send, recv, peer):
        return pltpu.make_async_remote_copy(
            src_ref=src,
            dst_ref=dst,
            send_sem=send,
            recv_sem=recv,
            device_id=peer,
            device_id_type=MESH,
        )

    def a_copy(o):
        there = at_x(o)
        h2, p2 = there // 2, lax.rem(there, 2)
        rows = pl.ds(pl.multiple_of(p2 * 64, 64), 192)
        return remote(
            rx.at[x, h2, rows],
            rx.at[x, h2, rows],
            a_send.at[o],
            a_recv.at[x],
            (z * LANES_X + there, ten),
        )

    def b_copies(o):
        there = at_x(o)
        h2, p2 = there // 2, lax.rem(there, 2)
        rows = pl.ds(pl.multiple_of((1 - p2) * 192, 64), 64)
        peer = (z * LANES_X + there, ten)
        return (
            remote(
                rx.at[x, h2, rows], rx.at[x, h2, rows], b_send.at[o], b_recv.at[x], peer
            ),
            remote(
                rx.at[x, 1 - h2], rx.at[x, 1 - h2], c_send.at[o], c_recv.at[x], peer
            ),
        )

    for o in (2, 1, 3):
        a_copy(o).start()
    my_rows = pl.ds(pl.multiple_of(part * 64, 64), 192)
    for o in (1, 3, 2):
        source = at_x(o)
        remote(
            rx.at[source, head, my_rows],
            rx.at[source, head, my_rows],
            a_send.at[o],
            a_recv.at[source],
            (seq, ten),
        ).wait_recv()

    w_rows = pl.ds(pl.multiple_of(part * 192, 64), 64)
    ts = [rx[i, head, pl.ds(64, 128)] for i in range(LANES_X)]
    ws = [rx[i, head, w_rows] for i in range(LANES_X)]
    t10, t32 = dot(ts[1], ts[0]), dot(ts[3], ts[2])
    w10 = dot(ws[0], ts[1], (1, 1)) + ws[1].astype(F32)
    w32 = dot(ws[2], ts[3], (1, 1)) + ws[3].astype(F32)
    zmsg[64:192] = mm3(t32, t10).astype(BF16)
    th, tl = split(t32)
    wh, wl = split(w10)
    mixed = dot(jnp.concatenate([wh, wl], 0), th, (1, 1))
    w_all = mixed[:64] + mixed[64:] + dot(wh, tl, (1, 1)) + w32
    zmsg[0:64] = w_all.astype(BF16)

    def z_copy(o):
        return remote(
            zmsg,
            rz.at[z],
            z_send.at[o],
            z_recv.at[z],
            ((z + o) * LANES_X + x, ten),
        )

    for o in range(1, nz):

        @pl.when(z + o < nz)
        def _():
            z_copy(o).start()

    for o in range(1, LANES_X):

        @pl.when(x + o < LANES_X)
        def _():
            for one in b_copies(o):
                one.start()

    for i in range(nz - 1):

        @pl.when(i < z)
        def _():
            remote(
                rz.at[i], rz.at[i], z_send.at[0], z_recv.at[i], (seq, ten)
            ).wait_recv()
            if i == 0:
                chain[...] = rz[0, 0:64].astype(F32)
            else:
                chain[...] = chain_step(chain[...], rz[i, 64:192], rz[i, 0:64])

    entering = chain[...].astype(BF16)
    pmsg[...] = entering
    p_rows = pl.ds(pl.multiple_of(part * 64, 64), 64)
    rp[head, p_rows] = entering

    def p_copy(o):
        return remote(
            pmsg,
            rp.at[head, p_rows],
            p_send.at[o],
            p_recv.at[x],
            (z * LANES_X + at_x(o), ten),
        )

    for o in (2, 1, 3):
        p_copy(o).start()
    for i in range(LANES_X - 1):

        @pl.when(i < x)
        def _():
            other = pl.ds(pl.multiple_of((1 - part) * 192, 64), 64)
            remote(
                rx.at[i, head, other],
                rx.at[i, head, other],
                b_send.at[0],
                b_recv.at[i],
                (seq, ten),
            ).wait_recv()
            remote(
                rx.at[i, 1 - head], rx.at[i, 1 - head], c_send.at[0], c_recv.at[i], (seq, ten)
            ).wait_recv()

    for o in (1, 3, 2):
        source = at_x(o)
        rows = pl.ds(pl.multiple_of(lax.rem(source, 2) * 64, 64), 64)
        remote(
            rp.at[source // 2, rows],
            rp.at[source // 2, rows],
            p_send.at[o],
            p_recv.at[source],
            (seq, ten),
        ).wait_recv()

    state = [rp[h].astype(F32) for h in range(2)]
    for i in range(LANES_X - 1):
        for h in range(2):
            write = jnp.concatenate([rx[i, h, 0:64], rx[i, h, 192:256]], 0)
            moved = chain_step(state[h], rx[i, h, 64:192], write)
            state[h] = jnp.where(i < x, moved, state[h])

    gain = og_ref[...]
    pieces = []
    for h in range(2):
        qh, ql = split(qt_ref[h])
        sh, sl = split(state[h])
        head_out = dot(qh, sh, (1, 1)) + dot(ql, sh, (1, 1)) + dot(qh, sl, (1, 1)) + lo_ref[h]
        power = jnp.mean(head_out * head_out, -1, keepdims=True)
        normed = head_out * lax.rsqrt(power + 1e-05) * gain
        pieces.append(res_ref[:, 128 * h : 128 * h + 128].astype(F32) + normed)
    xg[ten] = jnp.concatenate(pieces, 1).astype(BF16)

    reach = ny // 2
    ways = (1, -1)
    halves = [pl.ds(0, xg.shape[1] // 2), pl.ds(xg.shape[1] // 2, xg.shape[1] // 2)]

    def sent(i, d, part_at):
        return d < reach or part_at == i

    messages = [
        (i, d, p)
        for d in range(1, reach + 1)
        for p in range(2)
        for i in range(2)
        if sent(i, d, p)
    ]

    hop = (0, 1, 2, 1, 2)

    def across(i, d):
        return (seq, at_y(ny + ways[i] * hop[d]) * 2 + core)

    def ring(i, d, p):
        origin = 0 if d <= 2 else 2
        block = xg.at[at_y(ny - ways[i] * origin) * 2 + core, halves[p]]
        return remote(block, block, g_send.at[i, d, p], g_recv.at[i, d, p], across(i, d))

    def got(i, d, p):
        block = xg.at[at_y(ny - ways[i] * d) * 2 + core, halves[p]]
        remote(block, block, g_send.at[i, d, p], g_recv.at[i, d, p], (seq, ten)).wait_recv()

    def pass_on(i, d, p):
        block = xg.at[at_y(ny - ways[i] * d) * 2 + core, halves[p]]
        return remote(block, block, f_send.at[i, d, p], f_recv.at[i, d, p], (seq, partner))

    def passed(i, d, p):
        block = xg.at[at_y(ny - ways[i] * d) * 2 + 1 - core, halves[p]]
        remote(block, block, f_send.at[i, d, p], f_recv.at[i, d, p], (seq, ten)).wait_recv()

    def own_copy():
        return remote(xg.at[ten], xg.at[ten], o_sem.at[0], o_sem.at[1], (seq, partner))

    for level in (2, 1):
        for i, d, p in messages:
            if d == level:
                ring(i, d, p).start()
    own_copy().start()

    load_up.wait()
    load_down.wait()
    load_table.wait()

    def absorb(slot, first, power):
        wide = xg[slot].astype(F32)
        power = power + jnp.sum(wide * wide, -1, keepdims=True)
        scaled = (wide * fg_ref[slot]).astype(BF16)
        weights = jnp.concatenate(
            [
                jnp.concatenate(
                    [up_v[c, inv_ref[c, 2 * slot + b]] for c in range(groups)], 1
                )
                for b in range(2)
            ],
            0,
        )
        term = dot(scaled, weights)
        if first:
            acc[...] = term
        else:
            acc[...] += term
        return power

    def blocks(d):
        return [at_y(d)] if d == reach else [at_y(ny - d), at_y(d)]

    power = absorb(ten, True, jnp.zeros((xg.shape[1], 1), F32))
    remote(xg.at[partner], xg.at[partner], o_sem.at[0], o_sem.at[1], (seq, ten)).wait_recv()
    power = absorb(partner, False, power)

    def take(d):
        for i, e, p in messages:
            if e == d:
                got(i, d, p)
                if d == 2:
                    for later in (4, 3):
                        if sent(i, later, p):
                            ring(i, later, p).start()
                pass_on(i, d, p).start()

    def near(d, power):
        for where in blocks(d):
            power = absorb(where * 2 + core, False, power)
        return power

    def far_side(d, power):
        for i, e, p in messages:
            if e == d:
                passed(i, e, p)
        for where in blocks(d):
            power = absorb(where * 2 + 1 - core, False, power)
        return power

    take(2)
    power = near(2, power)
    take(1)
    power = near(1, power)
    power = far_side(2, power)
    power = far_side(1, power)
    take(3)
    power = near(3, power)
    take(4)
    power = near(4, power)
    power = far_side(3, power)
    power = far_side(4, power)

    width = 256 * xg.shape[0]
    scale = lax.rsqrt(power / width + 1e-05)
    act[...] = jax.nn.gelu(acc[...] * scale).astype(BF16)

    def share(slot):
        weights = jnp.concatenate(
            [
                jnp.concatenate(
                    [down_v[c, inv_ref[groups + c, 2 * slot + b]] for b in range(2)], 1
                )
                for c in range(groups)
            ],
            0,
        )
        return dot(act[...], weights).astype(BF16)

    def s_copy(off):
        k = off + reach - 1
        return remote(
            pair_out.at[k], pair_in.at[k], s_send.at[k], s_recv.at[k], (seq, partner)
        )

    def offer(off):
        pair_out[off + reach - 1] = share(at_y(ny + off) * 2 + 1 - core)
        s_copy(off).start()

    def pair_sum(off):
        mine = share(at_y(ny + off) * 2 + core).astype(F32)
        s_copy(off).wait_recv()
        return mine + pair_in[off + reach - 1].astype(F32)

    def m_copy(i, d, p):
        return remote(
            psum.at[i, d, halves[p]],
            rs.at[i, d, halves[p]],
            r_send.at[i, d, p],
            r_recv.at[i, d, p],
            across(i, d),
        )

    def m_got(i, d, p):
        block = rs.at[i, d, halves[p]]
        remote(block, block, r_send.at[i, d, p], r_recv.at[i, d, p], (seq, ten)).wait_recv()
        return rs[i, d, halves[p]].astype(F32)

    rows_dev = xg.shape[1] // 2

    def rows_of(value, p):
        return value[p * rows_dev : (p + 1) * rows_dev]

    def ship(i, d, p, value):
        psum[i, d, halves[p]] = value.astype(BF16)
        m_copy(i, d, p).start()

    def ship_both(d):
        for i in range(2):
            value = pair_sum(ways[i] * d)
            for p in range(2):
                ship(i, d, p, rows_of(value, p))

    for off in (4, 3, -3):
        offer(off)
    far = pair_sum(4)
    for i in range(2):
        ship(i, 4, i, rows_of(far, i))
    for off in (2, -2):
        offer(off)
    ship_both(3)
    for off in (1, -1, 0):
        offer(off)
    ship_both(1)
    sums = [pair_sum(2), pair_sum(-2)]
    total = pair_sum(0) + xg[ten].astype(F32)
    for p in range(2):
        for i in range(2):
            value = rows_of(sums[i], p) + m_got(i, 3, p)
            if sent(i, 4, p):
                value = value + m_got(i, 4, p)
            ship(i, 2, p, value)
    for p in range(2):
        value = rows_of(total, p)
        for d in (1, 2):
            for i in range(2):
                value = value + m_got(i, d, p)
        out_ref[halves[p], :] = value.astype(BF16)

    for o in range(1, LANES_X):
        a_copy(o).wait_send()
        p_copy(o).wait_send()

        @pl.when(x + o < LANES_X)
        def _():
            for one in b_copies(o):
                one.wait_send()

    for o in range(1, nz):

        @pl.when(z + o < nz)
        def _():
            z_copy(o).wait_send()

    own_copy().wait_send()
    for off in range(1 - reach, reach + 1):
        s_copy(off).wait_send()
    for i, d, p in messages:
        ring(i, d, p).wait_send()
        pass_on(i, d, p).wait_send()
        m_copy(i, d, p).wait_send()


def solution(mesh):
    nseq, nten = mesh.shape["seq"], mesh.shape["tensor"]
    nz, ny = nseq // LANES_X, nten // 2
    vmem = pl.BlockSpec(memory_space=pltpu.VMEM)
    hbm = pl.BlockSpec(memory_space=pltpu.HBM)
    dma = pltpu.SemaphoreType.DMA

    def per_device(
        queries,
        keys,
        values,
        beta,
        decay,
        out_gain,
        residual,
        ffn_gain,
        up_blocks,
        up_index,
        down_kept_tiles,
        down_index,
    ):
        tok = queries.shape[0]
        groups, kept = up_index.shape
        return pl.pallas_call(
            functools.partial(main_kernel, nz, ny),
            out_shape=jax.ShapeDtypeStruct((tok, 256), BF16),
            in_specs=[hbm] * 12,
            out_specs=vmem,
            scratch_shapes=[
                pltpu.VMEM((2 * tok, 128), BF16),
                pltpu.VMEM((4 * tok, 128), BF16),
                pltpu.VMEM((4 * tok, 128), BF16),
                pltpu.VMEM((2, 2, tok), F32),
                pltpu.VMEM((2, tok), F32),
                pltpu.VMEM((groups, kept), jnp.int32),
                pltpu.VMEM((groups, kept), jnp.int32),
                pltpu.VMEM((tok, 256), BF16),
                pltpu.VMEM((1, 128), F32),
                pltpu.VMEM((nten, 1, 256), F32),
                dma((10,)),
                pltpu.VMEM((2, tok, 128), F32),
                pltpu.VMEM((2, tok, 128), F32),
                pltpu.VMEM((2 * groups, 128), jnp.int32),
                pltpu.SMEM((2 * groups, 128), jnp.int32),
                pltpu.VMEM((groups, kept + 1, 128, 128), BF16),
                pltpu.VMEM((groups, kept + 1, 128, 128), BF16),
                pltpu.VMEM((LANES_X, 2, 256, 128), BF16),
                pltpu.VMEM((192, 128), BF16),
                pltpu.VMEM((nz, 192, 128), BF16),
                pltpu.VMEM((64, 128), F32),
                pltpu.VMEM((64, 128), BF16),
                pltpu.VMEM((2, 128, 128), BF16),
                pltpu.VMEM((nten, tok, 256), BF16),
                pltpu.VMEM((tok, groups * 128), F32),
                pltpu.VMEM((tok, groups * 128), BF16),
                pltpu.VMEM((ny, tok, 256), BF16),
                pltpu.VMEM((ny, tok, 256), BF16),
                pltpu.VMEM((2, ny // 2 + 1, tok, 256), BF16),
                pltpu.VMEM((2, ny // 2 + 1, tok, 256), BF16),
                dma((3,)),
                dma((LANES_X,)),
                dma((LANES_X,)),
                dma((LANES_X,)),
                dma((LANES_X,)),
                dma((LANES_X,)),
                dma((LANES_X,)),
                dma((nz,)),
                dma((nz,)),
                dma((LANES_X,)),
                dma((LANES_X,)),
                dma((2, ny // 2 + 1, 2)),
                dma((2, ny // 2 + 1, 2)),
                dma((2, ny // 2 + 1, 2)),
                dma((2, ny // 2 + 1, 2)),
                dma((2,)),
                dma((ny,)),
                dma((ny,)),
                dma((2, ny // 2 + 1, 2)),
                dma((2, ny // 2 + 1, 2)),
            ],
            compiler_params=pltpu.CompilerParams(
                collective_id=0, has_side_effects=True, vmem_limit_bytes=VMEM_LIMIT
            ),
            name="layer",
        )(*(pltpu.with_memory_space_constraint(a, pltpu.HBM) for a in (
            queries.reshape(2 * tok, 128),
            keys.reshape(4 * tok, 128),
            values.reshape(4 * tok, 128),
            beta,
            decay,
            up_index,
            down_index,
            residual,
            out_gain.reshape(1, 128),
            ffn_gain.reshape(nten, 1, 256),
            up_blocks,
            down_kept_tiles,
        )))

    placed = (
        P("seq", "tensor", None),
        P(None, "seq", "tensor", None),
        P(None, "seq", "tensor", None),
        P(None, "tensor", "seq"),
        P("tensor", "seq"),
        P(),
        P("seq", "tensor"),
        P(),
        P("tensor", None, None, None),
        P("tensor", None),
        P("tensor", None, None, None),
        P("tensor", None),
    )
    return jax.shard_map(
        per_device, mesh=mesh, in_specs=placed, out_specs=P("seq", "tensor"), check_vma=False
    )
```

```python
import functools

import jax
import jax.numpy as jnp
from jax import lax
from jax.experimental import pallas as pl
from jax.experimental.pallas import tpu as pltpu
from jax.sharding import PartitionSpec as P

F32 = jnp.float32
BF16 = jnp.bfloat16
HIGHEST = lax.Precision.HIGHEST
LANES_X = 4
VMEM_LIMIT = 24 << 20
MESH = pl.DeviceIdType.MESH


def dot(a, b, contract=(1, 0), precision=None):
    return lax.dot_general(
        a,
        b,
        (((contract[0],), (contract[1],)), ((), ())),
        precision=precision,
        preferred_element_type=F32,
    )


def split(a):
    high = a.astype(BF16)
    return high, (a - high.astype(F32)).astype(BF16)


def mm3(a, b):
    ah, al = split(a)
    bh, bl = split(b)
    left = jnp.concatenate([ah, al], 1)
    right = jnp.concatenate(
        [jnp.concatenate([bh, bl], 1), jnp.concatenate([bh, jnp.zeros_like(bl)], 1)], 0
    )
    both = dot(left, right)
    n = b.shape[1]
    return both[:, :n] + both[:, n:]


def iota(shape, axis):
    return lax.broadcasted_iota(jnp.int32, shape, axis)


def unit_lower_inverse(lowers):
    n = lowers[0].shape[0]
    rows, cols = iota((n, n), 0), iota((n, n), 1)
    eye = (rows == cols).astype(F32)
    base = (rows >> 3) == (cols >> 3)
    n1 = [jnp.where(base, -low, 0.0) for low in lowers]
    n2 = [mm3(a, a) for a in n1]
    n3 = [mm3(a, b) for a, b in zip(n1, n2)]
    n4 = [mm3(a, a) for a in n2]
    y = [eye + a + b + c for a, b, c in zip(n1, n2, n3)]
    x = [a + mm3(a, b) for a, b in zip(y, n4)]
    shift = 3
    while (1 << shift) < n:
        pick = ((rows >> (shift + 1)) == (cols >> (shift + 1))) & ((rows >> shift) != (cols >> shift))
        links = [jnp.where(pick, low, 0.0) for low in lowers]
        right = [mm3(c, a) for c, a in zip(links, x)]
        x = [a - mm3(a, b) for a, b in zip(x, right)]
        shift += 1
    return x


def inverse_table(index, kept):
    lanes = iota((index.shape[0], 128), 1)
    found = jnp.full(lanes.shape, kept, jnp.int32)
    for j in range(kept):
        found = jnp.where(index[:, j : j + 1] == lanes, j, found)
    return found


def local_terms(q_ref, k_ref, v_ref, beta_ref, decay_ref, tw_ref, qt_ref, lo_ref):
    tok = q_ref.shape[0] // 2
    span = 2 * tok
    heads = 2
    half = span // 2

    kv = jnp.concatenate([k_ref[...], v_ref[...]], 1)
    small = jnp.concatenate(
        [decay_ref[...], beta_ref[0], beta_ref[1], jnp.zeros((2, tok), F32)], 0
    )
    s1 = small.astype(BF16)
    rest = small - s1.astype(F32)
    s2 = rest.astype(BF16)
    s3 = (rest - s2.astype(F32)).astype(BF16)
    parts = jnp.concatenate([s1, s2, s3, jnp.zeros_like(s1)], 0)
    m_at, t_at = iota((span, tok), 0), iota((span, tok), 1)
    upto = t_at <= (m_at >> 1)
    first = (t_at == (m_at >> 1)) & ((m_at & 1) == 0)
    second = (t_at == (m_at >> 1)) & ((m_at & 1) == 1)
    upto_tok = iota((tok, tok), 1) <= iota((tok, tok), 0)
    picks = jnp.concatenate([e.astype(BF16) for e in (upto, first, second, upto_tok)], 0)
    cols3 = dot(picks, parts, (1, 1))
    col = cols3[:, 0:8] + cols3[:, 8:16] + cols3[:, 16:24]
    rows3 = dot(parts, picks, (1, 1))
    row = rows3[0:8] + rows3[8:16] + rows3[16:24]
    run_col, one_col, two_col = col[:span], col[span : 2 * span], col[2 * span : 3 * span]
    tok_col = col[3 * span :]
    run_row, one_row, two_row = row[:, :span], row[:, span : 2 * span], row[:, 2 * span : 3 * span]

    rows, cols = iota((span, span), 0), iota((span, span), 1)
    below = cols < rows
    same = rows == cols
    reach = iota((tok, span), 1) <= 2 * iota((tok, span), 0) + 1
    eye = (iota((tok, tok), 0) == iota((tok, tok), 1)).astype(F32)
    row_of = iota((span, 4 * tok), 0)
    place = (row_of & 1) * span + (row_of >> 1) * 2
    column = iota((span, 4 * tok), 1)
    q_place = iota((tok, span), 0) * 2
    q_column = iota((tok, span), 1)

    ks, vs, qs, gammas, lowers, keep = [], [], [], [], [], []
    for h in range(heads):
        pick = (column == place + h).astype(BF16)
        both = dot(pick, kv).astype(BF16)
        k, v = both[:, :128], both[:, 128:]
        gram = dot(k, k, (1, 1))
        diag = jnp.where(same, gram, 0.0)
        rk_col = lax.rsqrt(jnp.sum(diag, 1, keepdims=True) + 1e-06)
        rk_row = lax.rsqrt(jnp.sum(diag, 0, keepdims=True) + 1e-06)
        run_c, run_r = run_col[:, h : h + 1], run_row[h : h + 1, :]
        beta_c = one_col[:, 2 + h : 3 + h] + two_col[:, 4 + h : 5 + h]
        beta_r = one_row[2 + h : 3 + h, :] + two_row[4 + h : 5 + h, :]
        fade = jnp.exp(jnp.where(below, run_c - run_r, 0.0))
        low = jnp.where(below, (beta_c * rk_col) * fade * gram * rk_row, 0.0)
        keep.append((k, v, rk_col, rk_row, run_c, run_r, beta_r, low))
        lowers += [low[:half, :half], low[half:, half:]]

    inverses = unit_lower_inverse(lowers)
    mids = [mm3(keep[h][7][half:, :half], inverses[2 * h]) for h in range(heads)]
    crosses = [mm3(inverses[2 * h + 1], mids[h]) for h in range(heads)]
    left = []
    for h in range(heads):
        k, v, rk_col, rk_row, run_c, run_r, beta_r, low = keep[h]
        a = jnp.concatenate(
            [
                jnp.concatenate([inverses[2 * h], jnp.zeros((half, half), F32)], 1),
                jnp.concatenate([-crosses[h], inverses[2 * h + 1]], 1),
            ],
            0,
        )
        a_val = a * beta_r
        a_key = a_val * (jnp.exp(run_r) * rk_row)
        ah, al = split(a_val)
        u = dot(ah, v) + dot(al, v)
        ah, al = split(a_key)
        w = dot(ah, k) + dot(al, k)
        last = run_c[span - 1 : span, :]
        remain = jnp.exp(last - run_c) * rk_col
        uh, ul = split(u * remain)
        write_t = dot(uh, k, (0, 0)) + dot(ul, k, (0, 0))
        wh, wl = split(w * remain)
        trans = jnp.exp(last) * eye - dot(k, wh, (0, 0)) - dot(k, wl, (0, 0))
        tw_ref[h, 0:64, :] = write_t[:64].astype(BF16)
        tw_ref[h, 64:192, :] = trans.astype(BF16)
        tw_ref[h, 192:256, :] = write_t[64:].astype(BF16)
        left.append((k, u, w, rk_row, run_r, tok_col[:, h : h + 1]))

    def queries():
        q_all = q_ref[...]
        for h in range(heads):
            k, u, w, rk_row, run_r, tok_run = left[h]
            q = dot((q_column == q_place + h).astype(BF16), q_all)
            rq = lax.rsqrt(jnp.sum(q * q, 1, keepdims=True) + 1e-06)
            qk = dot(q.astype(BF16), k, (1, 1))
            mixing = jnp.where(
                reach, jnp.exp(jnp.where(reach, tok_run - run_r, 0.0)) * qk * rq * rk_row, 0.0
            )
            mh, ml = split(mixing)
            bh, bl = split(jnp.concatenate([w, u], 1))
            mixed = dot(mh, bh) + dot(ml, bh) + dot(mh, bl)
            qt_ref[h] = (jnp.exp(tok_run) * rq) * q - mixed[:, :128]
            lo_ref[h] = mixed[:, 128:]

    return queries


def chain_step(state, trans, write):
    n = state.shape[0]
    high, low = split(state)
    both = dot(jnp.concatenate([high, low], 0), trans, (1, 1))
    return both[:n] + both[n:] + write.astype(F32)


def main_kernel(
    nz,
    ny,
    q_in,
    k_in,
    v_in,
    beta_in,
    decay_in,
    up_in,
    down_in,
    res_in,
    og_in,
    fg_in,
    up_hbm,
    down_hbm,
    out_ref,
    q_ref,
    k_ref,
    v_ref,
    beta_ref,
    decay_ref,
    up_ref,
    down_ref,
    res_ref,
    og_ref,
    fg_ref,
    l_sem,
    qt_ref,
    lo_ref,
    table_v,
    inv_ref,
    up_v,
    down_v,
    rx,
    zmsg,
    rz,
    chain,
    since,
    before_t,
    before_w,
    pmsg,
    rp,
    xg,
    acc,
    act,
    pair_out,
    pair_in,
    psum,
    rs,
    wsem,
    a_send,
    a_recv,
    b_send,
    b_recv,
    c_send,
    c_recv,
    z_send,
    z_recv,
    p_send,
    p_recv,
    g_send,
    g_recv,
    f_send,
    f_recv,
    o_sem,
    s_send,
    s_recv,
    r_send,
    r_recv,
):
    seq, ten = lax.axis_index("seq"), lax.axis_index("tensor")
    z, x = seq // LANES_X, lax.rem(seq, LANES_X)
    y, core = ten // 2, lax.rem(ten, 2)
    partner = y * 2 + 1 - core
    head, part = x // 2, lax.rem(x, 2)
    groups = up_hbm.shape[0]
    kept = up_hbm.shape[1]

    def at_x(o):
        return lax.rem(x + o, LANES_X)

    def at_y(o):
        return lax.rem(y + o, ny)

    barrier = pltpu.get_barrier_semaphore()
    peers = [(z * LANES_X + at_x(o), ten) for o in range(1, LANES_X)]
    peers += [(lax.rem(z + o, nz) * LANES_X + x, ten) for o in range(1, nz)]
    peers += [(seq, at_y(o) * 2 + core) for o in (1, 2, ny - 2, ny - 1)]
    peers += [(seq, partner)]
    for peer in peers:
        pl.semaphore_signal(barrier, inc=1, device_id=peer, device_id_type=MESH)

    inputs = (
        (k_in, k_ref),
        (v_in, v_ref),
        (q_in, q_ref),
        (beta_in, beta_ref),
        (decay_in, decay_ref),
        (up_in, up_ref),
        (down_in, down_ref),
        (res_in, res_ref),
        (og_in, og_ref),
        (fg_in, fg_ref),
    )
    loads = [
        pltpu.make_async_copy(here, there, l_sem.at[n]) for n, (here, there) in enumerate(inputs)
    ]
    for load in loads:
        load.start()
    load_up = pltpu.make_async_copy(up_hbm, up_v.at[:, pl.ds(0, kept)], wsem.at[0])
    load_down = pltpu.make_async_copy(down_hbm, down_v.at[:, pl.ds(0, kept)], wsem.at[1])
    load_up.start()
    load_down.start()
    for load in loads:
        load.wait()
    queries = local_terms(q_ref, k_ref, v_ref, beta_ref, decay_ref, rx.at[x], qt_ref, lo_ref)
    pl.semaphore_wait(barrier, len(peers))

    def remote(src, dst, send, recv, peer):
        return pltpu.make_async_remote_copy(
            src_ref=src,
            dst_ref=dst,
            send_sem=send,
            recv_sem=recv,
            device_id=peer,
            device_id_type=MESH,
        )

    w_rows = pl.ds(pl.multiple_of(part * 192, 64), 64)
    my_rows = pl.ds(pl.multiple_of(part * 64, 64), 192)

    def a_copy(o, only_write):
        there = at_x(o)
        h2, p2 = there // 2, lax.rem(there, 2)
        if only_write:
            rows = pl.ds(pl.multiple_of(p2 * 192, 64), 64)
        else:
            rows = pl.ds(pl.multiple_of(p2 * 64, 64), 192)
        return remote(
            rx.at[x, h2, rows],
            rx.at[x, h2, rows],
            a_send.at[o],
            a_recv.at[x],
            (z * LANES_X + there, ten),
        )

    def on_first(act_on):
        @pl.when(seq == 0)
        def _():
            act_on(True)

        @pl.when(seq != 0)
        def _():
            act_on(False)

    def a_wait(i):
        def wait(only_write):
            block = rx.at[i, head, w_rows if only_write else my_rows]
            remote(block, block, a_send.at[0], a_recv.at[i], (seq, ten)).wait_recv()

        @pl.when(i != x)
        def _():
            if i == 0:

                @pl.when(z == 0)
                def _():
                    wait(True)
                    rx[0, head, 64:192] = jnp.zeros((128, 128), BF16)

                @pl.when(z != 0)
                def _():
                    wait(False)
            else:
                wait(False)

    def b_copies(o):
        there = at_x(o)
        h2, p2 = there // 2, lax.rem(there, 2)
        rows = pl.ds(pl.multiple_of((1 - p2) * 192, 64), 64)
        peer = (z * LANES_X + there, ten)
        return (
            remote(
                rx.at[x, h2, rows], rx.at[x, h2, rows], b_send.at[o], b_recv.at[x], peer
            ),
            remote(
                rx.at[x, 1 - h2], rx.at[x, 1 - h2], c_send.at[o], c_recv.at[x], peer
            ),
        )

    for o in (2, 1, 3):
        on_first(lambda only_write: a_copy(o, only_write).start())

    chain[...] = jnp.zeros_like(chain)
    eye = (iota((128, 128), 0) == iota((128, 128), 1)).astype(F32)
    since[...] = eye
    for h in range(2):
        before_t[h] = eye
        before_w[h] = jnp.zeros((128, 128), F32)
    table_v[0:groups] = inverse_table(up_ref[...], kept)
    table_v[groups : 2 * groups] = inverse_table(down_ref[...], kept)
    load_table = pltpu.make_async_copy(table_v, inv_ref, wsem.at[2])
    load_table.start()
    for c in range(groups):
        up_v[c, kept] = jnp.zeros(up_v.shape[2:], BF16)
        down_v[c, kept] = jnp.zeros(up_v.shape[2:], BF16)
    queries()

    def apply(write, trans):
        high, low = split(trans)
        return dot(write, high, (1, 1)) + dot(write, low, (1, 1))

    def extend(trans, earlier):
        high, low = split(trans)
        both = dot(jnp.concatenate([high, low], 0), earlier)
        return both[:128] + both[128:]

    for i in (3, 2, 1):
        a_wait(i)
    ts = [rx[i, head, pl.ds(64, 128)] for i in range(1, LANES_X)]
    ws = [rx[i, head, w_rows] for i in range(1, LANES_X)]
    t32 = dot(ts[2], ts[1])
    w32 = dot(ws[1], ts[2], (1, 1)) + ws[2].astype(F32)
    t321 = extend(t32, ts[0])
    w321 = apply(ws[0], t32) + w32
    a_wait(0)
    zmsg[0:64] = (apply(rx[0, head, w_rows], t321) + w321).astype(BF16)
    zmsg[64:192] = extend(t321, rx[0, head, pl.ds(64, 128)]).astype(BF16)

    def z_copy(o, only_write):
        rows = pl.ds(0, 64 if only_write else 192)
        return remote(
            zmsg.at[rows],
            rz.at[z, rows],
            z_send.at[o],
            z_recv.at[z],
            ((z + o) * LANES_X + x, ten),
        )

    def on_first_group(act_on):
        @pl.when(z == 0)
        def _():
            act_on(True)

        @pl.when(z != 0)
        def _():
            act_on(False)

    for o in range(1, nz):

        @pl.when(z + o < nz)
        def _():
            on_first_group(lambda only_write: z_copy(o, only_write).start())

    for o in range(1, LANES_X):

        @pl.when(x + o < LANES_X)
        def _():
            for one in b_copies(o):
                one.start()

    for i in range(LANES_X - 1):

        @pl.when(i < x)
        def _():
            other = pl.ds(pl.multiple_of((1 - part) * 192, 64), 64)
            remote(
                rx.at[i, head, other],
                rx.at[i, head, other],
                b_send.at[0],
                b_recv.at[i],
                (seq, ten),
            ).wait_recv()
            remote(
                rx.at[i, 1 - head], rx.at[i, 1 - head], c_send.at[0], c_recv.at[i], (seq, ten)
            ).wait_recv()
            for h in range(2):
                trans = rx[i, h, 64:192]
                write = jnp.concatenate([rx[i, h, 0:64], rx[i, h, 192:256]], 0)
                if i == 0:
                    before_t[h] = trans.astype(F32)
                    before_w[h] = write.astype(F32)
                else:
                    high, low = split(before_t[h])
                    both = dot(trans, jnp.concatenate([high, low], 1))
                    before_t[h] = both[:, :128] + both[:, 128:]
                    before_w[h] = chain_step(before_w[h], trans, write)

    def z_wait(i):
        block = rz.at[i, pl.ds(0, 64 if i == 0 else 192)]
        remote(block, block, z_send.at[0], z_recv.at[i], (seq, ten)).wait_recv()

    for i in range(nz - 2, 0, -1):

        @pl.when(i < z)
        def _():
            z_wait(i)
            chain[...] += apply(rz[i, 0:64], since[...])
            since[...] = extend(since[...], rz[i, 64:192])

    if nz > 1:

        @pl.when(z > 0)
        def _():
            z_wait(0)
            chain[...] += apply(rz[0, 0:64], since[...])

    entering = chain[...].astype(BF16)
    pmsg[...] = entering
    p_rows = pl.ds(pl.multiple_of(part * 64, 64), 64)
    rp[head, p_rows] = entering

    def p_copy(o):
        return remote(
            pmsg,
            rp.at[head, p_rows],
            p_send.at[o],
            p_recv.at[x],
            (z * LANES_X + at_x(o), ten),
        )

    for o in (2, 1, 3):
        p_copy(o).start()
    for o in (1, 3, 2):
        source = at_x(o)
        rows = pl.ds(pl.multiple_of(lax.rem(source, 2) * 64, 64), 64)
        remote(
            rp.at[source // 2, rows],
            rp.at[source // 2, rows],
            p_send.at[o],
            p_recv.at[source],
            (seq, ten),
        ).wait_recv()

    state = [apply(rp[h], before_t[h]) + before_w[h] for h in range(2)]
    gain = og_ref[...]
    pieces = []
    for h in range(2):
        qh, ql = split(qt_ref[h])
        sh, sl = split(state[h])
        head_out = dot(qh, sh, (1, 1)) + dot(ql, sh, (1, 1)) + dot(qh, sl, (1, 1)) + lo_ref[h]
        power = jnp.mean(head_out * head_out, -1, keepdims=True)
        normed = head_out * lax.rsqrt(power + 1e-05) * gain
        pieces.append(res_ref[:, 128 * h : 128 * h + 128].astype(F32) + normed)
    xg[ten] = jnp.concatenate(pieces, 1).astype(BF16)

    reach = ny // 2
    ways = (1, -1)
    halves = [pl.ds(0, xg.shape[1] // 2), pl.ds(xg.shape[1] // 2, xg.shape[1] // 2)]

    def sent(i, d, part_at):
        return d < reach or part_at == i

    messages = [
        (i, d, p)
        for d in range(1, reach + 1)
        for p in range(2)
        for i in range(2)
        if sent(i, d, p)
    ]

    hop = (0, 1, 2, 1, 2)

    def across(i, d):
        return (seq, at_y(ny + ways[i] * hop[d]) * 2 + core)

    def ring(i, d, p):
        origin = 0 if d <= 2 else 2
        block = xg.at[at_y(ny - ways[i] * origin) * 2 + core, halves[p]]
        return remote(block, block, g_send.at[i, d - 1, p], g_recv.at[i, d - 1, p], across(i, d))

    def got(i, d, p):
        block = xg.at[at_y(ny - ways[i] * d) * 2 + core, halves[p]]
        remote(block, block, g_send.at[i, d - 1, p], g_recv.at[i, d - 1, p], (seq, ten)).wait_recv()

    def pass_on(i, d, p):
        block = xg.at[at_y(ny - ways[i] * d) * 2 + core, halves[p]]
        return remote(block, block, f_send.at[i, d - 1, p], f_recv.at[i, d - 1, p], (seq, partner))

    def passed(i, d, p):
        block = xg.at[at_y(ny - ways[i] * d) * 2 + 1 - core, halves[p]]
        remote(block, block, f_send.at[i, d - 1, p], f_recv.at[i, d - 1, p], (seq, ten)).wait_recv()

    def own_copy():
        return remote(xg.at[ten], xg.at[ten], o_sem.at[0], o_sem.at[1], (seq, partner))

    for level in (2, 1):
        for i, d, p in messages:
            if d == level:
                ring(i, d, p).start()
    own_copy().start()

    load_up.wait()
    load_down.wait()
    load_table.wait()

    def absorb(slot, first, power):
        wide = xg[slot].astype(F32)
        power = power + jnp.sum(wide * wide, -1, keepdims=True)
        scaled = (wide * fg_ref[slot]).astype(BF16)
        weights = jnp.concatenate(
            [
                jnp.concatenate(
                    [up_v[c, inv_ref[c, 2 * slot + b]] for c in range(groups)], 1
                )
                for b in range(2)
            ],
            0,
        )
        term = dot(scaled, weights)
        if first:
            acc[...] = term
        else:
            acc[...] += term
        return power

    def blocks(d):
        return [at_y(d)] if d == reach else [at_y(ny - d), at_y(d)]

    power = absorb(ten, True, jnp.zeros((xg.shape[1], 1), F32))
    remote(xg.at[partner], xg.at[partner], o_sem.at[0], o_sem.at[1], (seq, ten)).wait_recv()
    power = absorb(partner, False, power)

    def take(d):
        for i, e, p in messages:
            if e == d:
                got(i, d, p)
                if d == 2:
                    for later in (4, 3):
                        if sent(i, later, p):
                            ring(i, later, p).start()
                pass_on(i, d, p).start()

    def near(d, power):
        for where in blocks(d):
            power = absorb(where * 2 + core, False, power)
        return power

    def far_side(d, power):
        for i, e, p in messages:
            if e == d:
                passed(i, e, p)
        for where in blocks(d):
            power = absorb(where * 2 + 1 - core, False, power)
        return power

    take(2)
    power = near(2, power)
    take(1)
    power = near(1, power)
    power = far_side(2, power)
    power = far_side(1, power)
    take(3)
    power = near(3, power)
    take(4)
    power = near(4, power)
    power = far_side(3, power)
    power = far_side(4, power)

    width = 256 * xg.shape[0]
    scale = lax.rsqrt(power / width + 1e-05)
    act[...] = jax.nn.gelu(acc[...] * scale).astype(BF16)

    def share(slot):
        weights = jnp.concatenate(
            [
                jnp.concatenate(
                    [down_v[c, inv_ref[groups + c, 2 * slot + b]] for b in range(2)], 1
                )
                for c in range(groups)
            ],
            0,
        )
        return dot(act[...], weights).astype(BF16)

    def s_copy(off):
        k = off + reach - 1
        return remote(
            pair_out.at[k], pair_in.at[k], s_send.at[k], s_recv.at[k], (seq, partner)
        )

    def offer(off):
        pair_out[off + reach - 1] = share(at_y(ny + off) * 2 + 1 - core)
        s_copy(off).start()

    def pair_sum(off):
        mine = share(at_y(ny + off) * 2 + core).astype(F32)
        s_copy(off).wait_recv()
        return mine + pair_in[off + reach - 1].astype(F32)

    def m_copy(i, d, p):
        return remote(
            psum.at[i, d, halves[p]],
            rs.at[i, d, halves[p]],
            r_send.at[i, d - 1, p],
            r_recv.at[i, d - 1, p],
            across(i, d),
        )

    def m_got(i, d, p):
        block = rs.at[i, d, halves[p]]
        remote(block, block, r_send.at[i, d - 1, p], r_recv.at[i, d - 1, p], (seq, ten)).wait_recv()
        return rs[i, d, halves[p]].astype(F32)

    rows_dev = xg.shape[1] // 2

    def rows_of(value, p):
        return value[p * rows_dev : (p + 1) * rows_dev]

    def ship(i, d, p, value):
        psum[i, d, halves[p]] = value.astype(BF16)
        m_copy(i, d, p).start()

    def ship_both(d):
        for i in range(2):
            value = pair_sum(ways[i] * d)
            for p in range(2):
                ship(i, d, p, rows_of(value, p))

    for off in (4, 3, -3):
        offer(off)
    far = pair_sum(4)
    for i in range(2):
        ship(i, 4, i, rows_of(far, i))
    for off in (2, -2):
        offer(off)
    ship_both(3)
    for off in (1, -1, 0):
        offer(off)
    ship_both(1)
    sums = [pair_sum(2), pair_sum(-2)]
    total = pair_sum(0) + xg[ten].astype(F32)
    for p in range(2):
        for i in range(2):
            value = rows_of(sums[i], p) + m_got(i, 3, p)
            if sent(i, 4, p):
                value = value + m_got(i, 4, p)
            ship(i, 2, p, value)
    for p in range(2):
        value = rows_of(total, p)
        for d in (1, 2):
            for i in range(2):
                value = value + m_got(i, d, p)
        out_ref[halves[p], :] = value.astype(BF16)

    for o in range(1, LANES_X):
        on_first(lambda only_write: a_copy(o, only_write).wait_send())
        p_copy(o).wait_send()

        @pl.when(x + o < LANES_X)
        def _():
            for one in b_copies(o):
                one.wait_send()

    for o in range(1, nz):

        @pl.when(z + o < nz)
        def _():
            on_first_group(lambda only_write: z_copy(o, only_write).wait_send())

    own_copy().wait_send()
    for off in range(1 - reach, reach + 1):
        s_copy(off).wait_send()
    for i, d, p in messages:
        ring(i, d, p).wait_send()
        pass_on(i, d, p).wait_send()
        m_copy(i, d, p).wait_send()


def solution(mesh):
    nseq, nten = mesh.shape["seq"], mesh.shape["tensor"]
    nz, ny = nseq // LANES_X, nten // 2
    vmem = pl.BlockSpec(memory_space=pltpu.VMEM)
    hbm = pl.BlockSpec(memory_space=pltpu.HBM)
    dma = pltpu.SemaphoreType.DMA

    def per_device(
        queries,
        keys,
        values,
        beta,
        decay,
        out_gain,
        residual,
        ffn_gain,
        up_blocks,
        up_index,
        down_kept_tiles,
        down_index,
    ):
        tok = queries.shape[0]
        groups, kept = up_index.shape
        return pl.pallas_call(
            functools.partial(main_kernel, nz, ny),
            out_shape=jax.ShapeDtypeStruct((tok, 256), BF16),
            in_specs=[hbm] * 12,
            out_specs=vmem,
            scratch_shapes=[
                pltpu.VMEM((2 * tok, 128), BF16),
                pltpu.VMEM((4 * tok, 128), BF16),
                pltpu.VMEM((4 * tok, 128), BF16),
                pltpu.VMEM((2, 2, tok), F32),
                pltpu.VMEM((2, tok), F32),
                pltpu.VMEM((groups, kept), jnp.int32),
                pltpu.VMEM((groups, kept), jnp.int32),
                pltpu.VMEM((tok, 256), BF16),
                pltpu.VMEM((1, 128), F32),
                pltpu.VMEM((nten, 1, 256), F32),
                dma((10,)),
                pltpu.VMEM((2, tok, 128), F32),
                pltpu.VMEM((2, tok, 128), F32),
                pltpu.VMEM((2 * groups, 128), jnp.int32),
                pltpu.SMEM((2 * groups, 128), jnp.int32),
                pltpu.VMEM((groups, kept + 1, 128, 128), BF16),
                pltpu.VMEM((groups, kept + 1, 128, 128), BF16),
                pltpu.VMEM((LANES_X, 2, 256, 128), BF16),
                pltpu.VMEM((192, 128), BF16),
                pltpu.VMEM((nz, 192, 128), BF16),
                pltpu.VMEM((64, 128), F32),
                pltpu.VMEM((128, 128), F32),
                pltpu.VMEM((2, 128, 128), F32),
                pltpu.VMEM((2, 128, 128), F32),
                pltpu.VMEM((64, 128), BF16),
                pltpu.VMEM((2, 128, 128), BF16),
                pltpu.VMEM((nten, tok, 256), BF16),
                pltpu.VMEM((tok, groups * 128), F32),
                pltpu.VMEM((tok, groups * 128), BF16),
                pltpu.VMEM((ny, tok, 256), BF16),
                pltpu.VMEM((ny, tok, 256), BF16),
                pltpu.VMEM((2, ny // 2 + 1, tok, 256), BF16),
                pltpu.VMEM((2, ny // 2 + 1, tok, 256), BF16),
                dma((3,)),
                dma((LANES_X,)),
                dma((LANES_X,)),
                dma((LANES_X,)),
                dma((LANES_X,)),
                dma((LANES_X,)),
                dma((LANES_X,)),
                dma((nz,)),
                dma((nz,)),
                dma((LANES_X,)),
                dma((LANES_X,)),
                dma((2, ny // 2, 2)),
                dma((2, ny // 2, 2)),
                dma((2, ny // 2, 2)),
                dma((2, ny // 2, 2)),
                dma((2,)),
                dma((ny,)),
                dma((ny,)),
                dma((2, ny // 2, 2)),
                dma((2, ny // 2, 2)),
            ],
            compiler_params=pltpu.CompilerParams(
                collective_id=0, has_side_effects=True, vmem_limit_bytes=VMEM_LIMIT
            ),
            name="layer",
        )(*(pltpu.with_memory_space_constraint(a, pltpu.HBM) for a in (
            queries.reshape(2 * tok, 128),
            keys.reshape(4 * tok, 128),
            values.reshape(4 * tok, 128),
            beta,
            decay,
            up_index,
            down_index,
            residual,
            out_gain.reshape(1, 128),
            ffn_gain.reshape(nten, 1, 256),
            up_blocks,
            down_kept_tiles,
        )))

    placed = (
        P("seq", "tensor", None),
        P(None, "seq", "tensor", None),
        P(None, "seq", "tensor", None),
        P(None, "tensor", "seq"),
        P("tensor", "seq"),
        P(),
        P("seq", "tensor"),
        P(),
        P("tensor", None, None, None),
        P("tensor", None),
        P("tensor", None, None, None),
        P("tensor", None),
    )
    return jax.shard_map(
        per_device, mesh=mesh, in_specs=placed, out_specs=P("seq", "tensor"), check_vma=False
    )
```

```python
import functools

import jax
import jax.numpy as jnp
from jax import lax
from jax.experimental import pallas as pl
from jax.experimental.pallas import tpu as pltpu
from jax.sharding import PartitionSpec as P

F32 = jnp.float32
BF16 = jnp.bfloat16
HIGHEST = lax.Precision.HIGHEST
LANES_X = 4
VMEM_LIMIT = 24 << 20
MESH = pl.DeviceIdType.MESH


def dot(a, b, contract=(1, 0), precision=None):
    return lax.dot_general(
        a,
        b,
        (((contract[0],), (contract[1],)), ((), ())),
        precision=precision,
        preferred_element_type=F32,
    )


def split(a):
    high = a.astype(BF16)
    return high, (a - high.astype(F32)).astype(BF16)


def mm3(a, b):
    ah, al = split(a)
    bh, bl = split(b)
    left = jnp.concatenate([ah, al], 1)
    right = jnp.concatenate(
        [jnp.concatenate([bh, bl], 1), jnp.concatenate([bh, jnp.zeros_like(bl)], 1)], 0
    )
    both = dot(left, right)
    n = b.shape[1]
    return both[:, :n] + both[:, n:]


def iota(shape, axis):
    return lax.broadcasted_iota(jnp.int32, shape, axis)


def unit_lower_inverse(lowers):
    n = lowers[0].shape[0]
    rows, cols = iota((n, n), 0), iota((n, n), 1)
    eye = (rows == cols).astype(F32)
    base = (rows >> 3) == (cols >> 3)
    n1 = [jnp.where(base, -low, 0.0) for low in lowers]
    n2 = [mm3(a, a) for a in n1]
    n3 = [mm3(a, b) for a, b in zip(n1, n2)]
    n4 = [mm3(a, a) for a in n2]
    y = [eye + a + b + c for a, b, c in zip(n1, n2, n3)]
    x = [a + mm3(a, b) for a, b in zip(y, n4)]
    shift = 3
    while (1 << shift) < n:
        pick = ((rows >> (shift + 1)) == (cols >> (shift + 1))) & ((rows >> shift) != (cols >> shift))
        links = [jnp.where(pick, low, 0.0) for low in lowers]
        right = [mm3(c, a) for c, a in zip(links, x)]
        x = [a - mm3(a, b) for a, b in zip(x, right)]
        shift += 1
    return x


def inverse_table(index, kept):
    lanes = iota((index.shape[0], 128), 1)
    found = jnp.full(lanes.shape, kept, jnp.int32)
    for j in range(kept):
        found = jnp.where(index[:, j : j + 1] == lanes, j, found)
    return found


def local_terms(q_ref, k_ref, v_ref, beta_ref, decay_ref, tw_ref, qt_ref, lo_ref):
    tok = q_ref.shape[0] // 2
    span = 2 * tok
    heads = 2
    half = span // 2

    kv = jnp.concatenate([k_ref[...], v_ref[...]], 1)
    small = jnp.concatenate(
        [decay_ref[...], beta_ref[0], beta_ref[1], jnp.zeros((2, tok), F32)], 0
    )
    s1 = small.astype(BF16)
    rest = small - s1.astype(F32)
    s2 = rest.astype(BF16)
    s3 = (rest - s2.astype(F32)).astype(BF16)
    parts = jnp.concatenate([s1, s2, s3, jnp.zeros_like(s1)], 0)
    m_at, t_at = iota((span, tok), 0), iota((span, tok), 1)
    upto = t_at <= (m_at >> 1)
    first = (t_at == (m_at >> 1)) & ((m_at & 1) == 0)
    second = (t_at == (m_at >> 1)) & ((m_at & 1) == 1)
    upto_tok = iota((tok, tok), 1) <= iota((tok, tok), 0)
    picks = jnp.concatenate([e.astype(BF16) for e in (upto, first, second, upto_tok)], 0)
    cols3 = dot(picks, parts, (1, 1))
    col = cols3[:, 0:8] + cols3[:, 8:16] + cols3[:, 16:24]
    rows3 = dot(parts, picks, (1, 1))
    row = rows3[0:8] + rows3[8:16] + rows3[16:24]
    run_col, one_col, two_col = col[:span], col[span : 2 * span], col[2 * span : 3 * span]
    tok_col = col[3 * span :]
    run_row, one_row, two_row = row[:, :span], row[:, span : 2 * span], row[:, 2 * span : 3 * span]

    rows, cols = iota((span, span), 0), iota((span, span), 1)
    below = cols < rows
    same = rows == cols
    reach = iota((tok, span), 1) <= 2 * iota((tok, span), 0) + 1
    eye = (iota((tok, tok), 0) == iota((tok, tok), 1)).astype(F32)
    row_of = iota((span, 4 * tok), 0)
    place = (row_of & 1) * span + (row_of >> 1) * 2
    column = iota((span, 4 * tok), 1)
    q_place = iota((tok, span), 0) * 2
    q_column = iota((tok, span), 1)

    ks, vs, qs, gammas, lowers, keep = [], [], [], [], [], []
    for h in range(heads):
        pick = (column == place + h).astype(BF16)
        both = dot(pick, kv).astype(BF16)
        k, v = both[:, :128], both[:, 128:]
        gram = dot(k, k, (1, 1))
        diag = jnp.where(same, gram, 0.0)
        rk_col = lax.rsqrt(jnp.sum(diag, 1, keepdims=True) + 1e-06)
        rk_row = lax.rsqrt(jnp.sum(diag, 0, keepdims=True) + 1e-06)
        run_c, run_r = run_col[:, h : h + 1], run_row[h : h + 1, :]
        beta_c = one_col[:, 2 + h : 3 + h] + two_col[:, 4 + h : 5 + h]
        beta_r = one_row[2 + h : 3 + h, :] + two_row[4 + h : 5 + h, :]
        fade = jnp.exp(jnp.where(below, run_c - run_r, 0.0))
        low = jnp.where(below, (beta_c * rk_col) * fade * gram * rk_row, 0.0)
        keep.append((k, v, rk_col, rk_row, run_c, run_r, beta_r, low))
        lowers += [low[:half, :half], low[half:, half:]]

    inverses = unit_lower_inverse(lowers)
    mids = [mm3(keep[h][7][half:, :half], inverses[2 * h]) for h in range(heads)]
    crosses = [mm3(inverses[2 * h + 1], mids[h]) for h in range(heads)]
    left = []
    for h in range(heads):
        k, v, rk_col, rk_row, run_c, run_r, beta_r, low = keep[h]
        a = jnp.concatenate(
            [
                jnp.concatenate([inverses[2 * h], jnp.zeros((half, half), F32)], 1),
                jnp.concatenate([-crosses[h], inverses[2 * h + 1]], 1),
            ],
            0,
        )
        a_val = a * beta_r
        a_key = a_val * (jnp.exp(run_r) * rk_row)
        ah, al = split(a_val)
        u = dot(ah, v) + dot(al, v)
        ah, al = split(a_key)
        w = dot(ah, k) + dot(al, k)
        last = run_c[span - 1 : span, :]
        remain = jnp.exp(last - run_c) * rk_col
        uh, ul = split(u * remain)
        write_t = dot(uh, k, (0, 0)) + dot(ul, k, (0, 0))
        wh, wl = split(w * remain)
        trans = jnp.exp(last) * eye - dot(k, wh, (0, 0)) - dot(k, wl, (0, 0))
        tw_ref[h, 0:64, :] = write_t[:64].astype(BF16)
        tw_ref[h, 64:192, :] = trans.astype(BF16)
        tw_ref[h, 192:256, :] = write_t[64:].astype(BF16)
        left.append((k, u, w, rk_row, run_r, tok_col[:, h : h + 1]))

    def queries():
        q_all = q_ref[...]
        for h in range(heads):
            k, u, w, rk_row, run_r, tok_run = left[h]
            q = dot((q_column == q_place + h).astype(BF16), q_all)
            rq = lax.rsqrt(jnp.sum(q * q, 1, keepdims=True) + 1e-06)
            qk = dot(q.astype(BF16), k, (1, 1))
            mixing = jnp.where(
                reach, jnp.exp(jnp.where(reach, tok_run - run_r, 0.0)) * qk * rq * rk_row, 0.0
            )
            mh, ml = split(mixing)
            bh, bl = split(jnp.concatenate([w, u], 1))
            mixed = dot(mh, bh) + dot(ml, bh) + dot(mh, bl)
            qt_ref[h] = (jnp.exp(tok_run) * rq) * q - mixed[:, :128]
            lo_ref[h] = mixed[:, 128:]

    return queries


def chain_step(state, trans, write):
    n = state.shape[0]
    high, low = split(state)
    both = dot(jnp.concatenate([high, low], 0), trans, (1, 1))
    return both[:n] + both[n:] + write.astype(F32)


def main_kernel(
    nz,
    ny,
    q_in,
    k_in,
    v_in,
    beta_in,
    decay_in,
    up_in,
    down_in,
    res_in,
    og_in,
    fg_in,
    up_hbm,
    down_hbm,
    out_ref,
    q_ref,
    k_ref,
    v_ref,
    beta_ref,
    decay_ref,
    up_ref,
    down_ref,
    res_ref,
    og_ref,
    fg_ref,
    l_sem,
    qt_ref,
    lo_ref,
    table_v,
    inv_ref,
    up_v,
    down_v,
    rx,
    zmsg,
    rz,
    chain,
    since,
    before_t,
    before_w,
    pmsg,
    rp,
    xg,
    acc,
    act,
    pair_out,
    pair_in,
    psum,
    rs,
    wsem,
    a_send,
    a_recv,
    b_send,
    b_recv,
    c_send,
    c_recv,
    z_send,
    z_recv,
    p_send,
    p_recv,
    g_send,
    g_recv,
    f_send,
    f_recv,
    o_sem,
    s_send,
    s_recv,
    r_send,
    r_recv,
):
    seq, ten = lax.axis_index("seq"), lax.axis_index("tensor")
    z, x = seq // LANES_X, lax.rem(seq, LANES_X)
    y, core = ten // 2, lax.rem(ten, 2)
    partner = y * 2 + 1 - core
    head, part = x // 2, lax.rem(x, 2)
    groups = up_hbm.shape[0]
    kept = up_hbm.shape[1]

    def at_x(o):
        return lax.rem(x + o, LANES_X)

    def at_y(o):
        return lax.rem(y + o, ny)

    barrier = pltpu.get_barrier_semaphore()
    peers = [(z * LANES_X + at_x(o), ten) for o in range(1, LANES_X)]
    peers += [(lax.rem(z + o, nz) * LANES_X + x, ten) for o in range(1, nz)]
    peers += [(seq, at_y(o) * 2 + core) for o in (1, 2, ny - 2, ny - 1)]
    peers += [(seq, partner)]
    for peer in peers:
        pl.semaphore_signal(barrier, inc=1, device_id=peer, device_id_type=MESH)

    inputs = (
        (k_in, k_ref),
        (v_in, v_ref),
        (q_in, q_ref),
        (beta_in, beta_ref),
        (decay_in, decay_ref),
        (up_in, up_ref),
        (down_in, down_ref),
        (res_in, res_ref),
        (og_in, og_ref),
        (fg_in, fg_ref),
    )
    loads = [
        pltpu.make_async_copy(here, there, l_sem.at[n]) for n, (here, there) in enumerate(inputs)
    ]
    for load in loads:
        load.start()
    load_up = pltpu.make_async_copy(up_hbm, up_v.at[:, pl.ds(0, kept)], wsem.at[0])
    load_down = pltpu.make_async_copy(down_hbm, down_v.at[:, pl.ds(0, kept)], wsem.at[1])
    load_up.start()
    load_down.start()
    for load in loads:
        load.wait()
    queries = local_terms(q_ref, k_ref, v_ref, beta_ref, decay_ref, rx.at[x], qt_ref, lo_ref)
    pl.semaphore_wait(barrier, len(peers))

    def remote(src, dst, send, recv, peer):
        return pltpu.make_async_remote_copy(
            src_ref=src,
            dst_ref=dst,
            send_sem=send,
            recv_sem=recv,
            device_id=peer,
            device_id_type=MESH,
        )

    w_rows = pl.ds(pl.multiple_of(part * 192, 64), 64)
    my_rows = pl.ds(pl.multiple_of(part * 64, 64), 192)

    def a_copy(o, only_write):
        there = at_x(o)
        h2, p2 = there // 2, lax.rem(there, 2)
        if only_write:
            rows = pl.ds(pl.multiple_of(p2 * 192, 64), 64)
        else:
            rows = pl.ds(pl.multiple_of(p2 * 64, 64), 192)
        return remote(
            rx.at[x, h2, rows],
            rx.at[x, h2, rows],
            a_send.at[o],
            a_recv.at[x],
            (z * LANES_X + there, ten),
        )

    def on_first(act_on):
        @pl.when(seq == 0)
        def _():
            act_on(True)

        @pl.when(seq != 0)
        def _():
            act_on(False)

    def a_wait(i):
        def wait(only_write):
            block = rx.at[i, head, w_rows if only_write else my_rows]
            remote(block, block, a_send.at[0], a_recv.at[i], (seq, ten)).wait_recv()

        @pl.when(i != x)
        def _():
            if i == 0:

                @pl.when(z == 0)
                def _():
                    wait(True)
                    rx[0, head, 64:192] = jnp.zeros((128, 128), BF16)

                @pl.when(z != 0)
                def _():
                    wait(False)
            else:
                wait(False)

    def b_copies(o):
        there = at_x(o)
        h2, p2 = there // 2, lax.rem(there, 2)
        rows = pl.ds(pl.multiple_of((1 - p2) * 192, 64), 64)
        peer = (z * LANES_X + there, ten)
        return (
            remote(
                rx.at[x, h2, rows], rx.at[x, h2, rows], b_send.at[o], b_recv.at[x], peer
            ),
            remote(
                rx.at[x, 1 - h2], rx.at[x, 1 - h2], c_send.at[o], c_recv.at[x], peer
            ),
        )

    for o in (2, 1, 3):
        on_first(lambda only_write: a_copy(o, only_write).start())

    chain[...] = jnp.zeros_like(chain)
    eye = (iota((128, 128), 0) == iota((128, 128), 1)).astype(F32)
    since[...] = eye
    for h in range(2):
        before_t[h] = eye
        before_w[h] = jnp.zeros((128, 128), F32)
    table_v[0:groups] = inverse_table(up_ref[...], kept)
    table_v[groups : 2 * groups] = inverse_table(down_ref[...], kept)
    load_table = pltpu.make_async_copy(table_v, inv_ref, wsem.at[2])
    load_table.start()
    for c in range(groups):
        up_v[c, kept] = jnp.zeros(up_v.shape[2:], BF16)
        down_v[c, kept] = jnp.zeros(up_v.shape[2:], BF16)
    queries()

    def apply(write, trans):
        high, low = split(trans)
        return dot(write, high, (1, 1)) + dot(write, low, (1, 1))

    def extend(trans, earlier):
        high, low = split(trans)
        both = dot(jnp.concatenate([high, low], 0), earlier)
        return both[:128] + both[128:]

    for i in (3, 2, 1):
        a_wait(i)
    ts = [rx[i, head, pl.ds(64, 128)] for i in range(1, LANES_X)]
    ws = [rx[i, head, w_rows] for i in range(1, LANES_X)]
    t32 = dot(ts[2], ts[1])
    w32 = dot(ws[1], ts[2], (1, 1)) + ws[2].astype(F32)
    t321 = extend(t32, ts[0])
    w321 = apply(ws[0], t32) + w32
    a_wait(0)
    zmsg[0:64] = (apply(rx[0, head, w_rows], t321) + w321).astype(BF16)
    zmsg[64:192] = extend(t321, rx[0, head, pl.ds(64, 128)]).astype(BF16)

    def z_copy(o, only_write):
        rows = pl.ds(0, 64 if only_write else 192)
        return remote(
            zmsg.at[rows],
            rz.at[z, rows],
            z_send.at[o],
            z_recv.at[z],
            ((z + o) * LANES_X + x, ten),
        )

    def on_first_group(act_on):
        @pl.when(z == 0)
        def _():
            act_on(True)

        @pl.when(z != 0)
        def _():
            act_on(False)

    for o in range(1, nz):

        @pl.when(z + o < nz)
        def _():
            on_first_group(lambda only_write: z_copy(o, only_write).start())

    for o in range(1, LANES_X):

        @pl.when(x + o < LANES_X)
        def _():
            for one in b_copies(o):
                one.start()

    def z_wait(i):
        block = rz.at[i, pl.ds(0, 64 if i == 0 else 192)]
        remote(block, block, z_send.at[0], z_recv.at[i], (seq, ten)).wait_recv()

    for i in range(nz - 2, 0, -1):

        @pl.when(i < z)
        def _():
            z_wait(i)
            chain[...] += apply(rz[i, 0:64], since[...])
            since[...] = extend(since[...], rz[i, 64:192])

    if nz > 1:

        @pl.when(z > 0)
        def _():
            z_wait(0)
            chain[...] += apply(rz[0, 0:64], since[...])

    entering = chain[...].astype(BF16)
    pmsg[...] = entering
    p_rows = pl.ds(pl.multiple_of(part * 64, 64), 64)
    rp[head, p_rows] = entering

    def p_copy(o):
        return remote(
            pmsg,
            rp.at[head, p_rows],
            p_send.at[o],
            p_recv.at[x],
            (z * LANES_X + at_x(o), ten),
        )

    for o in (2, 1, 3):
        p_copy(o).start()

    for i in range(LANES_X - 1):

        @pl.when(i < x)
        def _():
            other = pl.ds(pl.multiple_of((1 - part) * 192, 64), 64)
            remote(
                rx.at[i, head, other],
                rx.at[i, head, other],
                b_send.at[0],
                b_recv.at[i],
                (seq, ten),
            ).wait_recv()
            remote(
                rx.at[i, 1 - head], rx.at[i, 1 - head], c_send.at[0], c_recv.at[i], (seq, ten)
            ).wait_recv()
            for h in range(2):
                trans = rx[i, h, 64:192]
                write = jnp.concatenate([rx[i, h, 0:64], rx[i, h, 192:256]], 0)
                if i == 0:
                    before_t[h] = trans.astype(F32)
                    before_w[h] = write.astype(F32)
                else:
                    high, low = split(before_t[h])
                    both = dot(trans, jnp.concatenate([high, low], 1))
                    before_t[h] = both[:, :128] + both[:, 128:]
                    before_w[h] = chain_step(before_w[h], trans, write)

    for o in (1, 3, 2):
        source = at_x(o)
        rows = pl.ds(pl.multiple_of(lax.rem(source, 2) * 64, 64), 64)
        remote(
            rp.at[source // 2, rows],
            rp.at[source // 2, rows],
            p_send.at[o],
            p_recv.at[source],
            (seq, ten),
        ).wait_recv()

    state = [apply(rp[h], before_t[h]) + before_w[h] for h in range(2)]
    gain = og_ref[...]
    pieces = []
    for h in range(2):
        qh, ql = split(qt_ref[h])
        sh, sl = split(state[h])
        head_out = dot(qh, sh, (1, 1)) + dot(ql, sh, (1, 1)) + dot(qh, sl, (1, 1)) + lo_ref[h]
        power = jnp.mean(head_out * head_out, -1, keepdims=True)
        normed = head_out * lax.rsqrt(power + 1e-05) * gain
        pieces.append(res_ref[:, 128 * h : 128 * h + 128].astype(F32) + normed)
    xg[ten] = jnp.concatenate(pieces, 1).astype(BF16)

    reach = ny // 2
    ways = (1, -1)
    halves = [pl.ds(0, xg.shape[1] // 2), pl.ds(xg.shape[1] // 2, xg.shape[1] // 2)]

    def sent(i, d, part_at):
        return d < reach or part_at == i

    messages = [
        (i, d, p)
        for d in range(1, reach + 1)
        for p in range(2)
        for i in range(2)
        if sent(i, d, p)
    ]

    hop = (0, 1, 2, 1, 2)

    def across(i, d):
        return (seq, at_y(ny + ways[i] * hop[d]) * 2 + core)

    def ring(i, d, p):
        origin = 0 if d <= 2 else 2
        block = xg.at[at_y(ny - ways[i] * origin) * 2 + core, halves[p]]
        return remote(block, block, g_send.at[i, d - 1, p], g_recv.at[i, d - 1, p], across(i, d))

    def got(i, d, p):
        block = xg.at[at_y(ny - ways[i] * d) * 2 + core, halves[p]]
        remote(block, block, g_send.at[i, d - 1, p], g_recv.at[i, d - 1, p], (seq, ten)).wait_recv()

    def pass_on(i, d, p):
        block = xg.at[at_y(ny - ways[i] * d) * 2 + core, halves[p]]
        return remote(block, block, f_send.at[i, d - 1, p], f_recv.at[i, d - 1, p], (seq, partner))

    def passed(i, d, p):
        block = xg.at[at_y(ny - ways[i] * d) * 2 + 1 - core, halves[p]]
        remote(block, block, f_send.at[i, d - 1, p], f_recv.at[i, d - 1, p], (seq, ten)).wait_recv()

    def own_copy():
        return remote(xg.at[ten], xg.at[ten], o_sem.at[0], o_sem.at[1], (seq, partner))

    for level in (2, 1):
        for i, d, p in messages:
            if d == level:
                ring(i, d, p).start()
    own_copy().start()

    load_up.wait()
    load_down.wait()
    load_table.wait()

    def absorb(slot, first, power):
        wide = xg[slot].astype(F32)
        power = power + jnp.sum(wide * wide, -1, keepdims=True)
        scaled = (wide * fg_ref[slot]).astype(BF16)
        weights = jnp.concatenate(
            [
                jnp.concatenate(
                    [up_v[c, inv_ref[c, 2 * slot + b]] for c in range(groups)], 1
                )
                for b in range(2)
            ],
            0,
        )
        term = dot(scaled, weights)
        if first:
            acc[...] = term
        else:
            acc[...] += term
        return power

    def blocks(d):
        return [at_y(d)] if d == reach else [at_y(ny - d), at_y(d)]

    power = absorb(ten, True, jnp.zeros((xg.shape[1], 1), F32))
    remote(xg.at[partner], xg.at[partner], o_sem.at[0], o_sem.at[1], (seq, ten)).wait_recv()
    power = absorb(partner, False, power)

    def take(d):
        for i, e, p in messages:
            if e == d:
                got(i, d, p)
                if d == 2:
                    for later in (4, 3):
                        if sent(i, later, p):
                            ring(i, later, p).start()
                pass_on(i, d, p).start()

    def near(d, power):
        for where in blocks(d):
            power = absorb(where * 2 + core, False, power)
        return power

    def far_side(d, power):
        for i, e, p in messages:
            if e == d:
                passed(i, e, p)
        for where in blocks(d):
            power = absorb(where * 2 + 1 - core, False, power)
        return power

    take(2)
    power = near(2, power)
    take(1)
    power = near(1, power)
    power = far_side(2, power)
    power = far_side(1, power)
    take(3)
    power = near(3, power)
    take(4)
    power = near(4, power)
    power = far_side(3, power)
    power = far_side(4, power)

    width = 256 * xg.shape[0]
    scale = lax.rsqrt(power / width + 1e-05)
    act[...] = jax.nn.gelu(acc[...] * scale).astype(BF16)

    def share(slot):
        weights = jnp.concatenate(
            [
                jnp.concatenate(
                    [down_v[c, inv_ref[groups + c, 2 * slot + b]] for b in range(2)], 1
                )
                for c in range(groups)
            ],
            0,
        )
        return dot(act[...], weights).astype(BF16)

    def s_copy(off):
        k = off + reach - 1
        return remote(
            pair_out.at[k], pair_in.at[k], s_send.at[k], s_recv.at[k], (seq, partner)
        )

    def offer(off):
        pair_out[off + reach - 1] = share(at_y(ny + off) * 2 + 1 - core)
        s_copy(off).start()

    def pair_sum(off):
        mine = share(at_y(ny + off) * 2 + core).astype(F32)
        s_copy(off).wait_recv()
        return mine + pair_in[off + reach - 1].astype(F32)

    def m_copy(i, d, p):
        return remote(
            psum.at[i, d, halves[p]],
            rs.at[i, d, halves[p]],
            r_send.at[i, d - 1, p],
            r_recv.at[i, d - 1, p],
            across(i, d),
        )

    def m_got(i, d, p):
        block = rs.at[i, d, halves[p]]
        remote(block, block, r_send.at[i, d - 1, p], r_recv.at[i, d - 1, p], (seq, ten)).wait_recv()
        return rs[i, d, halves[p]].astype(F32)

    rows_dev = xg.shape[1] // 2

    def rows_of(value, p):
        return value[p * rows_dev : (p + 1) * rows_dev]

    def ship(i, d, p, value):
        psum[i, d, halves[p]] = value.astype(BF16)
        m_copy(i, d, p).start()

    def ship_both(d):
        for i in range(2):
            value = pair_sum(ways[i] * d)
            for p in range(2):
                ship(i, d, p, rows_of(value, p))

    for off in (4, 3, -3):
        offer(off)
    far = pair_sum(4)
    for i in range(2):
        ship(i, 4, i, rows_of(far, i))
    for off in (2, -2):
        offer(off)
    ship_both(3)
    for off in (1, -1, 0):
        offer(off)
    ship_both(1)
    sums = [pair_sum(2), pair_sum(-2)]
    total = pair_sum(0) + xg[ten].astype(F32)
    for p in range(2):
        for i in range(2):
            value = rows_of(sums[i], p) + m_got(i, 3, p)
            if sent(i, 4, p):
                value = value + m_got(i, 4, p)
            ship(i, 2, p, value)
    for p in range(2):
        value = rows_of(total, p)
        for d in (1, 2):
            for i in range(2):
                value = value + m_got(i, d, p)
        out_ref[halves[p], :] = value.astype(BF16)

    for o in range(1, LANES_X):
        on_first(lambda only_write: a_copy(o, only_write).wait_send())
        p_copy(o).wait_send()

        @pl.when(x + o < LANES_X)
        def _():
            for one in b_copies(o):
                one.wait_send()

    for o in range(1, nz):

        @pl.when(z + o < nz)
        def _():
            on_first_group(lambda only_write: z_copy(o, only_write).wait_send())

    own_copy().wait_send()
    for off in range(1 - reach, reach + 1):
        s_copy(off).wait_send()
    for i, d, p in messages:
        ring(i, d, p).wait_send()
        pass_on(i, d, p).wait_send()
        m_copy(i, d, p).wait_send()


def solution(mesh):
    nseq, nten = mesh.shape["seq"], mesh.shape["tensor"]
    nz, ny = nseq // LANES_X, nten // 2
    vmem = pl.BlockSpec(memory_space=pltpu.VMEM)
    hbm = pl.BlockSpec(memory_space=pltpu.HBM)
    dma = pltpu.SemaphoreType.DMA

    def per_device(
        queries,
        keys,
        values,
        beta,
        decay,
        out_gain,
        residual,
        ffn_gain,
        up_blocks,
        up_index,
        down_kept_tiles,
        down_index,
    ):
        tok = queries.shape[0]
        groups, kept = up_index.shape
        return pl.pallas_call(
            functools.partial(main_kernel, nz, ny),
            out_shape=jax.ShapeDtypeStruct((tok, 256), BF16),
            in_specs=[hbm] * 12,
            out_specs=vmem,
            scratch_shapes=[
                pltpu.VMEM((2 * tok, 128), BF16),
                pltpu.VMEM((4 * tok, 128), BF16),
                pltpu.VMEM((4 * tok, 128), BF16),
                pltpu.VMEM((2, 2, tok), F32),
                pltpu.VMEM((2, tok), F32),
                pltpu.VMEM((groups, kept), jnp.int32),
                pltpu.VMEM((groups, kept), jnp.int32),
                pltpu.VMEM((tok, 256), BF16),
                pltpu.VMEM((1, 128), F32),
                pltpu.VMEM((nten, 1, 256), F32),
                dma((10,)),
                pltpu.VMEM((2, tok, 128), F32),
                pltpu.VMEM((2, tok, 128), F32),
                pltpu.VMEM((2 * groups, 128), jnp.int32),
                pltpu.SMEM((2 * groups, 128), jnp.int32),
                pltpu.VMEM((groups, kept + 1, 128, 128), BF16),
                pltpu.VMEM((groups, kept + 1, 128, 128), BF16),
                pltpu.VMEM((LANES_X, 2, 256, 128), BF16),
                pltpu.VMEM((192, 128), BF16),
                pltpu.VMEM((nz, 192, 128), BF16),
                pltpu.VMEM((64, 128), F32),
                pltpu.VMEM((128, 128), F32),
                pltpu.VMEM((2, 128, 128), F32),
                pltpu.VMEM((2, 128, 128), F32),
                pltpu.VMEM((64, 128), BF16),
                pltpu.VMEM((2, 128, 128), BF16),
                pltpu.VMEM((nten, tok, 256), BF16),
                pltpu.VMEM((tok, groups * 128), F32),
                pltpu.VMEM((tok, groups * 128), BF16),
                pltpu.VMEM((ny, tok, 256), BF16),
                pltpu.VMEM((ny, tok, 256), BF16),
                pltpu.VMEM((2, ny // 2 + 1, tok, 256), BF16),
                pltpu.VMEM((2, ny // 2 + 1, tok, 256), BF16),
                dma((3,)),
                dma((LANES_X,)),
                dma((LANES_X,)),
                dma((LANES_X,)),
                dma((LANES_X,)),
                dma((LANES_X,)),
                dma((LANES_X,)),
                dma((nz,)),
                dma((nz,)),
                dma((LANES_X,)),
                dma((LANES_X,)),
                dma((2, ny // 2, 2)),
                dma((2, ny // 2, 2)),
                dma((2, ny // 2, 2)),
                dma((2, ny // 2, 2)),
                dma((2,)),
                dma((ny,)),
                dma((ny,)),
                dma((2, ny // 2, 2)),
                dma((2, ny // 2, 2)),
            ],
            compiler_params=pltpu.CompilerParams(
                collective_id=0, has_side_effects=True, vmem_limit_bytes=VMEM_LIMIT
            ),
            name="layer",
        )(*(pltpu.with_memory_space_constraint(a, pltpu.HBM) for a in (
            queries.reshape(2 * tok, 128),
            keys.reshape(4 * tok, 128),
            values.reshape(4 * tok, 128),
            beta,
            decay,
            up_index,
            down_index,
            residual,
            out_gain.reshape(1, 128),
            ffn_gain.reshape(nten, 1, 256),
            up_blocks,
            down_kept_tiles,
        )))

    placed = (
        P("seq", "tensor", None),
        P(None, "seq", "tensor", None),
        P(None, "seq", "tensor", None),
        P(None, "tensor", "seq"),
        P("tensor", "seq"),
        P(),
        P("seq", "tensor"),
        P(),
        P("tensor", None, None, None),
        P("tensor", None),
        P("tensor", None, None, None),
        P("tensor", None),
    )
    return jax.shard_map(
        per_device, mesh=mesh, in_specs=placed, out_specs=P("seq", "tensor"), check_vma=False
    )
```

```python
import functools

import jax
import jax.numpy as jnp
from jax import lax
from jax.experimental import pallas as pl
from jax.experimental.pallas import tpu as pltpu
from jax.sharding import PartitionSpec as P

F32 = jnp.float32
BF16 = jnp.bfloat16
HIGHEST = lax.Precision.HIGHEST
LANES_X = 4
VMEM_LIMIT = 24 << 20
MESH = pl.DeviceIdType.MESH


def dot(a, b, contract=(1, 0), precision=None):
    return lax.dot_general(
        a,
        b,
        (((contract[0],), (contract[1],)), ((), ())),
        precision=precision,
        preferred_element_type=F32,
    )


def split(a):
    high = a.astype(BF16)
    return high, (a - high.astype(F32)).astype(BF16)


def mm3(a, b):
    ah, al = split(a)
    bh, bl = split(b)
    left = jnp.concatenate([ah, al], 1)
    right = jnp.concatenate(
        [jnp.concatenate([bh, bl], 1), jnp.concatenate([bh, jnp.zeros_like(bl)], 1)], 0
    )
    both = dot(left, right)
    n = b.shape[1]
    return both[:, :n] + both[:, n:]


def iota(shape, axis):
    return lax.broadcasted_iota(jnp.int32, shape, axis)


def unit_lower_inverse(lowers):
    n = lowers[0].shape[0]
    rows, cols = iota((n, n), 0), iota((n, n), 1)
    eye = (rows == cols).astype(F32)
    base = (rows >> 3) == (cols >> 3)
    n1 = [jnp.where(base, -low, 0.0) for low in lowers]
    n2 = [mm3(a, a) for a in n1]
    n3 = [mm3(a, b) for a, b in zip(n1, n2)]
    n4 = [mm3(a, a) for a in n2]
    y = [eye + a + b + c for a, b, c in zip(n1, n2, n3)]
    x = [a + mm3(a, b) for a, b in zip(y, n4)]
    shift = 3
    while (1 << shift) < n:
        pick = ((rows >> (shift + 1)) == (cols >> (shift + 1))) & ((rows >> shift) != (cols >> shift))
        links = [jnp.where(pick, low, 0.0) for low in lowers]
        right = [mm3(c, a) for c, a in zip(links, x)]
        x = [a - mm3(a, b) for a, b in zip(x, right)]
        shift += 1
    return x


def inverse_table(index, kept):
    lanes = iota((index.shape[0], 128), 1)
    found = jnp.full(lanes.shape, kept, jnp.int32)
    for j in range(kept):
        found = jnp.where(index[:, j : j + 1] == lanes, j, found)
    return found


def local_terms(q_ref, k_ref, v_ref, beta_ref, decay_ref, tw_ref, qt_ref, lo_ref):
    tok = q_ref.shape[0] // 2
    span = 2 * tok
    heads = 2
    half = span // 2

    kv = jnp.concatenate([k_ref[...], v_ref[...]], 1)
    small = jnp.concatenate(
        [decay_ref[...], beta_ref[0], beta_ref[1], jnp.zeros((2, tok), F32)], 0
    )
    s1 = small.astype(BF16)
    rest = small - s1.astype(F32)
    s2 = rest.astype(BF16)
    s3 = (rest - s2.astype(F32)).astype(BF16)
    parts = jnp.concatenate([s1, s2, s3, jnp.zeros_like(s1)], 0)
    m_at, t_at = iota((span, tok), 0), iota((span, tok), 1)
    upto = t_at <= (m_at >> 1)
    first = (t_at == (m_at >> 1)) & ((m_at & 1) == 0)
    second = (t_at == (m_at >> 1)) & ((m_at & 1) == 1)
    upto_tok = iota((tok, tok), 1) <= iota((tok, tok), 0)
    picks = jnp.concatenate([e.astype(BF16) for e in (upto, first, second, upto_tok)], 0)
    cols3 = dot(picks, parts, (1, 1))
    col = cols3[:, 0:8] + cols3[:, 8:16] + cols3[:, 16:24]
    rows3 = dot(parts, picks, (1, 1))
    row = rows3[0:8] + rows3[8:16] + rows3[16:24]
    run_col, one_col, two_col = col[:span], col[span : 2 * span], col[2 * span : 3 * span]
    tok_col = col[3 * span :]
    run_row, one_row, two_row = row[:, :span], row[:, span : 2 * span], row[:, 2 * span : 3 * span]

    rows, cols = iota((span, span), 0), iota((span, span), 1)
    below = cols < rows
    same = rows == cols
    reach = iota((tok, span), 1) <= 2 * iota((tok, span), 0) + 1
    eye = (iota((tok, tok), 0) == iota((tok, tok), 1)).astype(F32)
    row_of = iota((span, 4 * tok), 0)
    place = (row_of & 1) * span + (row_of >> 1) * 2
    column = iota((span, 4 * tok), 1)
    q_place = iota((tok, span), 0) * 2
    q_column = iota((tok, span), 1)

    ks, vs, qs, gammas, lowers, keep = [], [], [], [], [], []
    for h in range(heads):
        pick = (column == place + h).astype(BF16)
        both = dot(pick, kv).astype(BF16)
        k, v = both[:, :128], both[:, 128:]
        gram = dot(k, k, (1, 1))
        diag = jnp.where(same, gram, 0.0)
        rk_col = lax.rsqrt(jnp.sum(diag, 1, keepdims=True) + 1e-06)
        rk_row = lax.rsqrt(jnp.sum(diag, 0, keepdims=True) + 1e-06)
        run_c, run_r = run_col[:, h : h + 1], run_row[h : h + 1, :]
        beta_c = one_col[:, 2 + h : 3 + h] + two_col[:, 4 + h : 5 + h]
        beta_r = one_row[2 + h : 3 + h, :] + two_row[4 + h : 5 + h, :]
        fade = jnp.exp(jnp.where(below, run_c - run_r, 0.0))
        low = jnp.where(below, (beta_c * rk_col) * fade * gram * rk_row, 0.0)
        keep.append((k, v, rk_col, rk_row, run_c, run_r, beta_r, low))
        lowers += [low[:half, :half], low[half:, half:]]

    inverses = unit_lower_inverse(lowers)
    mids = [mm3(keep[h][7][half:, :half], inverses[2 * h]) for h in range(heads)]
    crosses = [mm3(inverses[2 * h + 1], mids[h]) for h in range(heads)]
    left = []
    for h in range(heads):
        k, v, rk_col, rk_row, run_c, run_r, beta_r, low = keep[h]
        a = jnp.concatenate(
            [
                jnp.concatenate([inverses[2 * h], jnp.zeros((half, half), F32)], 1),
                jnp.concatenate([-crosses[h], inverses[2 * h + 1]], 1),
            ],
            0,
        )
        a_val = a * beta_r
        a_key = a_val * (jnp.exp(run_r) * rk_row)
        ah, al = split(a_val)
        u = dot(ah, v) + dot(al, v)
        ah, al = split(a_key)
        w = dot(ah, k) + dot(al, k)
        last = run_c[span - 1 : span, :]
        remain = jnp.exp(last - run_c) * rk_col
        uh, ul = split(u * remain)
        write_t = dot(uh, k, (0, 0)) + dot(ul, k, (0, 0))
        wh, wl = split(w * remain)
        trans = jnp.exp(last) * eye - dot(k, wh, (0, 0)) - dot(k, wl, (0, 0))
        tw_ref[h, 0:64, :] = write_t[:64].astype(BF16)
        tw_ref[h, 64:192, :] = trans.astype(BF16)
        tw_ref[h, 192:256, :] = write_t[64:].astype(BF16)
        left.append((k, u, w, rk_row, run_r, tok_col[:, h : h + 1]))

    def queries():
        q_all = q_ref[...]
        for h in range(heads):
            k, u, w, rk_row, run_r, tok_run = left[h]
            q = dot((q_column == q_place + h).astype(BF16), q_all)
            rq = lax.rsqrt(jnp.sum(q * q, 1, keepdims=True) + 1e-06)
            qk = dot(q.astype(BF16), k, (1, 1))
            mixing = jnp.where(
                reach, jnp.exp(jnp.where(reach, tok_run - run_r, 0.0)) * qk * rq * rk_row, 0.0
            )
            mh, ml = split(mixing)
            bh, bl = split(jnp.concatenate([w, u], 1))
            mixed = dot(mh, bh) + dot(ml, bh) + dot(mh, bl)
            qt_ref[h] = (jnp.exp(tok_run) * rq) * q - mixed[:, :128]
            lo_ref[h] = mixed[:, 128:]

    return queries


def chain_step(state, trans, write):
    n = state.shape[0]
    high, low = split(state)
    both = dot(jnp.concatenate([high, low], 0), trans, (1, 1))
    return both[:n] + both[n:] + write.astype(F32)


def main_kernel(
    nz,
    ny,
    q_in,
    k_in,
    v_in,
    beta_in,
    decay_in,
    up_in,
    down_in,
    res_in,
    og_in,
    fg_in,
    up_hbm,
    down_hbm,
    out_ref,
    q_ref,
    k_ref,
    v_ref,
    beta_ref,
    decay_ref,
    up_ref,
    down_ref,
    res_ref,
    og_ref,
    fg_ref,
    l_sem,
    qt_ref,
    lo_ref,
    table_v,
    inv_ref,
    up_v,
    down_v,
    rx,
    zmsg,
    rz,
    chain,
    since,
    before_t,
    before_w,
    pmsg,
    rp,
    xg,
    acc,
    act,
    pair_out,
    pair_in,
    psum,
    rs,
    wsem,
    a_send,
    a_recv,
    b_send,
    b_recv,
    c_send,
    c_recv,
    z_send,
    z_recv,
    p_send,
    p_recv,
    g_send,
    g_recv,
    f_send,
    f_recv,
    o_sem,
    s_send,
    s_recv,
    r_send,
    r_recv,
):
    seq, ten = lax.axis_index("seq"), lax.axis_index("tensor")
    z, x = seq // LANES_X, lax.rem(seq, LANES_X)
    y, core = ten // 2, lax.rem(ten, 2)
    partner = y * 2 + 1 - core
    head, part = x // 2, lax.rem(x, 2)
    groups = up_hbm.shape[0]
    kept = up_hbm.shape[1]

    def at_x(o):
        return lax.rem(x + o, LANES_X)

    def at_y(o):
        return lax.rem(y + o, ny)

    barrier = pltpu.get_barrier_semaphore()
    peers = [(z * LANES_X + at_x(o), ten) for o in range(1, LANES_X)]
    peers += [(lax.rem(z + o, nz) * LANES_X + x, ten) for o in range(1, nz)]
    peers += [(seq, at_y(o) * 2 + core) for o in (1, 2, ny - 2, ny - 1)]
    peers += [(seq, partner)]
    inputs = (
        (k_in, k_ref),
        (v_in, v_ref),
        (q_in, q_ref),
        (beta_in, beta_ref),
        (decay_in, decay_ref),
        (up_in, up_ref),
        (down_in, down_ref),
        (res_in, res_ref),
        (og_in, og_ref),
        (fg_in, fg_ref),
    )
    loads = [
        pltpu.make_async_copy(here, there, l_sem.at[n]) for n, (here, there) in enumerate(inputs)
    ]
    for load in loads:
        load.start()
    for peer in peers:
        pl.semaphore_signal(barrier, inc=1, device_id=peer, device_id_type=MESH)
    load_up = pltpu.make_async_copy(up_hbm, up_v.at[:, pl.ds(0, kept)], wsem.at[0])
    load_down = pltpu.make_async_copy(down_hbm, down_v.at[:, pl.ds(0, kept)], wsem.at[1])
    load_up.start()
    load_down.start()
    for load in loads:
        load.wait()
    queries = local_terms(q_ref, k_ref, v_ref, beta_ref, decay_ref, rx.at[x], qt_ref, lo_ref)
    pl.semaphore_wait(barrier, len(peers))

    def remote(src, dst, send, recv, peer):
        return pltpu.make_async_remote_copy(
            src_ref=src,
            dst_ref=dst,
            send_sem=send,
            recv_sem=recv,
            device_id=peer,
            device_id_type=MESH,
        )

    w_rows = pl.ds(pl.multiple_of(part * 192, 64), 64)
    my_rows = pl.ds(pl.multiple_of(part * 64, 64), 192)

    def a_copy(o, only_write):
        there = at_x(o)
        h2, p2 = there // 2, lax.rem(there, 2)
        if only_write:
            rows = pl.ds(pl.multiple_of(p2 * 192, 64), 64)
        else:
            rows = pl.ds(pl.multiple_of(p2 * 64, 64), 192)
        return remote(
            rx.at[x, h2, rows],
            rx.at[x, h2, rows],
            a_send.at[o],
            a_recv.at[x],
            (z * LANES_X + there, ten),
        )

    def on_first(act_on):
        @pl.when(seq == 0)
        def _():
            act_on(True)

        @pl.when(seq != 0)
        def _():
            act_on(False)

    def a_wait(i):
        def wait(only_write):
            block = rx.at[i, head, w_rows if only_write else my_rows]
            remote(block, block, a_send.at[0], a_recv.at[i], (seq, ten)).wait_recv()

        @pl.when(i != x)
        def _():
            if i == 0:

                @pl.when(z == 0)
                def _():
                    wait(True)
                    rx[0, head, 64:192] = jnp.zeros((128, 128), BF16)

                @pl.when(z != 0)
                def _():
                    wait(False)
            else:
                wait(False)

    def b_copies(o):
        there = at_x(o)
        h2, p2 = there // 2, lax.rem(there, 2)
        rows = pl.ds(pl.multiple_of((1 - p2) * 192, 64), 64)
        peer = (z * LANES_X + there, ten)
        return (
            remote(
                rx.at[x, h2, rows], rx.at[x, h2, rows], b_send.at[o], b_recv.at[x], peer
            ),
            remote(
                rx.at[x, 1 - h2], rx.at[x, 1 - h2], c_send.at[o], c_recv.at[x], peer
            ),
        )

    for o in (2, 1, 3):
        on_first(lambda only_write: a_copy(o, only_write).start())

    chain[...] = jnp.zeros_like(chain)
    eye = (iota((128, 128), 0) == iota((128, 128), 1)).astype(F32)
    since[...] = eye
    for h in range(2):
        before_t[h] = eye
        before_w[h] = jnp.zeros((128, 128), F32)
    table_v[0:groups] = inverse_table(up_ref[...], kept)
    table_v[groups : 2 * groups] = inverse_table(down_ref[...], kept)
    load_table = pltpu.make_async_copy(table_v, inv_ref, wsem.at[2])
    load_table.start()
    for c in range(groups):
        up_v[c, kept] = jnp.zeros(up_v.shape[2:], BF16)
        down_v[c, kept] = jnp.zeros(up_v.shape[2:], BF16)
    queries()

    def apply(write, trans):
        high, low = split(trans)
        return dot(write, high, (1, 1)) + dot(write, low, (1, 1))

    def extend(trans, earlier):
        high, low = split(trans)
        both = dot(jnp.concatenate([high, low], 0), earlier)
        return both[:128] + both[128:]

    for i in (3, 2, 1):
        a_wait(i)
    ts = [rx[i, head, pl.ds(64, 128)] for i in range(1, LANES_X)]
    ws = [rx[i, head, w_rows] for i in range(1, LANES_X)]
    t32 = dot(ts[2], ts[1])
    w32 = dot(ws[1], ts[2], (1, 1)) + ws[2].astype(F32)
    t321 = extend(t32, ts[0])
    w321 = apply(ws[0], t32) + w32
    a_wait(0)
    zmsg[0:64] = (apply(rx[0, head, w_rows], t321) + w321).astype(BF16)
    zmsg[64:192] = extend(t321, rx[0, head, pl.ds(64, 128)]).astype(BF16)

    def z_copy(o, only_write):
        rows = pl.ds(0, 64 if only_write else 192)
        return remote(
            zmsg.at[rows],
            rz.at[z, rows],
            z_send.at[o],
            z_recv.at[z],
            ((z + o) * LANES_X + x, ten),
        )

    def on_first_group(act_on):
        @pl.when(z == 0)
        def _():
            act_on(True)

        @pl.when(z != 0)
        def _():
            act_on(False)

    for o in sorted(range(1, nz), key=lambda o: -min(o, nz - o)):

        @pl.when(z + o < nz)
        def _():
            on_first_group(lambda only_write: z_copy(o, only_write).start())

    for o in range(1, LANES_X):

        @pl.when(x + o < LANES_X)
        def _():
            for one in b_copies(o):
                one.start()

    def z_wait(i):
        block = rz.at[i, pl.ds(0, 64 if i == 0 else 192)]
        remote(block, block, z_send.at[0], z_recv.at[i], (seq, ten)).wait_recv()

    for i in range(nz - 2, 0, -1):

        @pl.when(i < z)
        def _():
            z_wait(i)
            chain[...] += apply(rz[i, 0:64], since[...])
            since[...] = extend(since[...], rz[i, 64:192])

    if nz > 1:

        @pl.when(z > 0)
        def _():
            z_wait(0)
            chain[...] += apply(rz[0, 0:64], since[...])

    entering = chain[...].astype(BF16)
    pmsg[...] = entering
    p_rows = pl.ds(pl.multiple_of(part * 64, 64), 64)
    rp[head, p_rows] = entering

    def p_copy(o):
        return remote(
            pmsg,
            rp.at[head, p_rows],
            p_send.at[o],
            p_recv.at[x],
            (z * LANES_X + at_x(o), ten),
        )

    for o in (2, 1, 3):
        p_copy(o).start()

    for i in range(LANES_X - 1):

        @pl.when(i < x)
        def _():
            other = pl.ds(pl.multiple_of((1 - part) * 192, 64), 64)
            remote(
                rx.at[i, head, other],
                rx.at[i, head, other],
                b_send.at[0],
                b_recv.at[i],
                (seq, ten),
            ).wait_recv()
            remote(
                rx.at[i, 1 - head], rx.at[i, 1 - head], c_send.at[0], c_recv.at[i], (seq, ten)
            ).wait_recv()
            for h in range(2):
                trans = rx[i, h, 64:192]
                write = jnp.concatenate([rx[i, h, 0:64], rx[i, h, 192:256]], 0)
                if i == 0:
                    before_t[h] = trans.astype(F32)
                    before_w[h] = write.astype(F32)
                else:
                    high, low = split(before_t[h])
                    both = dot(trans, jnp.concatenate([high, low], 1))
                    before_t[h] = both[:, :128] + both[:, 128:]
                    before_w[h] = chain_step(before_w[h], trans, write)

    for o in (1, 3, 2):
        source = at_x(o)
        rows = pl.ds(pl.multiple_of(lax.rem(source, 2) * 64, 64), 64)
        remote(
            rp.at[source // 2, rows],
            rp.at[source // 2, rows],
            p_send.at[o],
            p_recv.at[source],
            (seq, ten),
        ).wait_recv()

    state = [apply(rp[h], before_t[h]) + before_w[h] for h in range(2)]
    gain = og_ref[...]
    pieces = []
    for h in range(2):
        qh, ql = split(qt_ref[h])
        sh, sl = split(state[h])
        head_out = dot(qh, sh, (1, 1)) + dot(ql, sh, (1, 1)) + dot(qh, sl, (1, 1)) + lo_ref[h]
        power = jnp.mean(head_out * head_out, -1, keepdims=True)
        normed = head_out * lax.rsqrt(power + 1e-05) * gain
        pieces.append(res_ref[:, 128 * h : 128 * h + 128].astype(F32) + normed)
    xg[ten] = jnp.concatenate(pieces, 1).astype(BF16)

    reach = ny // 2
    ways = (1, -1)
    halves = [pl.ds(0, xg.shape[1] // 2), pl.ds(xg.shape[1] // 2, xg.shape[1] // 2)]

    def sent(i, d, part_at):
        return d < reach or part_at == i

    messages = [
        (i, d, p)
        for d in range(1, reach + 1)
        for p in range(2)
        for i in range(2)
        if sent(i, d, p)
    ]

    hop = (0, 1, 2, 1, 2)

    def across(i, d):
        return (seq, at_y(ny + ways[i] * hop[d]) * 2 + core)

    rows_all = xg.shape[1]
    quarter = rows_all // 4
    quarters = [(i, q) for q in range(4) for i in range(2)]
    crossing = [(i, 2, q * quarter, quarter) for i, q in quarters]
    crossing += [(i, 1, 0, rows_all) for i in range(2)]
    crossing += [(i, 3, q * quarter, quarter) for i, q in quarters]
    crossing += [(i, 4, q * quarter, quarter) for i, q in quarters if q % 2 == i]
    inside = [(i, d, 0, rows_all) for d in (1, 2) for i in range(2)]
    inside += [(i, 3, s * 2 * quarter, 2 * quarter) for s in range(2) for i in range(2)]
    inside += [key for key in crossing if key[1] == 4]

    def block_of(i, d, side, start, count):
        slot = at_y(ny - ways[i] * d) * 2 + (core if side == 0 else 1 - core)
        return xg.at[slot, pl.ds(start, count)]

    def ring(key):
        i, d, start, count = key
        n = crossing.index(key)
        block = block_of(i, 0 if d <= 2 else 2, 0, start, count)
        return remote(block, block, g_send.at[n], g_recv.at[n], across(i, d))

    def got(key):
        i, d, start, count = key
        n = crossing.index(key)
        block = block_of(i, d, 0, start, count)
        remote(block, block, g_send.at[n], g_recv.at[n], (seq, ten)).wait_recv()

    def pass_on(key):
        i, d, start, count = key
        n = inside.index(key)
        block = block_of(i, d, 0, start, count)
        return remote(block, block, f_send.at[n], f_recv.at[n], (seq, partner))

    def passed(key):
        i, d, start, count = key
        n = inside.index(key)
        block = block_of(i, d, 1, start, count)
        remote(block, block, f_send.at[n], f_recv.at[n], (seq, ten)).wait_recv()

    def own_copy():
        return remote(xg.at[ten], xg.at[ten], o_sem.at[0], o_sem.at[1], (seq, partner))

    for level in (2, 1):
        for key in crossing:
            if key[1] == level:
                ring(key).start()
    own_copy().start()

    load_up.wait()
    load_down.wait()
    load_table.wait()

    def absorb(slot, first, power):
        wide = xg[slot].astype(F32)
        power = power + jnp.sum(wide * wide, -1, keepdims=True)
        scaled = (wide * fg_ref[slot]).astype(BF16)
        weights = jnp.concatenate(
            [
                jnp.concatenate(
                    [up_v[c, inv_ref[c, 2 * slot + b]] for c in range(groups)], 1
                )
                for b in range(2)
            ],
            0,
        )
        term = dot(scaled, weights)
        if first:
            acc[...] = term
        else:
            acc[...] += term
        return power

    def blocks(d):
        return [at_y(d)] if d == reach else [at_y(ny - d), at_y(d)]

    power = absorb(ten, True, jnp.zeros((xg.shape[1], 1), F32))
    remote(xg.at[partner], xg.at[partner], o_sem.at[0], o_sem.at[1], (seq, ten)).wait_recv()
    power = absorb(partner, False, power)

    def near(d, power):
        for where in blocks(d):
            power = absorb(where * 2 + core, False, power)
        return power

    def far_side(d, power):
        for key in inside:
            if key[1] == d:
                passed(key)
        for where in blocks(d):
            power = absorb(where * 2 + 1 - core, False, power)
        return power

    for i, q in quarters:
        start = q * quarter
        got((i, 2, start, quarter))
        if q % 2 == i:
            ring((i, 4, start, quarter)).start()
        ring((i, 3, start, quarter)).start()
    for i in range(2):
        pass_on((i, 2, 0, rows_all)).start()
    for i in range(2):
        got((i, 1, 0, rows_all))
        pass_on((i, 1, 0, rows_all)).start()
    power = near(2, power)
    power = near(1, power)
    power = far_side(2, power)
    power = far_side(1, power)
    for q in range(4):
        start = q * quarter
        for i in range(2):
            got((i, 3, start, quarter))
            if q % 2 == 1:
                pass_on((i, 3, start - quarter, 2 * quarter)).start()
        last = (q % 2, 4, start, quarter)
        got(last)
        pass_on(last).start()
    power = near(3, power)
    power = near(4, power)
    power = far_side(3, power)
    power = far_side(4, power)

    width = 256 * xg.shape[0]
    scale = lax.rsqrt(power / width + 1e-05)
    act[...] = jax.nn.gelu(acc[...] * scale).astype(BF16)

    def share(slot):
        weights = jnp.concatenate(
            [
                jnp.concatenate(
                    [down_v[c, inv_ref[groups + c, 2 * slot + b]] for b in range(2)], 1
                )
                for c in range(groups)
            ],
            0,
        )
        return dot(act[...], weights).astype(BF16)

    def s_copy(off):
        k = off + reach - 1
        return remote(
            pair_out.at[k], pair_in.at[k], s_send.at[k], s_recv.at[k], (seq, partner)
        )

    def offer(off):
        pair_out[off + reach - 1] = share(at_y(ny + off) * 2 + 1 - core)
        s_copy(off).start()

    def pair_sum(off):
        mine = share(at_y(ny + off) * 2 + core).astype(F32)
        s_copy(off).wait_recv()
        return mine + pair_in[off + reach - 1].astype(F32)

    def m_copy(i, d, p):
        return remote(
            psum.at[i, d, halves[p]],
            rs.at[i, d, halves[p]],
            r_send.at[i, d - 1, p],
            r_recv.at[i, d - 1, p],
            across(i, d),
        )

    def m_got(i, d, p):
        block = rs.at[i, d, halves[p]]
        remote(block, block, r_send.at[i, d - 1, p], r_recv.at[i, d - 1, p], (seq, ten)).wait_recv()
        return rs[i, d, halves[p]].astype(F32)

    rows_dev = xg.shape[1] // 2

    def rows_of(value, p):
        return value[p * rows_dev : (p + 1) * rows_dev]

    def ship(i, d, p, value):
        psum[i, d, halves[p]] = value.astype(BF16)
        m_copy(i, d, p).start()

    def ship_both(d):
        for i in range(2):
            value = pair_sum(ways[i] * d)
            for p in range(2):
                ship(i, d, p, rows_of(value, p))

    for off in (4, 3, -3):
        offer(off)
    far = pair_sum(4)
    for i in range(2):
        ship(i, 4, i, rows_of(far, i))
    for off in (2, -2):
        offer(off)
    ship_both(3)
    for off in (1, -1, 0):
        offer(off)
    ship_both(1)
    sums = [pair_sum(2), pair_sum(-2)]
    total = pair_sum(0) + xg[ten].astype(F32)
    for p in range(2):
        for i in range(2):
            value = rows_of(sums[i], p) + m_got(i, 3, p)
            if sent(i, 4, p):
                value = value + m_got(i, 4, p)
            ship(i, 2, p, value)
    for p in range(2):
        value = rows_of(total, p)
        for d in (1, 2):
            for i in range(2):
                value = value + m_got(i, d, p)
        out_ref[halves[p], :] = value.astype(BF16)

    for o in range(1, LANES_X):
        on_first(lambda only_write: a_copy(o, only_write).wait_send())
        p_copy(o).wait_send()

        @pl.when(x + o < LANES_X)
        def _():
            for one in b_copies(o):
                one.wait_send()

    for o in range(1, nz):

        @pl.when(z + o < nz)
        def _():
            on_first_group(lambda only_write: z_copy(o, only_write).wait_send())

    own_copy().wait_send()
    for off in range(1 - reach, reach + 1):
        s_copy(off).wait_send()
    for i, d, p in messages:
        m_copy(i, d, p).wait_send()
    for key in crossing:
        ring(key).wait_send()
    for key in inside:
        pass_on(key).wait_send()


def solution(mesh):
    nseq, nten = mesh.shape["seq"], mesh.shape["tensor"]
    nz, ny = nseq // LANES_X, nten // 2
    vmem = pl.BlockSpec(memory_space=pltpu.VMEM)
    hbm = pl.BlockSpec(memory_space=pltpu.HBM)
    dma = pltpu.SemaphoreType.DMA

    def per_device(
        queries,
        keys,
        values,
        beta,
        decay,
        out_gain,
        residual,
        ffn_gain,
        up_blocks,
        up_index,
        down_kept_tiles,
        down_index,
    ):
        tok = queries.shape[0]
        groups, kept = up_index.shape
        return pl.pallas_call(
            functools.partial(main_kernel, nz, ny),
            out_shape=jax.ShapeDtypeStruct((tok, 256), BF16),
            in_specs=[hbm] * 12,
            out_specs=vmem,
            scratch_shapes=[
                pltpu.VMEM((2 * tok, 128), BF16),
                pltpu.VMEM((4 * tok, 128), BF16),
                pltpu.VMEM((4 * tok, 128), BF16),
                pltpu.VMEM((2, 2, tok), F32),
                pltpu.VMEM((2, tok), F32),
                pltpu.VMEM((groups, kept), jnp.int32),
                pltpu.VMEM((groups, kept), jnp.int32),
                pltpu.VMEM((tok, 256), BF16),
                pltpu.VMEM((1, 128), F32),
                pltpu.VMEM((nten, 1, 256), F32),
                dma((10,)),
                pltpu.VMEM((2, tok, 128), F32),
                pltpu.VMEM((2, tok, 128), F32),
                pltpu.VMEM((2 * groups, 128), jnp.int32),
                pltpu.SMEM((2 * groups, 128), jnp.int32),
                pltpu.VMEM((groups, kept + 1, 128, 128), BF16),
                pltpu.VMEM((groups, kept + 1, 128, 128), BF16),
                pltpu.VMEM((LANES_X, 2, 256, 128), BF16),
                pltpu.VMEM((192, 128), BF16),
                pltpu.VMEM((nz, 192, 128), BF16),
                pltpu.VMEM((64, 128), F32),
                pltpu.VMEM((128, 128), F32),
                pltpu.VMEM((2, 128, 128), F32),
                pltpu.VMEM((2, 128, 128), F32),
                pltpu.VMEM((64, 128), BF16),
                pltpu.VMEM((2, 128, 128), BF16),
                pltpu.VMEM((nten, tok, 256), BF16),
                pltpu.VMEM((tok, groups * 128), F32),
                pltpu.VMEM((tok, groups * 128), BF16),
                pltpu.VMEM((ny, tok, 256), BF16),
                pltpu.VMEM((ny, tok, 256), BF16),
                pltpu.VMEM((2, ny // 2 + 1, tok, 256), BF16),
                pltpu.VMEM((2, ny // 2 + 1, tok, 256), BF16),
                dma((3,)),
                dma((LANES_X,)),
                dma((LANES_X,)),
                dma((LANES_X,)),
                dma((LANES_X,)),
                dma((LANES_X,)),
                dma((LANES_X,)),
                dma((nz,)),
                dma((nz,)),
                dma((LANES_X,)),
                dma((LANES_X,)),
                dma((22,)),
                dma((22,)),
                dma((12,)),
                dma((12,)),
                dma((2,)),
                dma((ny,)),
                dma((ny,)),
                dma((2, ny // 2, 2)),
                dma((2, ny // 2, 2)),
            ],
            compiler_params=pltpu.CompilerParams(
                collective_id=0, has_side_effects=True, vmem_limit_bytes=VMEM_LIMIT
            ),
            name="layer",
        )(*(pltpu.with_memory_space_constraint(a, pltpu.HBM) for a in (
            queries.reshape(2 * tok, 128),
            keys.reshape(4 * tok, 128),
            values.reshape(4 * tok, 128),
            beta,
            decay,
            up_index,
            down_index,
            residual,
            out_gain.reshape(1, 128),
            ffn_gain.reshape(nten, 1, 256),
            up_blocks,
            down_kept_tiles,
        )))

    placed = (
        P("seq", "tensor", None),
        P(None, "seq", "tensor", None),
        P(None, "seq", "tensor", None),
        P(None, "tensor", "seq"),
        P("tensor", "seq"),
        P(),
        P("seq", "tensor"),
        P(),
        P("tensor", None, None, None),
        P("tensor", None),
        P("tensor", None, None, None),
        P("tensor", None),
    )
    return jax.shard_map(
        per_device, mesh=mesh, in_specs=placed, out_specs=P("seq", "tensor"), check_vma=False
    )
```

```python
import functools

import jax
import jax.numpy as jnp
from jax import lax
from jax.experimental import pallas as pl
from jax.experimental.pallas import tpu as pltpu
from jax.sharding import PartitionSpec as P

F32 = jnp.float32
BF16 = jnp.bfloat16
HIGHEST = lax.Precision.HIGHEST
LANES_X = 4
VMEM_LIMIT = 24 << 20
MESH = pl.DeviceIdType.MESH


def dot(a, b, contract=(1, 0), precision=None):
    return lax.dot_general(
        a,
        b,
        (((contract[0],), (contract[1],)), ((), ())),
        precision=precision,
        preferred_element_type=F32,
    )


def split(a):
    high = a.astype(BF16)
    return high, (a - high.astype(F32)).astype(BF16)


def mm3(a, b):
    ah, al = split(a)
    bh, bl = split(b)
    left = jnp.concatenate([ah, al], 1)
    right = jnp.concatenate(
        [jnp.concatenate([bh, bl], 1), jnp.concatenate([bh, jnp.zeros_like(bl)], 1)], 0
    )
    both = dot(left, right)
    n = b.shape[1]
    return both[:, :n] + both[:, n:]


def iota(shape, axis):
    return lax.broadcasted_iota(jnp.int32, shape, axis)


def unit_lower_inverse(lowers):
    n = lowers[0].shape[0]
    rows, cols = iota((n, n), 0), iota((n, n), 1)
    eye = (rows == cols).astype(F32)
    base = (rows >> 3) == (cols >> 3)
    n1 = [jnp.where(base, -low, 0.0) for low in lowers]
    n2 = [mm3(a, a) for a in n1]
    n3 = [mm3(a, b) for a, b in zip(n1, n2)]
    n4 = [mm3(a, a) for a in n2]
    y = [eye + a + b + c for a, b, c in zip(n1, n2, n3)]
    x = [a + mm3(a, b) for a, b in zip(y, n4)]
    shift = 3
    while (1 << shift) < n:
        pick = ((rows >> (shift + 1)) == (cols >> (shift + 1))) & ((rows >> shift) != (cols >> shift))
        links = [jnp.where(pick, low, 0.0) for low in lowers]
        right = [mm3(c, a) for c, a in zip(links, x)]
        x = [a - mm3(a, b) for a, b in zip(x, right)]
        shift += 1
    return x


def inverse_table(index, kept):
    lanes = iota((index.shape[0], 128), 1)
    found = jnp.full(lanes.shape, kept, jnp.int32)
    for j in range(kept):
        found = jnp.where(index[:, j : j + 1] == lanes, j, found)
    return found


def local_terms(q_ref, k_ref, v_ref, beta_ref, decay_ref, tw_ref, qt_ref, lo_ref):
    tok = q_ref.shape[0] // 2
    span = 2 * tok
    heads = 2
    half = span // 2

    kv = jnp.concatenate([k_ref[...], v_ref[...]], 1)
    small = jnp.concatenate(
        [decay_ref[...], beta_ref[0], beta_ref[1], jnp.zeros((2, tok), F32)], 0
    )
    s1 = small.astype(BF16)
    rest = small - s1.astype(F32)
    s2 = rest.astype(BF16)
    s3 = (rest - s2.astype(F32)).astype(BF16)
    parts = jnp.concatenate([s1, s2, s3, jnp.zeros_like(s1)], 0)
    m_at, t_at = iota((span, tok), 0), iota((span, tok), 1)
    upto = t_at <= (m_at >> 1)
    first = (t_at == (m_at >> 1)) & ((m_at & 1) == 0)
    second = (t_at == (m_at >> 1)) & ((m_at & 1) == 1)
    upto_tok = iota((tok, tok), 1) <= iota((tok, tok), 0)
    picks = jnp.concatenate([e.astype(BF16) for e in (upto, first, second, upto_tok)], 0)
    cols3 = dot(picks, parts, (1, 1))
    col = cols3[:, 0:8] + cols3[:, 8:16] + cols3[:, 16:24]
    rows3 = dot(parts, picks, (1, 1))
    row = rows3[0:8] + rows3[8:16] + rows3[16:24]
    run_col, one_col, two_col = col[:span], col[span : 2 * span], col[2 * span : 3 * span]
    tok_col = col[3 * span :]
    run_row, one_row, two_row = row[:, :span], row[:, span : 2 * span], row[:, 2 * span : 3 * span]

    rows, cols = iota((span, span), 0), iota((span, span), 1)
    below = cols < rows
    same = rows == cols
    reach = iota((tok, span), 1) <= 2 * iota((tok, span), 0) + 1
    eye = (iota((tok, tok), 0) == iota((tok, tok), 1)).astype(F32)
    row_of = iota((span, 4 * tok), 0)
    place = (row_of & 1) * span + (row_of >> 1) * 2
    column = iota((span, 4 * tok), 1)
    q_place = iota((tok, span), 0) * 2
    q_column = iota((tok, span), 1)

    ks, vs, qs, gammas, lowers, keep = [], [], [], [], [], []
    for h in range(heads):
        pick = (column == place + h).astype(BF16)
        both = dot(pick, kv).astype(BF16)
        k, v = both[:, :128], both[:, 128:]
        gram = dot(k, k, (1, 1))
        diag = jnp.where(same, gram, 0.0)
        rk_col = lax.rsqrt(jnp.sum(diag, 1, keepdims=True) + 1e-06)
        rk_row = lax.rsqrt(jnp.sum(diag, 0, keepdims=True) + 1e-06)
        run_c, run_r = run_col[:, h : h + 1], run_row[h : h + 1, :]
        beta_c = one_col[:, 2 + h : 3 + h] + two_col[:, 4 + h : 5 + h]
        beta_r = one_row[2 + h : 3 + h, :] + two_row[4 + h : 5 + h, :]
        fade = jnp.exp(jnp.where(below, run_c - run_r, 0.0))
        low = jnp.where(below, (beta_c * rk_col) * fade * gram * rk_row, 0.0)
        keep.append((k, v, rk_col, rk_row, run_c, run_r, beta_r, low))
        lowers += [low[:half, :half], low[half:, half:]]

    inverses = unit_lower_inverse(lowers)
    mids = [mm3(keep[h][7][half:, :half], inverses[2 * h]) for h in range(heads)]
    crosses = [mm3(inverses[2 * h + 1], mids[h]) for h in range(heads)]
    left = []
    for h in range(heads):
        k, v, rk_col, rk_row, run_c, run_r, beta_r, low = keep[h]
        a = jnp.concatenate(
            [
                jnp.concatenate([inverses[2 * h], jnp.zeros((half, half), F32)], 1),
                jnp.concatenate([-crosses[h], inverses[2 * h + 1]], 1),
            ],
            0,
        )
        a_val = a * beta_r
        a_key = a_val * (jnp.exp(run_r) * rk_row)
        ah, al = split(a_val)
        u = dot(ah, v) + dot(al, v)
        ah, al = split(a_key)
        w = dot(ah, k) + dot(al, k)
        last = run_c[span - 1 : span, :]
        remain = jnp.exp(last - run_c) * rk_col
        uh, ul = split(u * remain)
        write_t = dot(uh, k, (0, 0)) + dot(ul, k, (0, 0))
        wh, wl = split(w * remain)
        trans = jnp.exp(last) * eye - dot(k, wh, (0, 0)) - dot(k, wl, (0, 0))
        tw_ref[h, 0:64, :] = write_t[:64].astype(BF16)
        tw_ref[h, 64:192, :] = trans.astype(BF16)
        tw_ref[h, 192:256, :] = write_t[64:].astype(BF16)
        left.append((k, u, w, rk_row, run_r, tok_col[:, h : h + 1]))

    def queries():
        q_all = q_ref[...]
        for h in range(heads):
            k, u, w, rk_row, run_r, tok_run = left[h]
            q = dot((q_column == q_place + h).astype(BF16), q_all)
            rq = lax.rsqrt(jnp.sum(q * q, 1, keepdims=True) + 1e-06)
            qk = dot(q.astype(BF16), k, (1, 1))
            mixing = jnp.where(
                reach, jnp.exp(jnp.where(reach, tok_run - run_r, 0.0)) * qk * rq * rk_row, 0.0
            )
            mh, ml = split(mixing)
            bh, bl = split(jnp.concatenate([w, u], 1))
            mixed = dot(mh, bh) + dot(ml, bh) + dot(mh, bl)
            qt_ref[h] = (jnp.exp(tok_run) * rq) * q - mixed[:, :128]
            lo_ref[h] = mixed[:, 128:]

    return queries


def chain_step(state, trans, write):
    n = state.shape[0]
    high, low = split(state)
    both = dot(jnp.concatenate([high, low], 0), trans, (1, 1))
    return both[:n] + both[n:] + write.astype(F32)


def main_kernel(
    nz,
    ny,
    q_in,
    k_in,
    v_in,
    beta_in,
    decay_in,
    up_in,
    down_in,
    res_in,
    og_in,
    fg_in,
    up_hbm,
    down_hbm,
    out_ref,
    q_ref,
    k_ref,
    v_ref,
    beta_ref,
    decay_ref,
    up_ref,
    down_ref,
    res_ref,
    og_ref,
    fg_ref,
    l_sem,
    qt_ref,
    lo_ref,
    table_v,
    inv_ref,
    up_v,
    down_v,
    rx,
    zmsg,
    rz,
    chain,
    since,
    before_t,
    before_w,
    pmsg,
    rp,
    xg,
    acc,
    row_power,
    act,
    pair_out,
    pair_in,
    psum,
    rs,
    wsem,
    a_send,
    a_recv,
    b_send,
    b_recv,
    c_send,
    c_recv,
    z_send,
    z_recv,
    p_send,
    p_recv,
    g_send,
    g_recv,
    f_send,
    f_recv,
    o_sem,
    s_send,
    s_recv,
    r_send,
    r_recv,
):
    seq, ten = lax.axis_index("seq"), lax.axis_index("tensor")
    z, x = seq // LANES_X, lax.rem(seq, LANES_X)
    y, core = ten // 2, lax.rem(ten, 2)
    partner = y * 2 + 1 - core
    head, part = x // 2, lax.rem(x, 2)
    groups = up_hbm.shape[0]
    kept = up_hbm.shape[1]

    def at_x(o):
        return lax.rem(x + o, LANES_X)

    def at_y(o):
        return lax.rem(y + o, ny)

    barrier = pltpu.get_barrier_semaphore()
    peers = [(z * LANES_X + at_x(o), ten) for o in range(1, LANES_X)]
    peers += [(lax.rem(z + o, nz) * LANES_X + x, ten) for o in range(1, nz)]
    peers += [(seq, at_y(o) * 2 + core) for o in (1, 2, ny - 2, ny - 1)]
    peers += [(seq, partner)]
    inputs = (
        (k_in, k_ref),
        (v_in, v_ref),
        (q_in, q_ref),
        (beta_in, beta_ref),
        (decay_in, decay_ref),
        (up_in, up_ref),
        (down_in, down_ref),
        (res_in, res_ref),
        (og_in, og_ref),
        (fg_in, fg_ref),
    )
    loads = [
        pltpu.make_async_copy(here, there, l_sem.at[n]) for n, (here, there) in enumerate(inputs)
    ]
    for load in loads:
        load.start()
    for peer in peers:
        pl.semaphore_signal(barrier, inc=1, device_id=peer, device_id_type=MESH)
    load_up = pltpu.make_async_copy(up_hbm, up_v.at[:, pl.ds(0, kept)], wsem.at[0])
    load_down = pltpu.make_async_copy(down_hbm, down_v.at[:, pl.ds(0, kept)], wsem.at[1])
    load_up.start()
    load_down.start()
    for load in loads:
        load.wait()
    queries = local_terms(q_ref, k_ref, v_ref, beta_ref, decay_ref, rx.at[x], qt_ref, lo_ref)
    pl.semaphore_wait(barrier, len(peers))

    def remote(src, dst, send, recv, peer):
        return pltpu.make_async_remote_copy(
            src_ref=src,
            dst_ref=dst,
            send_sem=send,
            recv_sem=recv,
            device_id=peer,
            device_id_type=MESH,
        )

    w_rows = pl.ds(pl.multiple_of(part * 192, 64), 64)
    my_rows = pl.ds(pl.multiple_of(part * 64, 64), 192)

    def a_copy(o, only_write):
        there = at_x(o)
        h2, p2 = there // 2, lax.rem(there, 2)
        if only_write:
            rows = pl.ds(pl.multiple_of(p2 * 192, 64), 64)
        else:
            rows = pl.ds(pl.multiple_of(p2 * 64, 64), 192)
        return remote(
            rx.at[x, h2, rows],
            rx.at[x, h2, rows],
            a_send.at[o],
            a_recv.at[x],
            (z * LANES_X + there, ten),
        )

    def on_first(act_on):
        @pl.when(seq == 0)
        def _():
            act_on(True)

        @pl.when(seq != 0)
        def _():
            act_on(False)

    def a_wait(i):
        def wait(only_write):
            block = rx.at[i, head, w_rows if only_write else my_rows]
            remote(block, block, a_send.at[0], a_recv.at[i], (seq, ten)).wait_recv()

        @pl.when(i != x)
        def _():
            if i == 0:

                @pl.when(z == 0)
                def _():
                    wait(True)
                    rx[0, head, 64:192] = jnp.zeros((128, 128), BF16)

                @pl.when(z != 0)
                def _():
                    wait(False)
            else:
                wait(False)

    def b_copies(o):
        there = at_x(o)
        h2, p2 = there // 2, lax.rem(there, 2)
        rows = pl.ds(pl.multiple_of((1 - p2) * 192, 64), 64)
        peer = (z * LANES_X + there, ten)
        return (
            remote(
                rx.at[x, h2, rows], rx.at[x, h2, rows], b_send.at[o], b_recv.at[x], peer
            ),
            remote(
                rx.at[x, 1 - h2], rx.at[x, 1 - h2], c_send.at[o], c_recv.at[x], peer
            ),
        )

    for o in (2, 1, 3):
        on_first(lambda only_write: a_copy(o, only_write).start())

    chain[...] = jnp.zeros_like(chain)
    eye = (iota((128, 128), 0) == iota((128, 128), 1)).astype(F32)
    since[...] = eye
    for h in range(2):
        before_t[h] = eye
        before_w[h] = jnp.zeros((128, 128), F32)
    table_v[0:groups] = inverse_table(up_ref[...], kept)
    table_v[groups : 2 * groups] = inverse_table(down_ref[...], kept)
    load_table = pltpu.make_async_copy(table_v, inv_ref, wsem.at[2])
    load_table.start()
    for c in range(groups):
        up_v[c, kept] = jnp.zeros(up_v.shape[2:], BF16)
        down_v[c, kept] = jnp.zeros(up_v.shape[2:], BF16)
    queries()

    def apply(write, trans):
        high, low = split(trans)
        return dot(write, high, (1, 1)) + dot(write, low, (1, 1))

    def extend(trans, earlier):
        high, low = split(trans)
        both = dot(jnp.concatenate([high, low], 0), earlier)
        return both[:128] + both[128:]

    for i in (3, 2, 1):
        a_wait(i)
    ts = [rx[i, head, pl.ds(64, 128)] for i in range(1, LANES_X)]
    ws = [rx[i, head, w_rows] for i in range(1, LANES_X)]
    t32 = dot(ts[2], ts[1])
    w32 = dot(ws[1], ts[2], (1, 1)) + ws[2].astype(F32)
    t321 = extend(t32, ts[0])
    w321 = apply(ws[0], t32) + w32
    a_wait(0)
    zmsg[0:64] = (apply(rx[0, head, w_rows], t321) + w321).astype(BF16)
    zmsg[64:192] = extend(t321, rx[0, head, pl.ds(64, 128)]).astype(BF16)

    def z_copy(o, only_write):
        rows = pl.ds(0, 64 if only_write else 192)
        return remote(
            zmsg.at[rows],
            rz.at[z, rows],
            z_send.at[o],
            z_recv.at[z],
            ((z + o) * LANES_X + x, ten),
        )

    def on_first_group(act_on):
        @pl.when(z == 0)
        def _():
            act_on(True)

        @pl.when(z != 0)
        def _():
            act_on(False)

    for o in sorted(range(1, nz), key=lambda o: -min(o, nz - o)):

        @pl.when(z + o < nz)
        def _():
            on_first_group(lambda only_write: z_copy(o, only_write).start())

    for o in range(1, LANES_X):

        @pl.when(x + o < LANES_X)
        def _():
            for one in b_copies(o):
                one.start()

    def z_wait(i):
        block = rz.at[i, pl.ds(0, 64 if i == 0 else 192)]
        remote(block, block, z_send.at[0], z_recv.at[i], (seq, ten)).wait_recv()

    for i in range(nz - 2, 0, -1):

        @pl.when(i < z)
        def _():
            z_wait(i)
            chain[...] += apply(rz[i, 0:64], since[...])
            since[...] = extend(since[...], rz[i, 64:192])

    if nz > 1:

        @pl.when(z > 0)
        def _():
            z_wait(0)
            chain[...] += apply(rz[0, 0:64], since[...])

    entering = chain[...].astype(BF16)
    pmsg[...] = entering
    p_rows = pl.ds(pl.multiple_of(part * 64, 64), 64)
    rp[head, p_rows] = entering

    def p_copy(o):
        return remote(
            pmsg,
            rp.at[head, p_rows],
            p_send.at[o],
            p_recv.at[x],
            (z * LANES_X + at_x(o), ten),
        )

    for o in (2, 1, 3):
        p_copy(o).start()

    for i in range(LANES_X - 1):

        @pl.when(i < x)
        def _():
            other = pl.ds(pl.multiple_of((1 - part) * 192, 64), 64)
            remote(
                rx.at[i, head, other],
                rx.at[i, head, other],
                b_send.at[0],
                b_recv.at[i],
                (seq, ten),
            ).wait_recv()
            remote(
                rx.at[i, 1 - head], rx.at[i, 1 - head], c_send.at[0], c_recv.at[i], (seq, ten)
            ).wait_recv()
            for h in range(2):
                trans = rx[i, h, 64:192]
                write = jnp.concatenate([rx[i, h, 0:64], rx[i, h, 192:256]], 0)
                if i == 0:
                    before_t[h] = trans.astype(F32)
                    before_w[h] = write.astype(F32)
                else:
                    high, low = split(before_t[h])
                    both = dot(trans, jnp.concatenate([high, low], 1))
                    before_t[h] = both[:, :128] + both[:, 128:]
                    before_w[h] = chain_step(before_w[h], trans, write)

    for o in (1, 3, 2):
        source = at_x(o)
        rows = pl.ds(pl.multiple_of(lax.rem(source, 2) * 64, 64), 64)
        remote(
            rp.at[source // 2, rows],
            rp.at[source // 2, rows],
            p_send.at[o],
            p_recv.at[source],
            (seq, ten),
        ).wait_recv()

    state = [apply(rp[h], before_t[h]) + before_w[h] for h in range(2)]
    gain = og_ref[...]
    pieces = []
    for h in range(2):
        qh, ql = split(qt_ref[h])
        sh, sl = split(state[h])
        head_out = dot(qh, sh, (1, 1)) + dot(ql, sh, (1, 1)) + dot(qh, sl, (1, 1)) + lo_ref[h]
        power = jnp.mean(head_out * head_out, -1, keepdims=True)
        normed = head_out * lax.rsqrt(power + 1e-05) * gain
        pieces.append(res_ref[:, 128 * h : 128 * h + 128].astype(F32) + normed)
    xg[ten] = jnp.concatenate(pieces, 1).astype(BF16)

    reach = ny // 2
    ways = (1, -1)
    halves = [pl.ds(0, xg.shape[1] // 2), pl.ds(xg.shape[1] // 2, xg.shape[1] // 2)]

    def sent(i, d, part_at):
        return d < reach or part_at == i

    messages = [
        (i, d, p)
        for d in range(1, reach + 1)
        for p in range(2)
        for i in range(2)
        if sent(i, d, p)
    ]

    hop = (0, 1, 2, 1, 2)

    def across(i, d):
        return (seq, at_y(ny + ways[i] * hop[d]) * 2 + core)

    rows_all = xg.shape[1]
    quarter = rows_all // 4
    quarters = [(i, q) for q in range(4) for i in range(2)]
    crossing = [(i, 2, q * quarter, quarter) for i, q in quarters]
    crossing += [(i, 1, 0, rows_all) for i in range(2)]
    crossing += [(i, 3, q * quarter, quarter) for i, q in quarters]
    crossing += [(i, 4, q * quarter, quarter) for i, q in quarters if q % 2 == i]
    inside = [(i, d, 0, rows_all) for d in (1, 2) for i in range(2)]
    inside += [(i, 3, s * 2 * quarter, 2 * quarter) for s in range(2) for i in range(2)]
    inside += [key for key in crossing if key[1] == 4]

    def block_of(i, d, side, start, count):
        slot = at_y(ny - ways[i] * d) * 2 + (core if side == 0 else 1 - core)
        return xg.at[slot, pl.ds(start, count)]

    def ring(key):
        i, d, start, count = key
        n = crossing.index(key)
        block = block_of(i, 0 if d <= 2 else 2, 0, start, count)
        return remote(block, block, g_send.at[n], g_recv.at[n], across(i, d))

    def got(key):
        i, d, start, count = key
        n = crossing.index(key)
        block = block_of(i, d, 0, start, count)
        remote(block, block, g_send.at[n], g_recv.at[n], (seq, ten)).wait_recv()

    def pass_on(key):
        i, d, start, count = key
        n = inside.index(key)
        block = block_of(i, d, 0, start, count)
        return remote(block, block, f_send.at[n], f_recv.at[n], (seq, partner))

    def passed(key):
        i, d, start, count = key
        n = inside.index(key)
        block = block_of(i, d, 1, start, count)
        remote(block, block, f_send.at[n], f_recv.at[n], (seq, ten)).wait_recv()

    def own_copy():
        return remote(xg.at[ten], xg.at[ten], o_sem.at[0], o_sem.at[1], (seq, partner))

    for level in (2, 1):
        for key in crossing:
            if key[1] == level:
                ring(key).start()
    own_copy().start()

    load_up.wait()
    load_down.wait()
    load_table.wait()

    def absorb(slot, first=False):
        wide = xg[slot].astype(F32)
        squares = jnp.sum(wide * wide, -1, keepdims=True)
        scaled = (wide * fg_ref[slot]).astype(BF16)
        weights = jnp.concatenate(
            [
                jnp.concatenate(
                    [up_v[c, inv_ref[c, 2 * slot + b]] for c in range(groups)], 1
                )
                for b in range(2)
            ],
            0,
        )
        term = dot(scaled, weights)
        if first:
            acc[...] = term
            row_power[...] = squares
        else:
            acc[...] += term
            row_power[...] += squares

    sources = [(0, 2), (1, 2), (0, 1), (1, 1), (0, 3), (1, 3), (0, 4)]

    def source_y(source):
        return at_y(ny - ways[source[0]] * source[1])

    def keys_of(table, source):
        i, d = source
        return [key for key in table if key[1] == d and (d == 4 or key[0] == i)]

    def handle(source):
        d = source[1]
        for key in keys_of(crossing, source):
            i, _, start, count = key
            got(key)
            if d == 2:
                if (start // quarter) % 2 == i:
                    ring((i, 4, start, count)).start()
                ring((i, 3, start, count)).start()
            elif d == 3 and (start // quarter) % 2 == 1:
                pass_on((i, 3, start - quarter, 2 * quarter)).start()
            elif d == 4:
                pass_on(key).start()
        if d <= 2:
            pass_on(keys_of(inside, source)[0]).start()

    def finish(source):
        for key in keys_of(inside, source):
            passed(key)

    def early(source, act_on):
        @pl.when(source_y(source) != 0)
        def _():
            act_on(source)

    def late(source, act_on):
        @pl.when(source_y(source) == 0)
        def _():
            act_on(source)

    def near(source):
        absorb(source_y(source) * 2 + core)

    def far(source):
        finish(source)
        absorb(source_y(source) * 2 + 1 - core)

    absorb(ten, True)
    for group in (sources[:4], sources[4:]):
        for source in group:
            early(source, handle)
        for source in group:
            early(source, near)
        for source in group:
            early(source, far)
    remote(xg.at[partner], xg.at[partner], o_sem.at[0], o_sem.at[1], (seq, ten)).wait_recv()
    absorb(partner)
    for source in sources:
        late(source, handle)

    @pl.when(y != 0)
    def _():
        absorb(core)

    for source in sources:
        late(source, finish)

    @pl.when(y != 0)
    def _():
        absorb(1 - core)

    width = 256 * xg.shape[0]
    scale = lax.rsqrt(row_power[...] / width + 1e-05)
    act[...] = jax.nn.gelu(acc[...] * scale).astype(BF16)

    def share(slot):
        weights = jnp.concatenate(
            [
                jnp.concatenate(
                    [down_v[c, inv_ref[groups + c, 2 * slot + b]] for b in range(2)], 1
                )
                for c in range(groups)
            ],
            0,
        )
        return dot(act[...], weights).astype(BF16)

    def s_copy(off):
        k = off + reach - 1
        return remote(
            pair_out.at[k], pair_in.at[k], s_send.at[k], s_recv.at[k], (seq, partner)
        )

    def offer(off):
        pair_out[off + reach - 1] = share(at_y(ny + off) * 2 + 1 - core)
        s_copy(off).start()

    def pair_sum(off):
        mine = share(at_y(ny + off) * 2 + core).astype(F32)
        s_copy(off).wait_recv()
        return mine + pair_in[off + reach - 1].astype(F32)

    def m_copy(i, d, p):
        return remote(
            psum.at[i, d, halves[p]],
            rs.at[i, d, halves[p]],
            r_send.at[i, d - 1, p],
            r_recv.at[i, d - 1, p],
            across(i, d),
        )

    def m_got(i, d, p):
        block = rs.at[i, d, halves[p]]
        remote(block, block, r_send.at[i, d - 1, p], r_recv.at[i, d - 1, p], (seq, ten)).wait_recv()
        return rs[i, d, halves[p]].astype(F32)

    rows_dev = xg.shape[1] // 2

    def rows_of(value, p):
        return value[p * rows_dev : (p + 1) * rows_dev]

    def ship(i, d, p, value):
        psum[i, d, halves[p]] = value.astype(BF16)
        m_copy(i, d, p).start()

    def ship_both(d):
        for i in range(2):
            value = pair_sum(ways[i] * d)
            for p in range(2):
                ship(i, d, p, rows_of(value, p))

    for off in (4, 3, -3):
        offer(off)
    far = pair_sum(4)
    for i in range(2):
        ship(i, 4, i, rows_of(far, i))
    for off in (2, -2):
        offer(off)
    ship_both(3)
    for off in (1, -1, 0):
        offer(off)
    ship_both(1)
    sums = [pair_sum(2), pair_sum(-2)]
    total = pair_sum(0) + xg[ten].astype(F32)
    for p in range(2):
        for i in range(2):
            value = rows_of(sums[i], p) + m_got(i, 3, p)
            if sent(i, 4, p):
                value = value + m_got(i, 4, p)
            ship(i, 2, p, value)
    for p in range(2):
        value = rows_of(total, p)
        for d in (1, 2):
            for i in range(2):
                value = value + m_got(i, d, p)
        out_ref[halves[p], :] = value.astype(BF16)

    for o in range(1, LANES_X):
        on_first(lambda only_write: a_copy(o, only_write).wait_send())
        p_copy(o).wait_send()

        @pl.when(x + o < LANES_X)
        def _():
            for one in b_copies(o):
                one.wait_send()

    for o in range(1, nz):

        @pl.when(z + o < nz)
        def _():
            on_first_group(lambda only_write: z_copy(o, only_write).wait_send())

    own_copy().wait_send()
    for off in range(1 - reach, reach + 1):
        s_copy(off).wait_send()
    for i, d, p in messages:
        m_copy(i, d, p).wait_send()
    for key in crossing:
        ring(key).wait_send()
    for key in inside:
        pass_on(key).wait_send()


def solution(mesh):
    nseq, nten = mesh.shape["seq"], mesh.shape["tensor"]
    nz, ny = nseq // LANES_X, nten // 2
    vmem = pl.BlockSpec(memory_space=pltpu.VMEM)
    hbm = pl.BlockSpec(memory_space=pltpu.HBM)
    dma = pltpu.SemaphoreType.DMA

    def per_device(
        queries,
        keys,
        values,
        beta,
        decay,
        out_gain,
        residual,
        ffn_gain,
        up_blocks,
        up_index,
        down_kept_tiles,
        down_index,
    ):
        tok = queries.shape[0]
        groups, kept = up_index.shape
        return pl.pallas_call(
            functools.partial(main_kernel, nz, ny),
            out_shape=jax.ShapeDtypeStruct((tok, 256), BF16),
            in_specs=[hbm] * 12,
            out_specs=vmem,
            scratch_shapes=[
                pltpu.VMEM((2 * tok, 128), BF16),
                pltpu.VMEM((4 * tok, 128), BF16),
                pltpu.VMEM((4 * tok, 128), BF16),
                pltpu.VMEM((2, 2, tok), F32),
                pltpu.VMEM((2, tok), F32),
                pltpu.VMEM((groups, kept), jnp.int32),
                pltpu.VMEM((groups, kept), jnp.int32),
                pltpu.VMEM((tok, 256), BF16),
                pltpu.VMEM((1, 128), F32),
                pltpu.VMEM((nten, 1, 256), F32),
                dma((10,)),
                pltpu.VMEM((2, tok, 128), F32),
                pltpu.VMEM((2, tok, 128), F32),
                pltpu.VMEM((2 * groups, 128), jnp.int32),
                pltpu.SMEM((2 * groups, 128), jnp.int32),
                pltpu.VMEM((groups, kept + 1, 128, 128), BF16),
                pltpu.VMEM((groups, kept + 1, 128, 128), BF16),
                pltpu.VMEM((LANES_X, 2, 256, 128), BF16),
                pltpu.VMEM((192, 128), BF16),
                pltpu.VMEM((nz, 192, 128), BF16),
                pltpu.VMEM((64, 128), F32),
                pltpu.VMEM((128, 128), F32),
                pltpu.VMEM((2, 128, 128), F32),
                pltpu.VMEM((2, 128, 128), F32),
                pltpu.VMEM((64, 128), BF16),
                pltpu.VMEM((2, 128, 128), BF16),
                pltpu.VMEM((nten, tok, 256), BF16),
                pltpu.VMEM((tok, groups * 128), F32),
                pltpu.VMEM((tok, 1), F32),
                pltpu.VMEM((tok, groups * 128), BF16),
                pltpu.VMEM((ny, tok, 256), BF16),
                pltpu.VMEM((ny, tok, 256), BF16),
                pltpu.VMEM((2, ny // 2 + 1, tok, 256), BF16),
                pltpu.VMEM((2, ny // 2 + 1, tok, 256), BF16),
                dma((3,)),
                dma((LANES_X,)),
                dma((LANES_X,)),
                dma((LANES_X,)),
                dma((LANES_X,)),
                dma((LANES_X,)),
                dma((LANES_X,)),
                dma((nz,)),
                dma((nz,)),
                dma((LANES_X,)),
                dma((LANES_X,)),
                dma((22,)),
                dma((22,)),
                dma((12,)),
                dma((12,)),
                dma((2,)),
                dma((ny,)),
                dma((ny,)),
                dma((2, ny // 2, 2)),
                dma((2, ny // 2, 2)),
            ],
            compiler_params=pltpu.CompilerParams(
                collective_id=0, has_side_effects=True, vmem_limit_bytes=VMEM_LIMIT
            ),
            name="layer",
        )(*(pltpu.with_memory_space_constraint(a, pltpu.HBM) for a in (
            queries.reshape(2 * tok, 128),
            keys.reshape(4 * tok, 128),
            values.reshape(4 * tok, 128),
            beta,
            decay,
            up_index,
            down_index,
            residual,
            out_gain.reshape(1, 128),
            ffn_gain.reshape(nten, 1, 256),
            up_blocks,
            down_kept_tiles,
        )))

    placed = (
        P("seq", "tensor", None),
        P(None, "seq", "tensor", None),
        P(None, "seq", "tensor", None),
        P(None, "tensor", "seq"),
        P("tensor", "seq"),
        P(),
        P("seq", "tensor"),
        P(),
        P("tensor", None, None, None),
        P("tensor", None),
        P("tensor", None, None, None),
        P("tensor", None),
    )
    return jax.shard_map(
        per_device, mesh=mesh, in_specs=placed, out_specs=P("seq", "tensor"), check_vma=False
    )
```

```python
import functools

import jax
import jax.numpy as jnp
from jax import lax
from jax.experimental import pallas as pl
from jax.experimental.pallas import tpu as pltpu
from jax.sharding import PartitionSpec as P

F32 = jnp.float32
BF16 = jnp.bfloat16
HIGHEST = lax.Precision.HIGHEST
LANES_X = 4
VMEM_LIMIT = 24 << 20
MESH = pl.DeviceIdType.MESH


def dot(a, b, contract=(1, 0), precision=None):
    return lax.dot_general(
        a,
        b,
        (((contract[0],), (contract[1],)), ((), ())),
        precision=precision,
        preferred_element_type=F32,
    )


def split(a):
    high = a.astype(BF16)
    return high, (a - high.astype(F32)).astype(BF16)


def mm3(a, b):
    ah, al = split(a)
    bh, bl = split(b)
    left = jnp.concatenate([ah, al], 1)
    right = jnp.concatenate(
        [jnp.concatenate([bh, bl], 1), jnp.concatenate([bh, jnp.zeros_like(bl)], 1)], 0
    )
    both = dot(left, right)
    n = b.shape[1]
    return both[:, :n] + both[:, n:]


def iota(shape, axis):
    return lax.broadcasted_iota(jnp.int32, shape, axis)


def unit_lower_inverse(lowers):
    n = lowers[0].shape[0]
    rows, cols = iota((n, n), 0), iota((n, n), 1)
    eye = (rows == cols).astype(F32)
    base = (rows >> 3) == (cols >> 3)
    n1 = [jnp.where(base, -low, 0.0) for low in lowers]
    n2 = [mm3(a, a) for a in n1]
    n3 = [mm3(a, b) for a, b in zip(n1, n2)]
    n4 = [mm3(a, a) for a in n2]
    y = [eye + a + b + c for a, b, c in zip(n1, n2, n3)]
    x = [a + mm3(a, b) for a, b in zip(y, n4)]
    shift = 3
    while (1 << shift) < n:
        pick = ((rows >> (shift + 1)) == (cols >> (shift + 1))) & ((rows >> shift) != (cols >> shift))
        links = [jnp.where(pick, low, 0.0) for low in lowers]
        right = [mm3(c, a) for c, a in zip(links, x)]
        x = [a - mm3(a, b) for a, b in zip(x, right)]
        shift += 1
    return x


def inverse_table(index, kept):
    lanes = iota((index.shape[0], 128), 1)
    found = jnp.full(lanes.shape, kept, jnp.int32)
    for j in range(kept):
        found = jnp.where(index[:, j : j + 1] == lanes, j, found)
    return found


def local_terms(q_ref, k_ref, v_ref, beta_ref, decay_ref, tw_ref, qt_ref, lo_ref):
    tok = q_ref.shape[0] // 2
    span = 2 * tok
    heads = 2
    half = span // 2

    kv = jnp.concatenate([k_ref[...], v_ref[...]], 1)
    small = jnp.concatenate(
        [decay_ref[...], beta_ref[0], beta_ref[1], jnp.zeros((2, tok), F32)], 0
    )
    s1 = small.astype(BF16)
    rest = small - s1.astype(F32)
    s2 = rest.astype(BF16)
    s3 = (rest - s2.astype(F32)).astype(BF16)
    parts = jnp.concatenate([s1, s2, s3, jnp.zeros_like(s1)], 0)
    m_at, t_at = iota((span, tok), 0), iota((span, tok), 1)
    upto = t_at <= (m_at >> 1)
    first = (t_at == (m_at >> 1)) & ((m_at & 1) == 0)
    second = (t_at == (m_at >> 1)) & ((m_at & 1) == 1)
    upto_tok = iota((tok, tok), 1) <= iota((tok, tok), 0)
    picks = jnp.concatenate([e.astype(BF16) for e in (upto, first, second, upto_tok)], 0)
    cols3 = dot(picks, parts, (1, 1))
    col = cols3[:, 0:8] + cols3[:, 8:16] + cols3[:, 16:24]
    rows3 = dot(parts, picks, (1, 1))
    row = rows3[0:8] + rows3[8:16] + rows3[16:24]
    run_col, one_col, two_col = col[:span], col[span : 2 * span], col[2 * span : 3 * span]
    tok_col = col[3 * span :]
    run_row, one_row, two_row = row[:, :span], row[:, span : 2 * span], row[:, 2 * span : 3 * span]

    rows, cols = iota((span, span), 0), iota((span, span), 1)
    below = cols < rows
    same = rows == cols
    reach = iota((tok, span), 1) <= 2 * iota((tok, span), 0) + 1
    eye = (iota((tok, tok), 0) == iota((tok, tok), 1)).astype(F32)
    row_of = iota((span, 4 * tok), 0)
    place = (row_of & 1) * span + (row_of >> 1) * 2
    column = iota((span, 4 * tok), 1)
    q_place = iota((tok, span), 0) * 2
    q_column = iota((tok, span), 1)

    ks, vs, qs, gammas, lowers, keep = [], [], [], [], [], []
    for h in range(heads):
        pick = (column == place + h).astype(BF16)
        both = dot(pick, kv).astype(BF16)
        k, v = both[:, :128], both[:, 128:]
        gram = dot(k, k, (1, 1))
        diag = jnp.where(same, gram, 0.0)
        rk_col = lax.rsqrt(jnp.sum(diag, 1, keepdims=True) + 1e-06)
        rk_row = lax.rsqrt(jnp.sum(diag, 0, keepdims=True) + 1e-06)
        run_c, run_r = run_col[:, h : h + 1], run_row[h : h + 1, :]
        beta_c = one_col[:, 2 + h : 3 + h] + two_col[:, 4 + h : 5 + h]
        beta_r = one_row[2 + h : 3 + h, :] + two_row[4 + h : 5 + h, :]
        fade = jnp.exp(jnp.where(below, run_c - run_r, 0.0))
        low = jnp.where(below, (beta_c * rk_col) * fade * gram * rk_row, 0.0)
        keep.append((k, v, rk_col, rk_row, run_c, run_r, beta_r, low))
        lowers += [low[:half, :half], low[half:, half:]]

    inverses = unit_lower_inverse(lowers)
    mids = [mm3(keep[h][7][half:, :half], inverses[2 * h]) for h in range(heads)]
    crosses = [mm3(inverses[2 * h + 1], mids[h]) for h in range(heads)]
    left = []
    for h in range(heads):
        k, v, rk_col, rk_row, run_c, run_r, beta_r, low = keep[h]
        a = jnp.concatenate(
            [
                jnp.concatenate([inverses[2 * h], jnp.zeros((half, half), F32)], 1),
                jnp.concatenate([-crosses[h], inverses[2 * h + 1]], 1),
            ],
            0,
        )
        a_val = a * beta_r
        a_key = a_val * (jnp.exp(run_r) * rk_row)
        ah, al = split(a_val)
        u = dot(ah, v) + dot(al, v)
        ah, al = split(a_key)
        w = dot(ah, k) + dot(al, k)
        last = run_c[span - 1 : span, :]
        remain = jnp.exp(last - run_c) * rk_col
        uh, ul = split(u * remain)
        write_t = dot(uh, k, (0, 0)) + dot(ul, k, (0, 0))
        wh, wl = split(w * remain)
        trans = jnp.exp(last) * eye - dot(k, wh, (0, 0)) - dot(k, wl, (0, 0))
        tw_ref[h, 0:64, :] = write_t[:64].astype(BF16)
        tw_ref[h, 64:192, :] = trans.astype(BF16)
        tw_ref[h, 192:256, :] = write_t[64:].astype(BF16)
        left.append((k, u, w, rk_row, run_r, tok_col[:, h : h + 1]))

    def queries():
        q_all = q_ref[...]
        for h in range(heads):
            k, u, w, rk_row, run_r, tok_run = left[h]
            q = dot((q_column == q_place + h).astype(BF16), q_all)
            rq = lax.rsqrt(jnp.sum(q * q, 1, keepdims=True) + 1e-06)
            qk = dot(q.astype(BF16), k, (1, 1))
            mixing = jnp.where(
                reach, jnp.exp(jnp.where(reach, tok_run - run_r, 0.0)) * qk * rq * rk_row, 0.0
            )
            mh, ml = split(mixing)
            bh, bl = split(jnp.concatenate([w, u], 1))
            mixed = dot(mh, bh) + dot(ml, bh) + dot(mh, bl)
            qt_ref[h] = (jnp.exp(tok_run) * rq) * q - mixed[:, :128]
            lo_ref[h] = mixed[:, 128:]

    return queries


def chain_step(state, trans, write):
    n = state.shape[0]
    high, low = split(state)
    both = dot(jnp.concatenate([high, low], 0), trans, (1, 1))
    return both[:n] + both[n:] + write.astype(F32)


def main_kernel(
    nz,
    ny,
    q_in,
    k_in,
    v_in,
    beta_in,
    decay_in,
    up_in,
    down_in,
    res_in,
    og_in,
    fg_in,
    up_hbm,
    down_hbm,
    out_ref,
    q_ref,
    k_ref,
    v_ref,
    beta_ref,
    decay_ref,
    up_ref,
    down_ref,
    res_ref,
    og_ref,
    fg_ref,
    l_sem,
    qt_ref,
    lo_ref,
    table_v,
    inv_ref,
    up_v,
    down_v,
    rx,
    zmsg,
    rz,
    chain,
    since,
    before_t,
    before_w,
    pmsg,
    rp,
    xg,
    acc,
    row_power,
    act,
    pair_out,
    pair_in,
    psum,
    rs,
    wsem,
    a_send,
    a_recv,
    b_send,
    b_recv,
    c_send,
    c_recv,
    z_send,
    z_recv,
    p_send,
    p_recv,
    g_send,
    g_recv,
    f_send,
    f_recv,
    o_sem,
    s_send,
    s_recv,
    r_send,
    r_recv,
):
    seq, ten = lax.axis_index("seq"), lax.axis_index("tensor")
    z, x = seq // LANES_X, lax.rem(seq, LANES_X)
    y, core = ten // 2, lax.rem(ten, 2)
    partner = y * 2 + 1 - core
    head, part = x // 2, lax.rem(x, 2)
    groups = up_hbm.shape[0]
    kept = up_hbm.shape[1]

    def at_x(o):
        return lax.rem(x + o, LANES_X)

    def at_y(o):
        return lax.rem(y + o, ny)

    barrier = pltpu.get_barrier_semaphore()
    peers = [(z * LANES_X + at_x(o), ten) for o in range(1, LANES_X)]
    peers += [(lax.rem(z + o, nz) * LANES_X + x, ten) for o in range(1, nz)]
    peers += [(seq, at_y(o) * 2 + core) for o in (1, 2, ny - 2, ny - 1)]
    peers += [(seq, partner)]
    inputs = (
        (k_in, k_ref),
        (v_in, v_ref),
        (q_in, q_ref),
        (beta_in, beta_ref),
        (decay_in, decay_ref),
        (up_in, up_ref),
        (down_in, down_ref),
        (res_in, res_ref),
        (og_in, og_ref),
        (fg_in, fg_ref),
    )
    loads = [
        pltpu.make_async_copy(here, there, l_sem.at[n]) for n, (here, there) in enumerate(inputs)
    ]
    for load in loads:
        load.start()
    for peer in peers:
        pl.semaphore_signal(barrier, inc=1, device_id=peer, device_id_type=MESH)
    load_up = pltpu.make_async_copy(up_hbm, up_v.at[:, pl.ds(0, kept)], wsem.at[0])
    load_down = pltpu.make_async_copy(down_hbm, down_v.at[:, pl.ds(0, kept)], wsem.at[1])
    load_up.start()
    load_down.start()
    for load in loads:
        load.wait()
    queries = local_terms(q_ref, k_ref, v_ref, beta_ref, decay_ref, rx.at[x], qt_ref, lo_ref)
    pl.semaphore_wait(barrier, len(peers))

    def remote(src, dst, send, recv, peer):
        return pltpu.make_async_remote_copy(
            src_ref=src,
            dst_ref=dst,
            send_sem=send,
            recv_sem=recv,
            device_id=peer,
            device_id_type=MESH,
        )

    w_rows = pl.ds(pl.multiple_of(part * 192, 64), 64)
    my_rows = pl.ds(pl.multiple_of(part * 64, 64), 192)

    def a_copy(o, only_write):
        there = at_x(o)
        h2, p2 = there // 2, lax.rem(there, 2)
        if only_write:
            rows = pl.ds(pl.multiple_of(p2 * 192, 64), 64)
        else:
            rows = pl.ds(pl.multiple_of(p2 * 64, 64), 192)
        return remote(
            rx.at[x, h2, rows],
            rx.at[x, h2, rows],
            a_send.at[o],
            a_recv.at[x],
            (z * LANES_X + there, ten),
        )

    def on_first(act_on):
        @pl.when(seq == 0)
        def _():
            act_on(True)

        @pl.when(seq != 0)
        def _():
            act_on(False)

    def a_wait(i):
        def wait(only_write):
            block = rx.at[i, head, w_rows if only_write else my_rows]
            remote(block, block, a_send.at[0], a_recv.at[i], (seq, ten)).wait_recv()

        @pl.when(i != x)
        def _():
            if i == 0:

                @pl.when(z == 0)
                def _():
                    wait(True)
                    rx[0, head, 64:192] = jnp.zeros((128, 128), BF16)

                @pl.when(z != 0)
                def _():
                    wait(False)
            else:
                wait(False)

    def b_copies(o):
        there = at_x(o)
        h2, p2 = there // 2, lax.rem(there, 2)
        rows = pl.ds(pl.multiple_of((1 - p2) * 192, 64), 64)
        peer = (z * LANES_X + there, ten)
        return (
            remote(
                rx.at[x, h2, rows], rx.at[x, h2, rows], b_send.at[o], b_recv.at[x], peer
            ),
            remote(
                rx.at[x, 1 - h2], rx.at[x, 1 - h2], c_send.at[o], c_recv.at[x], peer
            ),
        )

    for o in (2, 1, 3):
        on_first(lambda only_write: a_copy(o, only_write).start())

    chain[...] = jnp.zeros_like(chain)
    eye = (iota((128, 128), 0) == iota((128, 128), 1)).astype(F32)
    since[...] = eye
    for h in range(2):
        before_t[h] = eye
        before_w[h] = jnp.zeros((128, 128), F32)
    table_v[0:groups] = inverse_table(up_ref[...], kept)
    table_v[groups : 2 * groups] = inverse_table(down_ref[...], kept)
    load_table = pltpu.make_async_copy(table_v, inv_ref, wsem.at[2])
    load_table.start()
    for c in range(groups):
        up_v[c, kept] = jnp.zeros(up_v.shape[2:], BF16)
        down_v[c, kept] = jnp.zeros(up_v.shape[2:], BF16)
    queries()

    def apply(write, trans):
        high, low = split(trans)
        return dot(write, high, (1, 1)) + dot(write, low, (1, 1))

    def extend(trans, earlier):
        high, low = split(trans)
        both = dot(jnp.concatenate([high, low], 0), earlier)
        return both[:128] + both[128:]

    for i in (3, 2, 1):
        a_wait(i)
    ts = [rx[i, head, pl.ds(64, 128)] for i in range(1, LANES_X)]
    ws = [rx[i, head, w_rows] for i in range(1, LANES_X)]
    t32 = dot(ts[2], ts[1])
    w32 = dot(ws[1], ts[2], (1, 1)) + ws[2].astype(F32)
    t321 = extend(t32, ts[0])
    w321 = apply(ws[0], t32) + w32
    a_wait(0)
    zmsg[0:64] = (apply(rx[0, head, w_rows], t321) + w321).astype(BF16)
    zmsg[64:192] = extend(t321, rx[0, head, pl.ds(64, 128)]).astype(BF16)

    def z_copy(o, only_write):
        rows = pl.ds(0, 64 if only_write else 192)
        return remote(
            zmsg.at[rows],
            rz.at[z, rows],
            z_send.at[o],
            z_recv.at[z],
            ((z + o) * LANES_X + x, ten),
        )

    def on_first_group(act_on):
        @pl.when(z == 0)
        def _():
            act_on(True)

        @pl.when(z != 0)
        def _():
            act_on(False)

    for o in sorted(range(1, nz), key=lambda o: -min(o, nz - o)):

        @pl.when(z + o < nz)
        def _():
            on_first_group(lambda only_write: z_copy(o, only_write).start())

    for o in range(1, LANES_X):

        @pl.when(x + o < LANES_X)
        def _():
            for one in b_copies(o):
                one.start()

    def z_wait(i):
        block = rz.at[i, pl.ds(0, 64 if i == 0 else 192)]
        remote(block, block, z_send.at[0], z_recv.at[i], (seq, ten)).wait_recv()

    for i in range(nz - 2, 0, -1):

        @pl.when(i < z)
        def _():
            z_wait(i)
            chain[...] += apply(rz[i, 0:64], since[...])
            since[...] = extend(since[...], rz[i, 64:192])

    if nz > 1:

        @pl.when(z > 0)
        def _():
            z_wait(0)
            chain[...] += apply(rz[0, 0:64], since[...])

    entering = chain[...].astype(BF16)
    pmsg[...] = entering
    p_rows = pl.ds(pl.multiple_of(part * 64, 64), 64)
    rp[head, p_rows] = entering

    def p_copy(o):
        return remote(
            pmsg,
            rp.at[head, p_rows],
            p_send.at[o],
            p_recv.at[x],
            (z * LANES_X + at_x(o), ten),
        )

    for o in (2, 1, 3):
        p_copy(o).start()

    for i in range(LANES_X - 1):

        @pl.when(i < x)
        def _():
            other = pl.ds(pl.multiple_of((1 - part) * 192, 64), 64)
            remote(
                rx.at[i, head, other],
                rx.at[i, head, other],
                b_send.at[0],
                b_recv.at[i],
                (seq, ten),
            ).wait_recv()
            remote(
                rx.at[i, 1 - head], rx.at[i, 1 - head], c_send.at[0], c_recv.at[i], (seq, ten)
            ).wait_recv()
            for h in range(2):
                trans = rx[i, h, 64:192]
                write = jnp.concatenate([rx[i, h, 0:64], rx[i, h, 192:256]], 0)
                if i == 0:
                    before_t[h] = trans.astype(F32)
                    before_w[h] = write.astype(F32)
                else:
                    high, low = split(before_t[h])
                    both = dot(trans, jnp.concatenate([high, low], 1))
                    before_t[h] = both[:, :128] + both[:, 128:]
                    before_w[h] = chain_step(before_w[h], trans, write)

    for o in (1, 3, 2):
        source = at_x(o)
        rows = pl.ds(pl.multiple_of(lax.rem(source, 2) * 64, 64), 64)
        remote(
            rp.at[source // 2, rows],
            rp.at[source // 2, rows],
            p_send.at[o],
            p_recv.at[source],
            (seq, ten),
        ).wait_recv()

    state = [apply(rp[h], before_t[h]) + before_w[h] for h in range(2)]
    gain = og_ref[...]
    pieces = []
    for h in range(2):
        qh, ql = split(qt_ref[h])
        sh, sl = split(state[h])
        head_out = dot(qh, sh, (1, 1)) + dot(ql, sh, (1, 1)) + dot(qh, sl, (1, 1)) + lo_ref[h]
        power = jnp.mean(head_out * head_out, -1, keepdims=True)
        normed = head_out * lax.rsqrt(power + 1e-05) * gain
        pieces.append(res_ref[:, 128 * h : 128 * h + 128].astype(F32) + normed)
    xg[ten] = jnp.concatenate(pieces, 1).astype(BF16)

    reach = ny // 2
    ways = (1, -1)
    halves = [pl.ds(0, xg.shape[1] // 2), pl.ds(xg.shape[1] // 2, xg.shape[1] // 2)]

    def sent(i, d, part_at):
        return d < reach or part_at == i

    messages = [
        (i, d, p)
        for d in range(1, reach + 1)
        for p in range(2)
        for i in range(2)
        if sent(i, d, p)
    ]

    hop = (0, 1, 2, 1, 2)

    def across(i, d):
        return (seq, at_y(ny + ways[i] * hop[d]) * 2 + core)

    rows_all = xg.shape[1]
    quarter = rows_all // 4
    quarters = [(i, q) for q in range(4) for i in range(2)]
    crossing = [(i, 2, q * quarter, quarter) for i, q in quarters]
    crossing += [(i, 1, 0, rows_all) for i in range(2)]
    crossing += [(i, 3, q * quarter, quarter) for i, q in quarters]
    crossing += [(i, 4, q * quarter, quarter) for i, q in quarters if q % 2 == i]
    inside = [(i, d, 0, rows_all) for d in (1, 2) for i in range(2)]
    inside += [(i, 3, s * 2 * quarter, 2 * quarter) for s in range(2) for i in range(2)]
    inside += [key for key in crossing if key[1] == 4]

    def block_of(i, d, side, start, count):
        slot = at_y(ny - ways[i] * d) * 2 + (core if side == 0 else 1 - core)
        return xg.at[slot, pl.ds(start, count)]

    def ring(key):
        i, d, start, count = key
        n = crossing.index(key)
        block = block_of(i, 0 if d <= 2 else 2, 0, start, count)
        return remote(block, block, g_send.at[n], g_recv.at[n], across(i, d))

    def got(key):
        i, d, start, count = key
        n = crossing.index(key)
        block = block_of(i, d, 0, start, count)
        remote(block, block, g_send.at[n], g_recv.at[n], (seq, ten)).wait_recv()

    def pass_on(key):
        i, d, start, count = key
        n = inside.index(key)
        block = block_of(i, d, 0, start, count)
        return remote(block, block, f_send.at[n], f_recv.at[n], (seq, partner))

    def passed(key):
        i, d, start, count = key
        n = inside.index(key)
        block = block_of(i, d, 1, start, count)
        remote(block, block, f_send.at[n], f_recv.at[n], (seq, ten)).wait_recv()

    def own_copy():
        return remote(xg.at[ten], xg.at[ten], o_sem.at[0], o_sem.at[1], (seq, partner))

    for level in (2, 1):
        for key in crossing:
            if key[1] == level:
                ring(key).start()
    own_copy().start()

    load_up.wait()
    load_down.wait()
    load_table.wait()

    def absorb(slot, first=False):
        wide = xg[slot].astype(F32)
        squares = jnp.sum(wide * wide, -1, keepdims=True)
        scaled = (wide * fg_ref[slot]).astype(BF16)
        weights = jnp.concatenate(
            [
                jnp.concatenate(
                    [up_v[c, inv_ref[c, 2 * slot + b]] for c in range(groups)], 1
                )
                for b in range(2)
            ],
            0,
        )
        term = dot(scaled, weights)
        if first:
            acc[...] = term
            row_power[...] = squares
        else:
            acc[...] += term
            row_power[...] += squares

    sources = [(0, 2), (1, 2), (0, 1), (1, 1), (0, 3), (1, 3), (0, 4)]

    def source_y(source):
        return at_y(ny - ways[source[0]] * source[1])

    def keys_of(table, source):
        i, d = source
        return [key for key in table if key[1] == d and (d == 4 or key[0] == i)]

    def handle(source):
        d = source[1]
        for key in keys_of(crossing, source):
            i, _, start, count = key
            got(key)
            if d == 2:
                if (start // quarter) % 2 == i:
                    ring((i, 4, start, count)).start()
                ring((i, 3, start, count)).start()
            elif d == 3 and (start // quarter) % 2 == 1:
                pass_on((i, 3, start - quarter, 2 * quarter)).start()
            elif d == 4:
                pass_on(key).start()
        if d <= 2:
            pass_on(keys_of(inside, source)[0]).start()

    def finish(source):
        for key in keys_of(inside, source):
            passed(key)

    def early(source, act_on):
        @pl.when(source_y(source) != 0)
        def _():
            act_on(source)

    def late(source, act_on):
        @pl.when(source_y(source) == 0)
        def _():
            act_on(source)

    def near(source):
        absorb(source_y(source) * 2 + core)

    def far(source):
        finish(source)
        absorb(source_y(source) * 2 + 1 - core)

    absorb(ten, True)
    for act_on in (handle, near, far):
        for source in sources[:4]:
            early(source, act_on)
    for source in sources[:4]:
        late(source, handle)
    remote(xg.at[partner], xg.at[partner], o_sem.at[0], o_sem.at[1], (seq, ten)).wait_recv()
    absorb(partner)
    for when in (early, late):
        for source in sources[4:]:
            when(source, handle)
    for act_on in (near, far):
        for source in sources[4:]:
            early(source, act_on)

    @pl.when(y != 0)
    def _():
        absorb(core)

    for source in sources:
        late(source, finish)

    @pl.when(y != 0)
    def _():
        absorb(1 - core)

    width = 256 * xg.shape[0]
    scale = lax.rsqrt(row_power[...] / width + 1e-05)
    act[...] = jax.nn.gelu(acc[...] * scale).astype(BF16)

    def share(slot):
        weights = jnp.concatenate(
            [
                jnp.concatenate(
                    [down_v[c, inv_ref[groups + c, 2 * slot + b]] for b in range(2)], 1
                )
                for c in range(groups)
            ],
            0,
        )
        return dot(act[...], weights).astype(BF16)

    def s_copy(off):
        k = off + reach - 1
        return remote(
            pair_out.at[k], pair_in.at[k], s_send.at[k], s_recv.at[k], (seq, partner)
        )

    def offer(off):
        pair_out[off + reach - 1] = share(at_y(ny + off) * 2 + 1 - core)
        s_copy(off).start()

    def pair_sum(off):
        mine = share(at_y(ny + off) * 2 + core).astype(F32)
        s_copy(off).wait_recv()
        return mine + pair_in[off + reach - 1].astype(F32)

    def m_copy(i, d, p):
        return remote(
            psum.at[i, d, halves[p]],
            rs.at[i, d, halves[p]],
            r_send.at[i, d - 1, p],
            r_recv.at[i, d - 1, p],
            across(i, d),
        )

    def m_got(i, d, p):
        block = rs.at[i, d, halves[p]]
        remote(block, block, r_send.at[i, d - 1, p], r_recv.at[i, d - 1, p], (seq, ten)).wait_recv()
        return rs[i, d, halves[p]].astype(F32)

    rows_dev = xg.shape[1] // 2

    def rows_of(value, p):
        return value[p * rows_dev : (p + 1) * rows_dev]

    def ship(i, d, p, value):
        psum[i, d, halves[p]] = value.astype(BF16)
        m_copy(i, d, p).start()

    def ship_both(d):
        for i in range(2):
            value = pair_sum(ways[i] * d)
            for p in range(2):
                ship(i, d, p, rows_of(value, p))

    for off in (4, 3, -3):
        offer(off)
    far = pair_sum(4)
    for i in range(2):
        ship(i, 4, i, rows_of(far, i))
    for off in (2, -2):
        offer(off)
    ship_both(3)
    for off in (1, -1, 0):
        offer(off)
    ship_both(1)
    sums = [pair_sum(2), pair_sum(-2)]
    total = pair_sum(0) + xg[ten].astype(F32)
    for p in range(2):
        for i in range(2):
            value = rows_of(sums[i], p) + m_got(i, 3, p)
            if sent(i, 4, p):
                value = value + m_got(i, 4, p)
            ship(i, 2, p, value)
    for p in range(2):
        value = rows_of(total, p)
        for d in (1, 2):
            for i in range(2):
                value = value + m_got(i, d, p)
        out_ref[halves[p], :] = value.astype(BF16)

    for o in range(1, LANES_X):
        on_first(lambda only_write: a_copy(o, only_write).wait_send())
        p_copy(o).wait_send()

        @pl.when(x + o < LANES_X)
        def _():
            for one in b_copies(o):
                one.wait_send()

    for o in range(1, nz):

        @pl.when(z + o < nz)
        def _():
            on_first_group(lambda only_write: z_copy(o, only_write).wait_send())

    own_copy().wait_send()
    for off in range(1 - reach, reach + 1):
        s_copy(off).wait_send()
    for i, d, p in messages:
        m_copy(i, d, p).wait_send()
    for key in crossing:
        ring(key).wait_send()
    for key in inside:
        pass_on(key).wait_send()


def solution(mesh):
    nseq, nten = mesh.shape["seq"], mesh.shape["tensor"]
    nz, ny = nseq // LANES_X, nten // 2
    vmem = pl.BlockSpec(memory_space=pltpu.VMEM)
    hbm = pl.BlockSpec(memory_space=pltpu.HBM)
    dma = pltpu.SemaphoreType.DMA

    def per_device(
        queries,
        keys,
        values,
        beta,
        decay,
        out_gain,
        residual,
        ffn_gain,
        up_blocks,
        up_index,
        down_kept_tiles,
        down_index,
    ):
        tok = queries.shape[0]
        groups, kept = up_index.shape
        return pl.pallas_call(
            functools.partial(main_kernel, nz, ny),
            out_shape=jax.ShapeDtypeStruct((tok, 256), BF16),
            in_specs=[hbm] * 12,
            out_specs=vmem,
            scratch_shapes=[
                pltpu.VMEM((2 * tok, 128), BF16),
                pltpu.VMEM((4 * tok, 128), BF16),
                pltpu.VMEM((4 * tok, 128), BF16),
                pltpu.VMEM((2, 2, tok), F32),
                pltpu.VMEM((2, tok), F32),
                pltpu.VMEM((groups, kept), jnp.int32),
                pltpu.VMEM((groups, kept), jnp.int32),
                pltpu.VMEM((tok, 256), BF16),
                pltpu.VMEM((1, 128), F32),
                pltpu.VMEM((nten, 1, 256), F32),
                dma((10,)),
                pltpu.VMEM((2, tok, 128), F32),
                pltpu.VMEM((2, tok, 128), F32),
                pltpu.VMEM((2 * groups, 128), jnp.int32),
                pltpu.SMEM((2 * groups, 128), jnp.int32),
                pltpu.VMEM((groups, kept + 1, 128, 128), BF16),
                pltpu.VMEM((groups, kept + 1, 128, 128), BF16),
                pltpu.VMEM((LANES_X, 2, 256, 128), BF16),
                pltpu.VMEM((192, 128), BF16),
                pltpu.VMEM((nz, 192, 128), BF16),
                pltpu.VMEM((64, 128), F32),
                pltpu.VMEM((128, 128), F32),
                pltpu.VMEM((2, 128, 128), F32),
                pltpu.VMEM((2, 128, 128), F32),
                pltpu.VMEM((64, 128), BF16),
                pltpu.VMEM((2, 128, 128), BF16),
                pltpu.VMEM((nten, tok, 256), BF16),
                pltpu.VMEM((tok, groups * 128), F32),
                pltpu.VMEM((tok, 1), F32),
                pltpu.VMEM((tok, groups * 128), BF16),
                pltpu.VMEM((ny, tok, 256), BF16),
                pltpu.VMEM((ny, tok, 256), BF16),
                pltpu.VMEM((2, ny // 2 + 1, tok, 256), BF16),
                pltpu.VMEM((2, ny // 2 + 1, tok, 256), BF16),
                dma((3,)),
                dma((LANES_X,)),
                dma((LANES_X,)),
                dma((LANES_X,)),
                dma((LANES_X,)),
                dma((LANES_X,)),
                dma((LANES_X,)),
                dma((nz,)),
                dma((nz,)),
                dma((LANES_X,)),
                dma((LANES_X,)),
                dma((22,)),
                dma((22,)),
                dma((12,)),
                dma((12,)),
                dma((2,)),
                dma((ny,)),
                dma((ny,)),
                dma((2, ny // 2, 2)),
                dma((2, ny // 2, 2)),
            ],
            compiler_params=pltpu.CompilerParams(
                collective_id=0, has_side_effects=True, vmem_limit_bytes=VMEM_LIMIT
            ),
            name="layer",
        )(*(pltpu.with_memory_space_constraint(a, pltpu.HBM) for a in (
            queries.reshape(2 * tok, 128),
            keys.reshape(4 * tok, 128),
            values.reshape(4 * tok, 128),
            beta,
            decay,
            up_index,
            down_index,
            residual,
            out_gain.reshape(1, 128),
            ffn_gain.reshape(nten, 1, 256),
            up_blocks,
            down_kept_tiles,
        )))

    placed = (
        P("seq", "tensor", None),
        P(None, "seq", "tensor", None),
        P(None, "seq", "tensor", None),
        P(None, "tensor", "seq"),
        P("tensor", "seq"),
        P(),
        P("seq", "tensor"),
        P(),
        P("tensor", None, None, None),
        P("tensor", None),
        P("tensor", None, None, None),
        P("tensor", None),
    )
    return jax.shard_map(
        per_device, mesh=mesh, in_specs=placed, out_specs=P("seq", "tensor"), check_vma=False
    )
```

```python
import functools

import jax
import jax.numpy as jnp
from jax import lax
from jax.experimental import pallas as pl
from jax.experimental.pallas import tpu as pltpu
from jax.sharding import PartitionSpec as P

F32 = jnp.float32
BF16 = jnp.bfloat16
HIGHEST = lax.Precision.HIGHEST
LANES_X = 4
VMEM_LIMIT = 24 << 20
MESH = pl.DeviceIdType.MESH


def dot(a, b, contract=(1, 0), precision=None):
    return lax.dot_general(
        a,
        b,
        (((contract[0],), (contract[1],)), ((), ())),
        precision=precision,
        preferred_element_type=F32,
    )


def split(a):
    high = a.astype(BF16)
    return high, (a - high.astype(F32)).astype(BF16)


def mm3(a, b):
    ah, al = split(a)
    bh, bl = split(b)
    left = jnp.concatenate([ah, al], 1)
    right = jnp.concatenate(
        [jnp.concatenate([bh, bl], 1), jnp.concatenate([bh, jnp.zeros_like(bl)], 1)], 0
    )
    both = dot(left, right)
    n = b.shape[1]
    return both[:, :n] + both[:, n:]


def iota(shape, axis):
    return lax.broadcasted_iota(jnp.int32, shape, axis)


def unit_lower_inverse(lowers):
    n = lowers[0].shape[0]
    rows, cols = iota((n, n), 0), iota((n, n), 1)
    eye = (rows == cols).astype(F32)
    base = (rows >> 3) == (cols >> 3)
    n1 = [jnp.where(base, -low, 0.0) for low in lowers]
    n2 = [mm3(a, a) for a in n1]
    n3 = [mm3(a, b) for a, b in zip(n1, n2)]
    n4 = [mm3(a, a) for a in n2]
    y = [eye + a + b + c for a, b, c in zip(n1, n2, n3)]
    x = [a + mm3(a, b) for a, b in zip(y, n4)]
    shift = 3
    while (1 << shift) < n:
        pick = ((rows >> (shift + 1)) == (cols >> (shift + 1))) & ((rows >> shift) != (cols >> shift))
        links = [jnp.where(pick, low, 0.0) for low in lowers]
        right = [mm3(c, a) for c, a in zip(links, x)]
        x = [a - mm3(a, b) for a, b in zip(x, right)]
        shift += 1
    return x


def inverse_table(index, kept):
    lanes = iota((index.shape[0], 128), 1)
    found = jnp.full(lanes.shape, kept, jnp.int32)
    for j in range(kept):
        found = jnp.where(index[:, j : j + 1] == lanes, j, found)
    return found


def local_terms(q_ref, k_ref, v_ref, beta_ref, decay_ref, tw_ref, qt_ref, lo_ref):
    tok = q_ref.shape[0] // 2
    span = 2 * tok
    heads = 2
    half = span // 2

    kv = jnp.concatenate([k_ref[...], v_ref[...]], 1)
    small = jnp.concatenate(
        [decay_ref[...], beta_ref[0], beta_ref[1], jnp.zeros((2, tok), F32)], 0
    )
    s1 = small.astype(BF16)
    rest = small - s1.astype(F32)
    s2 = rest.astype(BF16)
    s3 = (rest - s2.astype(F32)).astype(BF16)
    parts = jnp.concatenate([s1, s2, s3, jnp.zeros_like(s1)], 0)
    m_at, t_at = iota((span, tok), 0), iota((span, tok), 1)
    upto = t_at <= (m_at >> 1)
    first = (t_at == (m_at >> 1)) & ((m_at & 1) == 0)
    second = (t_at == (m_at >> 1)) & ((m_at & 1) == 1)
    upto_tok = iota((tok, tok), 1) <= iota((tok, tok), 0)
    picks = jnp.concatenate([e.astype(BF16) for e in (upto, first, second, upto_tok)], 0)
    cols3 = dot(picks, parts, (1, 1))
    col = cols3[:, 0:8] + cols3[:, 8:16] + cols3[:, 16:24]
    rows3 = dot(parts, picks, (1, 1))
    row = rows3[0:8] + rows3[8:16] + rows3[16:24]
    run_col, one_col, two_col = col[:span], col[span : 2 * span], col[2 * span : 3 * span]
    tok_col = col[3 * span :]
    run_row, one_row, two_row = row[:, :span], row[:, span : 2 * span], row[:, 2 * span : 3 * span]

    rows, cols = iota((span, span), 0), iota((span, span), 1)
    below = cols < rows
    same = rows == cols
    reach = iota((tok, span), 1) <= 2 * iota((tok, span), 0) + 1
    eye = (iota((tok, tok), 0) == iota((tok, tok), 1)).astype(F32)
    row_of = iota((span, 4 * tok), 0)
    place = (row_of & 1) * span + (row_of >> 1) * 2
    column = iota((span, 4 * tok), 1)
    q_place = iota((tok, span), 0) * 2
    q_column = iota((tok, span), 1)

    ks, vs, qs, gammas, lowers, keep = [], [], [], [], [], []
    for h in range(heads):
        pick = (column == place + h).astype(BF16)
        both = dot(pick, kv).astype(BF16)
        k, v = both[:, :128], both[:, 128:]
        gram = dot(k, k, (1, 1))
        diag = jnp.where(same, gram, 0.0)
        rk_col = lax.rsqrt(jnp.sum(diag, 1, keepdims=True) + 1e-06)
        rk_row = lax.rsqrt(jnp.sum(diag, 0, keepdims=True) + 1e-06)
        run_c, run_r = run_col[:, h : h + 1], run_row[h : h + 1, :]
        beta_c = one_col[:, 2 + h : 3 + h] + two_col[:, 4 + h : 5 + h]
        beta_r = one_row[2 + h : 3 + h, :] + two_row[4 + h : 5 + h, :]
        fade = jnp.exp(jnp.where(below, run_c - run_r, 0.0))
        low = jnp.where(below, (beta_c * rk_col) * fade * gram * rk_row, 0.0)
        keep.append((k, v, rk_col, rk_row, run_c, run_r, beta_r, low))
        lowers += [low[:half, :half], low[half:, half:]]

    inverses = unit_lower_inverse(lowers)
    mids = [mm3(keep[h][7][half:, :half], inverses[2 * h]) for h in range(heads)]
    crosses = [mm3(inverses[2 * h + 1], mids[h]) for h in range(heads)]
    left = []
    for h in range(heads):
        k, v, rk_col, rk_row, run_c, run_r, beta_r, low = keep[h]
        a = jnp.concatenate(
            [
                jnp.concatenate([inverses[2 * h], jnp.zeros((half, half), F32)], 1),
                jnp.concatenate([-crosses[h], inverses[2 * h + 1]], 1),
            ],
            0,
        )
        a_val = a * beta_r
        ah, al = split(a_val)
        u = dot(ah, v) + dot(al, v)
        last = run_c[span - 1 : span, :]
        remain = jnp.exp(last - run_c) * rk_col
        uh, ul = split(u * remain)
        write_t = dot(uh, k, (0, 0)) + dot(ul, k, (0, 0))
        tw_ref[h, 0:64, :] = write_t[:64].astype(BF16)
        tw_ref[h, 192:256, :] = write_t[64:].astype(BF16)
        mids[h] = (a_val, last, remain, u)

    def transitions():
        for h in range(heads):
            k, v, rk_col, rk_row, run_c, run_r, beta_r, low = keep[h]
            a_val, last, remain, u = mids[h]
            ah, al = split(a_val * (jnp.exp(run_r) * rk_row))
            w = dot(ah, k) + dot(al, k)
            wh, wl = split(w * remain)
            trans = jnp.exp(last) * eye - dot(k, wh, (0, 0)) - dot(k, wl, (0, 0))
            tw_ref[h, 64:192, :] = trans.astype(BF16)
            left.append((k, u, w, rk_row, run_r, tok_col[:, h : h + 1]))

    def queries():
        q_all = q_ref[...]
        for h in range(heads):
            k, u, w, rk_row, run_r, tok_run = left[h]
            q = dot((q_column == q_place + h).astype(BF16), q_all)
            rq = lax.rsqrt(jnp.sum(q * q, 1, keepdims=True) + 1e-06)
            qk = dot(q.astype(BF16), k, (1, 1))
            mixing = jnp.where(
                reach, jnp.exp(jnp.where(reach, tok_run - run_r, 0.0)) * qk * rq * rk_row, 0.0
            )
            mh, ml = split(mixing)
            bh, bl = split(jnp.concatenate([w, u], 1))
            mixed = dot(mh, bh) + dot(ml, bh) + dot(mh, bl)
            qt_ref[h] = (jnp.exp(tok_run) * rq) * q - mixed[:, :128]
            lo_ref[h] = mixed[:, 128:]

    return transitions, queries


def chain_step(state, trans, write):
    n = state.shape[0]
    high, low = split(state)
    both = dot(jnp.concatenate([high, low], 0), trans, (1, 1))
    return both[:n] + both[n:] + write.astype(F32)


def main_kernel(
    nz,
    ny,
    q_in,
    k_in,
    v_in,
    beta_in,
    decay_in,
    up_in,
    down_in,
    res_in,
    og_in,
    fg_in,
    up_hbm,
    down_hbm,
    out_ref,
    q_ref,
    k_ref,
    v_ref,
    beta_ref,
    decay_ref,
    up_ref,
    down_ref,
    res_ref,
    og_ref,
    fg_ref,
    l_sem,
    qt_ref,
    lo_ref,
    table_v,
    inv_ref,
    up_v,
    down_v,
    rx,
    zmsg,
    rz,
    chain,
    since,
    before_t,
    before_w,
    pmsg,
    rp,
    xg,
    acc,
    act,
    pair_out,
    pair_in,
    psum,
    rs,
    wsem,
    a_send,
    a_recv,
    b_send,
    b_recv,
    c_send,
    c_recv,
    z_send,
    z_recv,
    p_send,
    p_recv,
    g_send,
    g_recv,
    f_send,
    f_recv,
    o_sem,
    s_send,
    s_recv,
    r_send,
    r_recv,
):
    seq, ten = lax.axis_index("seq"), lax.axis_index("tensor")
    z, x = seq // LANES_X, lax.rem(seq, LANES_X)
    y, core = ten // 2, lax.rem(ten, 2)
    partner = y * 2 + 1 - core
    head, part = x // 2, lax.rem(x, 2)
    groups = up_hbm.shape[0]
    kept = up_hbm.shape[1]

    def at_x(o):
        return lax.rem(x + o, LANES_X)

    def at_y(o):
        return lax.rem(y + o, ny)

    barrier = pltpu.get_barrier_semaphore()
    peers = [(z * LANES_X + at_x(o), ten) for o in range(1, LANES_X)]
    peers += [(lax.rem(z + o, nz) * LANES_X + x, ten) for o in range(1, nz)]
    peers += [(seq, at_y(o) * 2 + core) for o in (1, 2, ny - 2, ny - 1)]
    peers += [(seq, partner)]
    inputs = (
        (k_in, k_ref),
        (v_in, v_ref),
        (q_in, q_ref),
        (beta_in, beta_ref),
        (decay_in, decay_ref),
        (up_in, up_ref),
        (down_in, down_ref),
        (res_in, res_ref),
        (og_in, og_ref),
        (fg_in, fg_ref),
    )
    loads = [
        pltpu.make_async_copy(here, there, l_sem.at[n]) for n, (here, there) in enumerate(inputs)
    ]
    for load in loads:
        load.start()
    for peer in peers:
        pl.semaphore_signal(barrier, inc=1, device_id=peer, device_id_type=MESH)
    load_up = pltpu.make_async_copy(up_hbm, up_v.at[:, pl.ds(0, kept)], wsem.at[0])
    load_down = pltpu.make_async_copy(down_hbm, down_v.at[:, pl.ds(0, kept)], wsem.at[1])
    load_up.start()
    load_down.start()
    for load in loads:
        load.wait()
    transitions, queries = local_terms(q_ref, k_ref, v_ref, beta_ref, decay_ref, rx.at[x], qt_ref, lo_ref)
    pl.semaphore_wait(barrier, len(peers))

    def remote(src, dst, send, recv, peer):
        return pltpu.make_async_remote_copy(
            src_ref=src,
            dst_ref=dst,
            send_sem=send,
            recv_sem=recv,
            device_id=peer,
            device_id_type=MESH,
        )

    w_rows = pl.ds(pl.multiple_of(part * 192, 64), 64)
    my_rows = pl.ds(pl.multiple_of(part * 64, 64), 192)

    def a_copy(o, only_write):
        there = at_x(o)
        h2, p2 = there // 2, lax.rem(there, 2)
        if only_write:
            rows = pl.ds(pl.multiple_of(p2 * 192, 64), 64)
        else:
            rows = pl.ds(pl.multiple_of(p2 * 64, 64), 192)
        return remote(
            rx.at[x, h2, rows],
            rx.at[x, h2, rows],
            a_send.at[o],
            a_recv.at[x],
            (z * LANES_X + there, ten),
        )

    def on_first(act_on):
        @pl.when(seq == 0)
        def _():
            act_on(True)

        @pl.when(seq != 0)
        def _():
            act_on(False)

    def a_wait(i):
        def wait(only_write):
            block = rx.at[i, head, w_rows if only_write else my_rows]
            remote(block, block, a_send.at[0], a_recv.at[i], (seq, ten)).wait_recv()

        @pl.when(i != x)
        def _():
            if i == 0:

                @pl.when(z == 0)
                def _():
                    wait(True)
                    rx[0, head, 64:192] = jnp.zeros((128, 128), BF16)

                @pl.when(z != 0)
                def _():
                    wait(False)
            else:
                wait(False)

    def b_copies(o):
        there = at_x(o)
        h2, p2 = there // 2, lax.rem(there, 2)
        rows = pl.ds(pl.multiple_of((1 - p2) * 192, 64), 64)
        peer = (z * LANES_X + there, ten)
        return (
            remote(
                rx.at[x, h2, rows], rx.at[x, h2, rows], b_send.at[o], b_recv.at[x], peer
            ),
            remote(
                rx.at[x, 1 - h2], rx.at[x, 1 - h2], c_send.at[o], c_recv.at[x], peer
            ),
        )

    @pl.when(seq == 0)
    def _():
        for o in (2, 1, 3):
            a_copy(o, True).start()

    transitions()

    @pl.when(seq != 0)
    def _():
        for o in (2, 1, 3):
            a_copy(o, False).start()

    chain[...] = jnp.zeros_like(chain)
    eye = (iota((128, 128), 0) == iota((128, 128), 1)).astype(F32)
    since[...] = eye
    for h in range(2):
        before_t[h] = eye
        before_w[h] = jnp.zeros((128, 128), F32)
    table_v[0:groups] = inverse_table(up_ref[...], kept)
    table_v[groups : 2 * groups] = inverse_table(down_ref[...], kept)
    load_table = pltpu.make_async_copy(table_v, inv_ref, wsem.at[2])
    load_table.start()
    for c in range(groups):
        up_v[c, kept] = jnp.zeros(up_v.shape[2:], BF16)
        down_v[c, kept] = jnp.zeros(up_v.shape[2:], BF16)
    queries()

    def apply(write, trans):
        high, low = split(trans)
        return dot(write, high, (1, 1)) + dot(write, low, (1, 1))

    def extend(trans, earlier):
        high, low = split(trans)
        both = dot(jnp.concatenate([high, low], 0), earlier)
        return both[:128] + both[128:]

    for i in (3, 2, 1):
        a_wait(i)
    ts = [rx[i, head, pl.ds(64, 128)] for i in range(1, LANES_X)]
    ws = [rx[i, head, w_rows] for i in range(1, LANES_X)]
    t32 = dot(ts[2], ts[1])
    w32 = dot(ws[1], ts[2], (1, 1)) + ws[2].astype(F32)
    t321 = extend(t32, ts[0])
    w321 = apply(ws[0], t32) + w32
    a_wait(0)
    zmsg[0:64] = (apply(rx[0, head, w_rows], t321) + w321).astype(BF16)
    zmsg[64:192] = extend(t321, rx[0, head, pl.ds(64, 128)]).astype(BF16)

    def z_copy(o, only_write):
        rows = pl.ds(0, 64 if only_write else 192)
        return remote(
            zmsg.at[rows],
            rz.at[z, rows],
            z_send.at[o],
            z_recv.at[z],
            ((z + o) * LANES_X + x, ten),
        )

    def on_first_group(act_on):
        @pl.when(z == 0)
        def _():
            act_on(True)

        @pl.when(z != 0)
        def _():
            act_on(False)

    for o in sorted(range(1, nz), key=lambda o: -min(o, nz - o)):

        @pl.when(z + o < nz)
        def _():
            on_first_group(lambda only_write: z_copy(o, only_write).start())

    for o in range(1, LANES_X):

        @pl.when(x + o < LANES_X)
        def _():
            for one in b_copies(o):
                one.start()

    def z_wait(i):
        block = rz.at[i, pl.ds(0, 64 if i == 0 else 192)]
        remote(block, block, z_send.at[0], z_recv.at[i], (seq, ten)).wait_recv()

    for i in range(nz - 2, 0, -1):

        @pl.when(i < z)
        def _():
            z_wait(i)
            chain[...] += apply(rz[i, 0:64], since[...])
            since[...] = extend(since[...], rz[i, 64:192])

    if nz > 1:

        @pl.when(z > 0)
        def _():
            z_wait(0)
            chain[...] += apply(rz[0, 0:64], since[...])

    entering = chain[...].astype(BF16)
    pmsg[...] = entering
    p_rows = pl.ds(pl.multiple_of(part * 64, 64), 64)
    rp[head, p_rows] = entering

    def p_copy(o):
        return remote(
            pmsg,
            rp.at[head, p_rows],
            p_send.at[o],
            p_recv.at[x],
            (z * LANES_X + at_x(o), ten),
        )

    for o in (2, 1, 3):
        p_copy(o).start()

    for i in range(LANES_X - 1):

        @pl.when(i < x)
        def _():
            other = pl.ds(pl.multiple_of((1 - part) * 192, 64), 64)
            remote(
                rx.at[i, head, other],
                rx.at[i, head, other],
                b_send.at[0],
                b_recv.at[i],
                (seq, ten),
            ).wait_recv()
            remote(
                rx.at[i, 1 - head], rx.at[i, 1 - head], c_send.at[0], c_recv.at[i], (seq, ten)
            ).wait_recv()
            for h in range(2):
                trans = rx[i, h, 64:192]
                write = jnp.concatenate([rx[i, h, 0:64], rx[i, h, 192:256]], 0)
                if i == 0:
                    before_t[h] = trans.astype(F32)
                    before_w[h] = write.astype(F32)
                else:
                    high, low = split(before_t[h])
                    both = dot(trans, jnp.concatenate([high, low], 1))
                    before_t[h] = both[:, :128] + both[:, 128:]
                    before_w[h] = chain_step(before_w[h], trans, write)

    for o in (1, 3, 2):
        source = at_x(o)
        rows = pl.ds(pl.multiple_of(lax.rem(source, 2) * 64, 64), 64)
        remote(
            rp.at[source // 2, rows],
            rp.at[source // 2, rows],
            p_send.at[o],
            p_recv.at[source],
            (seq, ten),
        ).wait_recv()

    state = [apply(rp[h], before_t[h]) + before_w[h] for h in range(2)]
    gain = og_ref[...]
    pieces = []
    for h in range(2):
        qh, ql = split(qt_ref[h])
        sh, sl = split(state[h])
        head_out = dot(qh, sh, (1, 1)) + dot(ql, sh, (1, 1)) + dot(qh, sl, (1, 1)) + lo_ref[h]
        power = jnp.mean(head_out * head_out, -1, keepdims=True)
        normed = head_out * lax.rsqrt(power + 1e-05) * gain
        pieces.append(res_ref[:, 128 * h : 128 * h + 128].astype(F32) + normed)
    xg[ten] = jnp.concatenate(pieces, 1).astype(BF16)

    reach = ny // 2
    ways = (1, -1)
    halves = [pl.ds(0, xg.shape[1] // 2), pl.ds(xg.shape[1] // 2, xg.shape[1] // 2)]

    def sent(i, d, part_at):
        return d < reach or part_at == i

    messages = [
        (i, d, p)
        for d in range(1, reach + 1)
        for p in range(2)
        for i in range(2)
        if sent(i, d, p)
    ]

    hop = (0, 1, 2, 1, 2)

    def across(i, d):
        return (seq, at_y(ny + ways[i] * hop[d]) * 2 + core)

    rows_all = xg.shape[1]
    quarter = rows_all // 4
    quarters = [(i, q) for q in range(4) for i in range(2)]
    crossing = [(i, 2, q * quarter, quarter) for i, q in quarters]
    crossing += [(i, 1, 0, rows_all) for i in range(2)]
    crossing += [(i, 3, q * quarter, quarter) for i, q in quarters]
    crossing += [(i, 4, q * quarter, quarter) for i, q in quarters if q % 2 == i]
    inside = [(i, d, 0, rows_all) for d in (1, 2) for i in range(2)]
    inside += [(i, 3, s * 2 * quarter, 2 * quarter) for s in range(2) for i in range(2)]
    inside += [key for key in crossing if key[1] == 4]

    def block_of(i, d, side, start, count):
        slot = at_y(ny - ways[i] * d) * 2 + (core if side == 0 else 1 - core)
        return xg.at[slot, pl.ds(start, count)]

    def ring(key):
        i, d, start, count = key
        n = crossing.index(key)
        block = block_of(i, 0 if d <= 2 else 2, 0, start, count)
        return remote(block, block, g_send.at[n], g_recv.at[n], across(i, d))

    def got(key):
        i, d, start, count = key
        n = crossing.index(key)
        block = block_of(i, d, 0, start, count)
        remote(block, block, g_send.at[n], g_recv.at[n], (seq, ten)).wait_recv()

    def pass_on(key):
        i, d, start, count = key
        n = inside.index(key)
        block = block_of(i, d, 0, start, count)
        return remote(block, block, f_send.at[n], f_recv.at[n], (seq, partner))

    def passed(key):
        i, d, start, count = key
        n = inside.index(key)
        block = block_of(i, d, 1, start, count)
        remote(block, block, f_send.at[n], f_recv.at[n], (seq, ten)).wait_recv()

    def own_copy():
        return remote(xg.at[ten], xg.at[ten], o_sem.at[0], o_sem.at[1], (seq, partner))

    for level in (2, 1):
        for key in crossing:
            if key[1] == level:
                ring(key).start()
    own_copy().start()

    load_up.wait()
    load_down.wait()
    load_table.wait()

    def absorb(slot, first, power):
        wide = xg[slot].astype(F32)
        power = power + jnp.sum(wide * wide, -1, keepdims=True)
        scaled = (wide * fg_ref[slot]).astype(BF16)
        weights = jnp.concatenate(
            [
                jnp.concatenate(
                    [up_v[c, inv_ref[c, 2 * slot + b]] for c in range(groups)], 1
                )
                for b in range(2)
            ],
            0,
        )
        term = dot(scaled, weights)
        if first:
            acc[...] = term
        else:
            acc[...] += term
        return power

    def blocks(d):
        return [at_y(d)] if d == reach else [at_y(ny - d), at_y(d)]

    power = absorb(ten, True, jnp.zeros((xg.shape[1], 1), F32))
    remote(xg.at[partner], xg.at[partner], o_sem.at[0], o_sem.at[1], (seq, ten)).wait_recv()
    power = absorb(partner, False, power)

    def near(d, power):
        for where in blocks(d):
            power = absorb(where * 2 + core, False, power)
        return power

    def far_side(d, power):
        for key in inside:
            if key[1] == d:
                passed(key)
        for where in blocks(d):
            power = absorb(where * 2 + 1 - core, False, power)
        return power

    for i, q in quarters:
        start = q * quarter
        got((i, 2, start, quarter))
        if q % 2 == i:
            ring((i, 4, start, quarter)).start()
        ring((i, 3, start, quarter)).start()
    for i in range(2):
        pass_on((i, 2, 0, rows_all)).start()
    for i in range(2):
        got((i, 1, 0, rows_all))
        pass_on((i, 1, 0, rows_all)).start()
    power = near(2, power)
    power = near(1, power)
    power = far_side(2, power)
    power = far_side(1, power)
    for q in range(4):
        start = q * quarter
        for i in range(2):
            got((i, 3, start, quarter))
            if q % 2 == 1:
                pass_on((i, 3, start - quarter, 2 * quarter)).start()
        last = (q % 2, 4, start, quarter)
        got(last)
        pass_on(last).start()
    power = near(3, power)
    power = near(4, power)
    power = far_side(3, power)
    power = far_side(4, power)

    width = 256 * xg.shape[0]
    scale = lax.rsqrt(power / width + 1e-05)
    act[...] = jax.nn.gelu(acc[...] * scale).astype(BF16)

    def share(slot):
        weights = jnp.concatenate(
            [
                jnp.concatenate(
                    [down_v[c, inv_ref[groups + c, 2 * slot + b]] for b in range(2)], 1
                )
                for c in range(groups)
            ],
            0,
        )
        return dot(act[...], weights).astype(BF16)

    def s_copy(off):
        k = off + reach - 1
        return remote(
            pair_out.at[k], pair_in.at[k], s_send.at[k], s_recv.at[k], (seq, partner)
        )

    def offer(off):
        pair_out[off + reach - 1] = share(at_y(ny + off) * 2 + 1 - core)
        s_copy(off).start()

    def pair_sum(off):
        mine = share(at_y(ny + off) * 2 + core).astype(F32)
        s_copy(off).wait_recv()
        return mine + pair_in[off + reach - 1].astype(F32)

    def m_copy(i, d, p):
        return remote(
            psum.at[i, d, halves[p]],
            rs.at[i, d, halves[p]],
            r_send.at[i, d - 1, p],
            r_recv.at[i, d - 1, p],
            across(i, d),
        )

    def m_got(i, d, p):
        block = rs.at[i, d, halves[p]]
        remote(block, block, r_send.at[i, d - 1, p], r_recv.at[i, d - 1, p], (seq, ten)).wait_recv()
        return rs[i, d, halves[p]].astype(F32)

    rows_dev = xg.shape[1] // 2

    def rows_of(value, p):
        return value[p * rows_dev : (p + 1) * rows_dev]

    def ship(i, d, p, value):
        psum[i, d, halves[p]] = value.astype(BF16)
        m_copy(i, d, p).start()

    def ship_both(d):
        for i in range(2):
            value = pair_sum(ways[i] * d)
            for p in range(2):
                ship(i, d, p, rows_of(value, p))

    for off in (4, 3, -3):
        offer(off)
    far = pair_sum(4)
    for i in range(2):
        ship(i, 4, i, rows_of(far, i))
    for off in (2, -2):
        offer(off)
    ship_both(3)
    for off in (1, -1, 0):
        offer(off)
    ship_both(1)
    sums = [pair_sum(2), pair_sum(-2)]
    total = pair_sum(0) + xg[ten].astype(F32)
    for p in range(2):
        for i in range(2):
            value = rows_of(sums[i], p) + m_got(i, 3, p)
            if sent(i, 4, p):
                value = value + m_got(i, 4, p)
            ship(i, 2, p, value)
    for p in range(2):
        value = rows_of(total, p)
        for d in (1, 2):
            for i in range(2):
                value = value + m_got(i, d, p)
        out_ref[halves[p], :] = value.astype(BF16)

    for o in range(1, LANES_X):
        on_first(lambda only_write: a_copy(o, only_write).wait_send())
        p_copy(o).wait_send()

        @pl.when(x + o < LANES_X)
        def _():
            for one in b_copies(o):
                one.wait_send()

    for o in range(1, nz):

        @pl.when(z + o < nz)
        def _():
            on_first_group(lambda only_write: z_copy(o, only_write).wait_send())

    own_copy().wait_send()
    for off in range(1 - reach, reach + 1):
        s_copy(off).wait_send()
    for i, d, p in messages:
        m_copy(i, d, p).wait_send()
    for key in crossing:
        ring(key).wait_send()
    for key in inside:
        pass_on(key).wait_send()


def solution(mesh):
    nseq, nten = mesh.shape["seq"], mesh.shape["tensor"]
    nz, ny = nseq // LANES_X, nten // 2
    vmem = pl.BlockSpec(memory_space=pltpu.VMEM)
    hbm = pl.BlockSpec(memory_space=pltpu.HBM)
    dma = pltpu.SemaphoreType.DMA

    def per_device(
        queries,
        keys,
        values,
        beta,
        decay,
        out_gain,
        residual,
        ffn_gain,
        up_blocks,
        up_index,
        down_kept_tiles,
        down_index,
    ):
        tok = queries.shape[0]
        groups, kept = up_index.shape
        return pl.pallas_call(
            functools.partial(main_kernel, nz, ny),
            out_shape=jax.ShapeDtypeStruct((tok, 256), BF16),
            in_specs=[hbm] * 12,
            out_specs=vmem,
            scratch_shapes=[
                pltpu.VMEM((2 * tok, 128), BF16),
                pltpu.VMEM((4 * tok, 128), BF16),
                pltpu.VMEM((4 * tok, 128), BF16),
                pltpu.VMEM((2, 2, tok), F32),
                pltpu.VMEM((2, tok), F32),
                pltpu.VMEM((groups, kept), jnp.int32),
                pltpu.VMEM((groups, kept), jnp.int32),
                pltpu.VMEM((tok, 256), BF16),
                pltpu.VMEM((1, 128), F32),
                pltpu.VMEM((nten, 1, 256), F32),
                dma((10,)),
                pltpu.VMEM((2, tok, 128), F32),
                pltpu.VMEM((2, tok, 128), F32),
                pltpu.VMEM((2 * groups, 128), jnp.int32),
                pltpu.SMEM((2 * groups, 128), jnp.int32),
                pltpu.VMEM((groups, kept + 1, 128, 128), BF16),
                pltpu.VMEM((groups, kept + 1, 128, 128), BF16),
                pltpu.VMEM((LANES_X, 2, 256, 128), BF16),
                pltpu.VMEM((192, 128), BF16),
                pltpu.VMEM((nz, 192, 128), BF16),
                pltpu.VMEM((64, 128), F32),
                pltpu.VMEM((128, 128), F32),
                pltpu.VMEM((2, 128, 128), F32),
                pltpu.VMEM((2, 128, 128), F32),
                pltpu.VMEM((64, 128), BF16),
                pltpu.VMEM((2, 128, 128), BF16),
                pltpu.VMEM((nten, tok, 256), BF16),
                pltpu.VMEM((tok, groups * 128), F32),
                pltpu.VMEM((tok, groups * 128), BF16),
                pltpu.VMEM((ny, tok, 256), BF16),
                pltpu.VMEM((ny, tok, 256), BF16),
                pltpu.VMEM((2, ny // 2 + 1, tok, 256), BF16),
                pltpu.VMEM((2, ny // 2 + 1, tok, 256), BF16),
                dma((3,)),
                dma((LANES_X,)),
                dma((LANES_X,)),
                dma((LANES_X,)),
                dma((LANES_X,)),
                dma((LANES_X,)),
                dma((LANES_X,)),
                dma((nz,)),
                dma((nz,)),
                dma((LANES_X,)),
                dma((LANES_X,)),
                dma((22,)),
                dma((22,)),
                dma((12,)),
                dma((12,)),
                dma((2,)),
                dma((ny,)),
                dma((ny,)),
                dma((2, ny // 2, 2)),
                dma((2, ny // 2, 2)),
            ],
            compiler_params=pltpu.CompilerParams(
                collective_id=0, has_side_effects=True, vmem_limit_bytes=VMEM_LIMIT
            ),
            name="layer",
        )(*(pltpu.with_memory_space_constraint(a, pltpu.HBM) for a in (
            queries.reshape(2 * tok, 128),
            keys.reshape(4 * tok, 128),
            values.reshape(4 * tok, 128),
            beta,
            decay,
            up_index,
            down_index,
            residual,
            out_gain.reshape(1, 128),
            ffn_gain.reshape(nten, 1, 256),
            up_blocks,
            down_kept_tiles,
        )))

    placed = (
        P("seq", "tensor", None),
        P(None, "seq", "tensor", None),
        P(None, "seq", "tensor", None),
        P(None, "tensor", "seq"),
        P("tensor", "seq"),
        P(),
        P("seq", "tensor"),
        P(),
        P("tensor", None, None, None),
        P("tensor", None),
        P("tensor", None, None, None),
        P("tensor", None),
    )
    return jax.shard_map(
        per_device, mesh=mesh, in_specs=placed, out_specs=P("seq", "tensor"), check_vma=False
    )
```
